128 devices in a mesh: row: 16 (over x_hi, z, core), col: 8 (over x_lo, y).
Axes of the slice: x: 4 (x_hi: 2, x_lo: 2; x = x_hi * 2 + x_lo), y: 4, z: 4, core: 2. Of those that a mesh axis runs over, the one named last changes fastest.
Arguments:
- tokens: bfloat16 [2048, 6144], P('row', 'col'), may hold values from -6 to 6
- gate_weight: bfloat16 [6144, 8192], P('col', 'row'), may hold values from -0.078125 to 0.078125
- up_weight: bfloat16 [6144, 8192], P('col', 'row'), may hold values from -0.25515518 to 0.25515518
- route: int32 [1024], replicated, may hold values from 0 to 2047
- live: int32 [1024], replicated, may hold values 0 or 1
Outputs:
- panels: float32 [8192, 512], P('col')
- trailing: float32 [8192, 8192], P('col', 'row')
The draws below stay inside these ranges and needn't reach their ends.
Inputs may be any that keep to these rules, and one draw needn't show every extreme that they name: `route`: indices of tokens routed to the expert; a token may appear more than once.
All inputs are finite; a program needn't handle non-finite values.
Results may differ from the reference program's by a relative error of at most 0.0043.
Values may be sent and summed in bfloat16 or wider, within the bound.
A program may use at most 128 MiB of HBM per device.

```python
import math
import jax
import jax.numpy as jnp
from jax import lax

D = 6144
FF = 8192
ROWS = 1024
PANEL = 512
PANELS = 1
POOL = 2048


def draw_up_weight(key, part):
    first = jax.random.fold_in(key, 11)
    second = jax.random.fold_in(key, 23)
    columns = jnp.arange(FF, dtype=jnp.float32) / FF
    spread = jax.random.uniform(second, (FF,), jnp.float32)
    scale = 0.6 * 3.0 ** columns * 3.0 ** (spread - 0.5)
    entries = jax.random.truncated_normal(first, -6.0, 6.0, (D, FF), jnp.float32)
    return (entries * scale[None, :] / math.sqrt(D)).astype(jnp.bfloat16)


def plant(result, stream_key, smallest, largest):
    spot = [jax.random.randint(jax.random.fold_in(stream_key, axis), (), 0, length) for axis, length in enumerate(result.shape)]
    longest = result.shape.index(max(result.shape))
    neighbour = spot[:longest] + [(spot[longest] + 1) % result.shape[longest]] + spot[longest + 1:]
    return result.at[tuple(spot)].set(smallest).at[tuple(neighbour)].set(largest)


def shard_levels(stream_key, shape, split, smallest, largest):
    def one(axis_at, shards_of):
        heights = jax.random.uniform(jax.random.fold_in(jax.random.fold_in(stream_key, 6), axis_at), (shards_of,), jnp.float32, smallest / len(split), largest / len(split))
        return jnp.repeat(jnp.exp(heights), shape[axis_at] // shards_of).reshape((-1,) + (1,) * (len(shape) - axis_at - 1))

    factor_of = one(*split[0])
    for cut in split[1:]:
        factor_of = factor_of * one(*cut)
    return factor_of


def centred(key, dims, scale, limit, cuts=(), held_as=jnp.bfloat16):
    factor_of = shard_levels(key, dims, cuts, -0.22, 0.18) if cuts else 1.0
    values = jax.random.normal(key, dims, jnp.float32) * scale * factor_of
    return jnp.minimum(jnp.maximum(values, -limit), limit).astype(held_as)


def setup_inputs(seed: int = 0) -> dict:
    key_list = jax.random.split(jax.random.key(seed), 6)
    return {
        "tokens": centred(key_list[0], (POOL, D), 1.0, 6.0, ((0, 16), (1, 8))),
        "gate_weight": centred(key_list[1], (D, FF), D ** -0.5, 0.078125, ((0, 8), (1, 16))),
        "up_weight": draw_up_weight(jax.random.fold_in(key_list[5], 71), 0),
        "route": plant(jax.random.randint(key_list[3], (ROWS,), 0, POOL), jax.random.fold_in(key_list[3], 1), 0, POOL - 1).astype(jnp.int32),
        "live": plant((jax.random.randint(key_list[4], (ROWS,), 0, 4) < 3).astype(jnp.int32), jax.random.fold_in(key_list[4], 1), 0, 1),
    }


damping = 0.1

def reference(tokens, gate_weight, up_weight, route, live):
    chosen = jnp.take(tokens, route.astype(jnp.int32), axis=0)
    gate = jnp.dot(chosen.astype(jnp.float32), gate_weight.astype(jnp.float32), preferred_element_type=jnp.float32)
    up = jnp.dot(chosen.astype(jnp.float32), up_weight.astype(jnp.float32), preferred_element_type=jnp.float32)
    mask = live.astype(jnp.float32)[:, None]
    hidden = (jax.nn.silu(gate) * up * mask).astype(jnp.bfloat16)
    gram = lax.dot_general(hidden.astype(jnp.float32), hidden.astype(jnp.float32), (((0,), (0,)), ((), ())), preferred_element_type=jnp.float32)
    widened = hidden.astype(jnp.float32)
    total = jnp.sum(widened * widened)
    ridge = damping * total / (ROWS * FF)
    index = jnp.arange(FF, dtype=jnp.int32)
    matrix = (gram / ROWS).at[index, index].add(ridge)
    outputs = []
    for step in range(PANELS):
        lower = step * PANEL
        corner = matrix[lower:lower + PANEL, lower:lower + PANEL]
        factor = jnp.linalg.cholesky(corner)
        column = matrix[:, lower:lower + PANEL]
        panel = jax.scipy.linalg.solve_triangular(factor, column.T, lower=True).T
        matrix = matrix - jnp.dot(panel.astype(jnp.float32), panel.T.astype(jnp.float32), precision=lax.Precision.HIGHEST, preferred_element_type=jnp.float32)
        outputs.append(panel)
    return (jnp.concatenate(outputs, axis=1), matrix)
```

```python
import functools

import jax
import jax.numpy as jnp
from jax import lax
from jax.experimental import pallas as pl
from jax.experimental.pallas import tpu as pltpu
from jax.sharding import Mesh
from jax.sharding import PartitionSpec as P

PANEL = 512
COL = ("col_0", "col_1")
ROW = ("row_0", "row_1", "row_2")
ROW_COL = ("row_0", "row_1", "row_2", "col_0", "col_1")
MESH = pl.DeviceIdType.MESH
F32 = jnp.float32
BF16 = jnp.bfloat16

damping = 0.1


def remote(src, dst, sems, slot, where):
    send, recv = sems
    return pltpu.make_async_remote_copy(
        src_ref=src, dst_ref=dst, send_sem=send.at[slot], recv_sem=recv.at[slot],
        device_id=where, device_id_type=MESH,
    )


def greet(peers):
    barrier = pltpu.get_barrier_semaphore()
    for peer in peers:
        pl.semaphore_signal(barrier, inc=1, device_id=peer, device_id_type=MESH)
    pl.semaphore_wait(barrier, len(peers))


def hidden_kernel(
    tok_ref, gate_ref, up_ref, route_ref, live_ref, hidden_ref,
    tk, gw, uw, tg, tu, rgx, rg1, rg2, ru1, ru2, rux, uout, local_sem,
    a_send, a_recv, r_send, r_recv,
):
    xh, z, core = (lax.axis_index(a) for a in ROW)
    xl, y = (lax.axis_index(a) for a in COL)
    oh, oc, ol = 1 - xh, 1 - core, 1 - xl
    zn, zp, zf = (z + 1) % 4, (z + 3) % 4, (z + 2) % 4
    yn, yp, yf = (y + 1) % 4, (y + 3) % 4, (y + 2) % 4
    to_x, to_core = {"row_0": oh}, {"row_2": oc}
    to_zn, to_zp = {"row_1": zn}, {"row_1": zp}
    to_l, to_yn, to_yp = {"col_0": ol}, {"col_1": yn}, {"col_1": yp}
    m = tok_ref.shape[0]
    half = m // 2

    own = pltpu.make_async_copy(tok_ref, tk.at[xh, z, core], local_sem.at[0])
    own.start()
    gcopy = pltpu.make_async_copy(gate_ref, gw, local_sem.at[1])
    gcopy.start()
    ucopy = pltpu.make_async_copy(up_ref, uw, local_sem.at[2])
    ucopy.start()
    greet([to_x, to_core, to_zn, to_zp, to_l, to_yn, to_yp])
    own.wait()

    started = []
    A = (a_send, a_recv)

    def block(h, zz, k, lo=0, n=m):
        return tk.at[h, zz, k, pl.ds(lo, n)]

    def send(slot, ref, where):
        copy = remote(ref, ref, A, slot, where)
        copy.start()
        started.append(copy)

    def arrive(slot, ref):
        remote(ref, ref, A, slot, to_x).wait_recv()

    send(0, block(xh, z, core), to_x)
    send(1, block(xh, z, core), to_zn)
    send(3, block(xh, z, core), to_zp)
    send(9, block(xh, z, core), to_core)
    arrive(1, block(xh, zp, core))
    send(5, block(xh, zp, core, 0, half), to_zn)
    arrive(3, block(xh, zn, core))
    send(7, block(xh, zn, core, half, half), to_zp)
    send(10, block(xh, zp, core), to_core)
    send(11, block(xh, zn, core), to_core)
    arrive(0, block(oh, z, core))
    send(2, block(oh, z, core), to_zn)
    send(4, block(oh, z, core), to_zp)
    send(12, block(oh, z, core), to_core)
    arrive(5, block(xh, zf, core, 0, half))
    send(13, block(xh, zf, core, 0, half), to_core)
    arrive(7, block(xh, zf, core, half, half))
    send(14, block(xh, zf, core, half, half), to_core)
    arrive(2, block(oh, zp, core))
    send(6, block(oh, zp, core, 0, half), to_zn)
    arrive(4, block(oh, zn, core))
    send(8, block(oh, zn, core, half, half), to_zp)
    send(15, block(oh, zp, core), to_core)
    send(16, block(oh, zn, core), to_core)
    arrive(6, block(oh, zf, core, 0, half))
    send(17, block(oh, zf, core, 0, half), to_core)
    arrive(8, block(oh, zf, core, half, half))
    send(18, block(oh, zf, core, half, half), to_core)
    for slot, (h, zz) in ((9, (xh, z)), (10, (xh, zp)), (11, (xh, zn)), (12, (oh, z)),
                          (15, (oh, zp)), (16, (oh, zn))):
        arrive(slot, block(h, zz, oc))
    for slot, h in ((13, xh), (17, oh)):
        arrive(slot, block(h, zf, oc, 0, half))
        arrive(slot + 1, block(h, zf, oc, half, half))
    gcopy.wait()
    ucopy.wait()

    R = (r_send, r_recv)
    rows = tg.shape[2]
    hr = rows // 2
    pool = 16 * m
    width = tk.shape[-1]

    def tile(b):
        spots = jnp.concatenate(
            [route_ref[pl.ds(pl.multiple_of((e * 4 + b) * rows, rows), rows), :] for e in range(2)], axis=0
        )
        hot = (spots == lax.broadcasted_iota(jnp.int32, (2 * rows, pool), 1)).astype(F32).astype(BF16)
        chosen = jnp.dot(hot, tk[...].reshape(pool, width), preferred_element_type=F32).astype(BF16)
        g = jnp.dot(chosen, gw[...], preferred_element_type=F32)
        u = jnp.dot(chosen, uw[...], preferred_element_type=F32)
        for e in range(2):
            tg[e, b] = g[e * rows:(e + 1) * rows]
            tu[e, b] = u[e * rows:(e + 1) * rows]

    def rsend(slot, src, dst, where):
        copy = remote(src, dst, R, slot, where)
        copy.start()
        started.append(copy)

    def rarrive(slot, ref):
        remote(ref, ref, R, slot, to_l).wait_recv()

    top, bottom = pl.ds(0, hr), pl.ds(hr, hr)
    tile(yf)
    rsend(0, tg.at[ol, yf], rgx.at[0], to_l)
    rsend(4, tu.at[0, yf], ru1.at[0], to_yn)
    rsend(5, tu.at[1, yf], ru1.at[1], to_yp)
    tile(yn)
    rsend(1, tg.at[ol, yn], rgx.at[1], to_l)
    rsend(6, tu.at[1, yn], ru2.at[0, 1], to_yn)
    tile(yp)
    rsend(2, tg.at[ol, yp], rgx.at[2], to_l)
    rsend(7, tu.at[0, yp], ru2.at[1, 0], to_yp)
    tile(y)
    rsend(3, tg.at[ol, y], rgx.at[3], to_l)
    rarrive(4, ru1.at[0])
    tu[0, yn] = tu[0, yn] + ru1[0]
    rsend(8, tu.at[0, yn], ru2.at[0, 0], to_yn)
    rarrive(5, ru1.at[1])
    tu[1, yp] = tu[1, yp] + ru1[1]
    rsend(9, tu.at[1, yp], ru2.at[1, 1], to_yp)
    rarrive(0, rgx.at[0])
    tg[xl, yf] = tg[xl, yf] + rgx[0]
    rsend(10, tg.at[xl, yf, top], rg1.at[0], to_yn)
    rsend(11, tg.at[xl, yf, bottom], rg1.at[1], to_yp)
    rarrive(1, rgx.at[1])
    tg[xl, yn] = tg[xl, yn] + rgx[1]
    rsend(12, tg.at[xl, yn, bottom], rg2.at[0, bottom], to_yn)
    rarrive(2, rgx.at[2])
    tg[xl, yp] = tg[xl, yp] + rgx[2]
    rsend(13, tg.at[xl, yp, top], rg2.at[1, top], to_yp)
    rarrive(6, ru2.at[0, 1])
    rarrive(8, ru2.at[0, 0])
    rarrive(7, ru2.at[1, 0])
    rarrive(9, ru2.at[1, 1])
    uout[...] = tu[ol, y] + ru2[0, ol] + ru2[1, ol]
    rsend(14, uout, rux, to_l)
    rarrive(10, rg1.at[0])
    tg[xl, yn, top] = tg[xl, yn, top] + rg1[0]
    rsend(15, tg.at[xl, yn, top], rg2.at[0, top], to_yn)
    rarrive(11, rg1.at[1])
    tg[xl, yp, bottom] = tg[xl, yp, bottom] + rg1[1]
    rsend(16, tg.at[xl, yp, bottom], rg2.at[1, bottom], to_yp)
    rarrive(3, rgx.at[3])
    rarrive(12, rg2.at[0, bottom])
    rarrive(13, rg2.at[1, top])
    rarrive(15, rg2.at[0, top])
    rarrive(16, rg2.at[1, bottom])
    rarrive(14, rux)
    gate = tg[xl, y] + rgx[3] + rg2[0] + rg2[1]
    up = tu[xl, y] + ru2[0, xl] + ru2[1, xl] + rux[...]
    mask = live_ref[pl.ds(pl.multiple_of((xl * 4 + y) * rows, rows), rows), :].astype(F32)
    hidden_ref[...] = (gate / (1.0 + jnp.exp(-gate)) * up * mask).astype(BF16)
    for copy in started:
        copy.wait_send()


def hidden_of(tokens, gate_weight, up_weight, route, live):
    m, width = tokens.shape
    own = gate_weight.shape[1]
    rows = route.shape[0] // 8
    hr = rows // 2
    vm = pltpu.VMEM
    hbm = pl.BlockSpec(memory_space=pl.ANY)
    whole = pl.BlockSpec(memory_space=pltpu.VMEM)
    return pl.pallas_call(
        hidden_kernel,
        name="hidden",
        out_shape=jax.ShapeDtypeStruct((rows, own), BF16),
        in_specs=[hbm, hbm, hbm, whole, whole],
        out_specs=whole,
        scratch_shapes=[
            vm((2, 4, 2, m, width), BF16),
            vm(gate_weight.shape, BF16),
            vm(up_weight.shape, BF16),
            vm((2, 4, rows, own), F32),
            vm((2, 4, rows, own), F32),
            vm((4, rows, own), F32),
            vm((2, hr, own), F32),
            vm((2, rows, own), F32),
            vm((2, rows, own), F32),
            vm((2, 2, rows, own), F32),
            vm((rows, own), F32),
            vm((rows, own), F32),
            pltpu.SemaphoreType.DMA((3,)),
            pltpu.SemaphoreType.DMA((19,)),
            pltpu.SemaphoreType.DMA((19,)),
            pltpu.SemaphoreType.DMA((17,)),
            pltpu.SemaphoreType.DMA((17,)),
        ],
        compiler_params=pltpu.CompilerParams(collective_id=0, has_side_effects=True, vmem_limit_bytes=60 * 2**20),
    )(tokens, gate_weight, up_weight, route[:, None], live[:, None])


def joined_along(tiles, dim):
    dims = list(tiles.shape[1:])
    dims[dim] *= tiles.shape[0]
    return jnp.moveaxis(tiles, 0, dim).reshape(dims)


def from_everyone(x, axis):
    devices = lax.axis_size(axis)
    return lax.all_to_all(jnp.broadcast_to(x[None], (devices, *x.shape)), axis, 0, 0, tiled=True)


def collect(x, axis, dim):
    return joined_along(from_everyone(x, axis), dim)


def from_root(x, axis, root):
    return lax.dynamic_index_in_dim(lax.all_gather(x, axis), root, 0, keepdims=False)


def by_axis(x, axes):
    return functools.reduce(lax.psum, axes, x)


def rows_for(lines, devices):
    spare = -len(lines) % devices
    return jnp.pad(lines, [(0, spare)] + [(0, 0)] * (lines.ndim - 1))


def broadcast_by_parts(x, axis, root):
    lines = jnp.where(lax.axis_index(axis) == root, x, jnp.zeros_like(x)).reshape(
        -1, *x.shape[1:][-1:]
    )
    padded = rows_for(lines, lax.axis_size(axis))
    own = lax.psum_scatter(padded, axis, scatter_dimension=0, tiled=True)
    return lax.all_gather(own, axis, axis=0, tiled=True)[: len(lines)].reshape(x.shape)


def per_device(tokens, gate_weight, up_weight, route, live):
    col_count = lax.axis_size(COL)
    col_index = lax.axis_index(COL)
    row_index = lax.axis_index(ROW)
    width = gate_weight.shape[1]
    full = width * lax.axis_size(ROW)
    rows_all = route.shape[0]
    tile_rows = full // col_count
    hidden = hidden_of(tokens, gate_weight, up_weight, route, live)
    stacked = collect(hidden, COL, 0)
    blocks = []
    for half in range(2):
        blocks.append(from_root(stacked, ROW, 2 * col_index + half))
    left = jnp.concatenate(blocks, axis=1)
    gram = lax.dot_general(
        left, stacked, (((0,), (0,)), ((), ())), preferred_element_type=jnp.float32
    )
    down_iota = lax.broadcasted_iota(jnp.int32, (tile_rows, width), 0) + col_index * tile_rows
    across_iota = lax.broadcasted_iota(jnp.int32, (tile_rows, width), 1) + row_index * width
    on_line = down_iota == across_iota
    widened = hidden.astype(jnp.float32)
    term = jnp.sum(widened * widened)
    total = by_axis(term, ROW_COL)
    ridge = damping * total / (rows_all * full)
    matrix = gram / rows_all + jnp.where(on_line, ridge, 0.0)
    corner_block = matrix[0:PANEL, 0:PANEL]
    corner = from_root(corner_block, COL, 0)
    factor = jnp.linalg.cholesky(corner)
    mine = jax.scipy.linalg.solve_triangular(factor, matrix.T, lower=True).T
    panel_down = broadcast_by_parts(mine, ROW, 0)
    offset = row_index % 2 * width
    piece = lax.dynamic_slice_in_dim(panel_down, offset, width, 0)
    panel_across = from_root(piece, COL, row_index // 2)
    matrix = matrix - jnp.dot(
        panel_down,
        panel_across.T,
        precision=lax.Precision.HIGHEST,
        preferred_element_type=jnp.float32,
    )
    return (panel_down, matrix)


def solution(mesh):
    finer = Mesh(mesh.devices.reshape(2, 4, 2, 2, 4), ("row_0", "row_1", "row_2", "col_0", "col_1"))
    placed = (P(ROW, COL), P(COL, ROW), P(COL, ROW), P(), P())
    return jax.shard_map(
        per_device,
        mesh=finer,
        in_specs=placed,
        out_specs=(P(COL, None), P(COL, ROW)),
        check_vma=False,
    )
```

```python
import functools

import jax
import jax.numpy as jnp
from jax import lax
from jax.experimental import pallas as pl
from jax.experimental.pallas import tpu as pltpu
from jax.sharding import Mesh
from jax.sharding import PartitionSpec as P

PANEL = 512
COL = ("col_0", "col_1")
ROW = ("row_0", "row_1", "row_2")
ROW_COL = ("row_0", "row_1", "row_2", "col_0", "col_1")
MESH = pl.DeviceIdType.MESH
F32 = jnp.float32
BF16 = jnp.bfloat16

damping = 0.1


def remote(src, dst, sems, slot, where):
    send, recv = sems
    return pltpu.make_async_remote_copy(
        src_ref=src, dst_ref=dst, send_sem=send.at[slot], recv_sem=recv.at[slot],
        device_id=where, device_id_type=MESH,
    )


def greet(peers):
    barrier = pltpu.get_barrier_semaphore()
    for peer in peers:
        pl.semaphore_signal(barrier, inc=1, device_id=peer, device_id_type=MESH)
    pl.semaphore_wait(barrier, len(peers))


def hidden_kernel(
    tok_ref, gate_ref, up_ref, route_ref, live_ref, hidden_ref,
    tk, gw, uw, tg, tu, rgx, rg1, rg2, ru1, ru2, rux, uout, local_sem,
    a_send, a_recv, r_send, r_recv,
):
    xh, z, core = (lax.axis_index(a) for a in ROW)
    xl, y = (lax.axis_index(a) for a in COL)
    oh, oc, ol = 1 - xh, 1 - core, 1 - xl
    zn, zp, zf = (z + 1) % 4, (z + 3) % 4, (z + 2) % 4
    yn, yp, yf = (y + 1) % 4, (y + 3) % 4, (y + 2) % 4
    to_x, to_core = {"row_0": oh}, {"row_2": oc}
    to_zn, to_zp = {"row_1": zn}, {"row_1": zp}
    to_l, to_yn, to_yp = {"col_0": ol}, {"col_1": yn}, {"col_1": yp}
    m = tok_ref.shape[0]
    half = m // 2

    own = pltpu.make_async_copy(tok_ref, tk.at[xh, z, core], local_sem.at[0])
    own.start()
    gcopy = pltpu.make_async_copy(gate_ref, gw, local_sem.at[1])
    gcopy.start()
    ucopy = pltpu.make_async_copy(up_ref, uw, local_sem.at[2])
    ucopy.start()
    greet([to_x, to_core, to_zn, to_zp, to_l, to_yn, to_yp])
    own.wait()

    started = []
    A = (a_send, a_recv)

    def block(h, zz, k, lo=0, n=m):
        return tk.at[h, zz, k, pl.ds(lo, n)]

    def send(slot, ref, where):
        copy = remote(ref, ref, A, slot, where)
        copy.start()
        started.append(copy)

    def arrive(slot, ref):
        remote(ref, ref, A, slot, to_x).wait_recv()

    send(0, block(xh, z, core), to_x)
    send(1, block(xh, z, core), to_zn)
    send(3, block(xh, z, core), to_zp)
    send(9, block(xh, z, core), to_core)
    arrive(1, block(xh, zp, core))
    send(5, block(xh, zp, core, 0, half), to_zn)
    arrive(3, block(xh, zn, core))
    send(7, block(xh, zn, core, half, half), to_zp)
    send(10, block(xh, zp, core), to_core)
    send(11, block(xh, zn, core), to_core)
    arrive(0, block(oh, z, core))
    send(2, block(oh, z, core), to_zn)
    send(4, block(oh, z, core), to_zp)
    send(12, block(oh, z, core), to_core)
    arrive(5, block(xh, zf, core, 0, half))
    send(13, block(xh, zf, core, 0, half), to_core)
    arrive(7, block(xh, zf, core, half, half))
    send(14, block(xh, zf, core, half, half), to_core)
    arrive(2, block(oh, zp, core))
    send(6, block(oh, zp, core, 0, half), to_zn)
    arrive(4, block(oh, zn, core))
    send(8, block(oh, zn, core, half, half), to_zp)
    send(15, block(oh, zp, core), to_core)
    send(16, block(oh, zn, core), to_core)
    arrive(6, block(oh, zf, core, 0, half))
    send(17, block(oh, zf, core, 0, half), to_core)
    arrive(8, block(oh, zf, core, half, half))
    send(18, block(oh, zf, core, half, half), to_core)
    for slot, (h, zz) in ((9, (xh, z)), (10, (xh, zp)), (11, (xh, zn)), (12, (oh, z)),
                          (15, (oh, zp)), (16, (oh, zn))):
        arrive(slot, block(h, zz, oc))
    for slot, h in ((13, xh), (17, oh)):
        arrive(slot, block(h, zf, oc, 0, half))
        arrive(slot + 1, block(h, zf, oc, half, half))
    gcopy.wait()
    ucopy.wait()

    R = (r_send, r_recv)
    rows = tg.shape[2]
    hr = rows // 2
    pool = 16 * m
    width = tk.shape[-1]

    def tile(b):
        spots = jnp.concatenate(
            [route_ref[pl.ds(pl.multiple_of((e * 4 + b) * rows, rows), rows), :] for e in range(2)], axis=0
        )
        hot = (spots == lax.broadcasted_iota(jnp.int32, (2 * rows, pool), 1)).astype(F32).astype(BF16)
        chosen = jnp.dot(hot, tk[...].reshape(pool, width), preferred_element_type=F32).astype(BF16)
        g = jnp.dot(chosen, gw[...], preferred_element_type=F32)
        u = jnp.dot(chosen, uw[...], preferred_element_type=F32)
        for e in range(2):
            tg[e, b] = g[e * rows:(e + 1) * rows]
            tu[e, b] = u[e * rows:(e + 1) * rows]

    def rsend(slot, src, dst, where):
        copy = remote(src, dst, R, slot, where)
        copy.start()
        started.append(copy)

    def rarrive(slot, ref):
        remote(ref, ref, R, slot, to_l).wait_recv()

    top, bottom = pl.ds(0, hr), pl.ds(hr, hr)
    tile(yf)
    rsend(0, tg.at[ol, yf], rgx.at[0], to_l)
    rsend(4, tu.at[0, yf], ru1.at[0], to_yn)
    rsend(5, tu.at[1, yf], ru1.at[1], to_yp)
    tile(yn)
    rsend(1, tg.at[ol, yn], rgx.at[1], to_l)
    rsend(6, tu.at[1, yn], ru2.at[0, 1], to_yn)
    tile(yp)
    rsend(2, tg.at[ol, yp], rgx.at[2], to_l)
    rsend(7, tu.at[0, yp], ru2.at[1, 0], to_yp)
    tile(y)
    rsend(3, tg.at[ol, y], rgx.at[3], to_l)
    rarrive(4, ru1.at[0])
    tu[0, yn] = tu[0, yn] + ru1[0]
    rsend(8, tu.at[0, yn], ru2.at[0, 0], to_yn)
    rarrive(5, ru1.at[1])
    tu[1, yp] = tu[1, yp] + ru1[1]
    rsend(9, tu.at[1, yp], ru2.at[1, 1], to_yp)
    rarrive(0, rgx.at[0])
    tg[xl, yf] = tg[xl, yf] + rgx[0]
    rsend(10, tg.at[xl, yf, top], rg1.at[0], to_yn)
    rsend(11, tg.at[xl, yf, bottom], rg1.at[1], to_yp)
    rarrive(1, rgx.at[1])
    tg[xl, yn] = tg[xl, yn] + rgx[1]
    rsend(12, tg.at[xl, yn, bottom], rg2.at[0, bottom], to_yn)
    rarrive(2, rgx.at[2])
    tg[xl, yp] = tg[xl, yp] + rgx[2]
    rsend(13, tg.at[xl, yp, top], rg2.at[1, top], to_yp)
    rarrive(6, ru2.at[0, 1])
    rarrive(8, ru2.at[0, 0])
    rarrive(7, ru2.at[1, 0])
    rarrive(9, ru2.at[1, 1])
    uout[...] = tu[ol, y] + ru2[0, ol] + ru2[1, ol]
    rsend(14, uout, rux, to_l)
    rarrive(10, rg1.at[0])
    tg[xl, yn, top] = tg[xl, yn, top] + rg1[0]
    rsend(15, tg.at[xl, yn, top], rg2.at[0, top], to_yn)
    rarrive(11, rg1.at[1])
    tg[xl, yp, bottom] = tg[xl, yp, bottom] + rg1[1]
    rsend(16, tg.at[xl, yp, bottom], rg2.at[1, bottom], to_yp)
    rarrive(3, rgx.at[3])
    rarrive(12, rg2.at[0, bottom])
    rarrive(13, rg2.at[1, top])
    rarrive(15, rg2.at[0, top])
    rarrive(16, rg2.at[1, bottom])
    rarrive(14, rux)
    gate = tg[xl, y] + rgx[3] + rg2[0] + rg2[1]
    up = tu[xl, y] + ru2[0, xl] + ru2[1, xl] + rux[...]
    mask = live_ref[pl.ds(pl.multiple_of((xl * 4 + y) * rows, rows), rows), :].astype(F32)
    hidden_ref[...] = (gate / (1.0 + jnp.exp(-gate)) * up * mask).astype(BF16)
    for copy in started:
        copy.wait_send()


def hidden_of(tokens, gate_weight, up_weight, route, live):
    m, width = tokens.shape
    own = gate_weight.shape[1]
    rows = route.shape[0] // 8
    hr = rows // 2
    vm = pltpu.VMEM
    hbm = pl.BlockSpec(memory_space=pl.ANY)
    whole = pl.BlockSpec(memory_space=pltpu.VMEM)
    return pl.pallas_call(
        hidden_kernel,
        name="hidden",
        out_shape=jax.ShapeDtypeStruct((rows, own), BF16),
        in_specs=[hbm, hbm, hbm, whole, whole],
        out_specs=whole,
        scratch_shapes=[
            vm((2, 4, 2, m, width), BF16),
            vm(gate_weight.shape, BF16),
            vm(up_weight.shape, BF16),
            vm((2, 4, rows, own), F32),
            vm((2, 4, rows, own), F32),
            vm((4, rows, own), F32),
            vm((2, hr, own), F32),
            vm((2, rows, own), F32),
            vm((2, rows, own), F32),
            vm((2, 2, rows, own), F32),
            vm((rows, own), F32),
            vm((rows, own), F32),
            pltpu.SemaphoreType.DMA((3,)),
            pltpu.SemaphoreType.DMA((19,)),
            pltpu.SemaphoreType.DMA((19,)),
            pltpu.SemaphoreType.DMA((17,)),
            pltpu.SemaphoreType.DMA((17,)),
        ],
        compiler_params=pltpu.CompilerParams(collective_id=0, has_side_effects=True, vmem_limit_bytes=60 * 2**20),
    )(tokens, gate_weight, up_weight, route[:, None], live[:, None])


NB = 128
HIGH = lax.Precision.HIGHEST


def spread(x):
    return jnp.broadcast_to(x, (8, NB))


def tile_inverse(rows):
    count = len(rows)
    lane = lax.broadcasted_iota(jnp.int32, (8, NB), 1)
    sub = lax.broadcasted_iota(jnp.int32, (8, NB), 0)
    rows = list(rows)
    out = []
    for g in range(count):
        column = [[spread(rows[i][:, 8 * g + c:8 * g + c + 1]) for c in range(8)] for i in range(g, count)]
        e = [[spread(column[0][b][a:a + 1, :]) for b in range(a + 1)] for a in range(8)]
        inside = (lane >= 8 * g) & (lane < 8 * g + 8)
        rows[g] = jnp.where(inside, (lane == sub + 8 * g).astype(F32), rows[g])
        for i in range(g + 1, count):
            rows[i] = jnp.where(inside, 0.0, rows[i])
        pivots = e[0][0]
        for c in range(8):
            if c:
                pivots = jnp.where(sub == c, e[c][c], pivots)
            inverse = 1.0 / e[c][c]
            for a in range(c + 1, 8):
                factor = e[a][c] * inverse
                for b in range(c + 1, a + 1):
                    e[a][b] = e[a][b] - factor * e[b][c]
            pivot_row = spread(rows[g][c:c + 1, :])
            for i in range(g, count):
                factor = column[i - g][c] * inverse
                if i == g:
                    factor = jnp.where(sub > c, factor, 0.0)
                for b in range(c + 1, 8):
                    column[i - g][b] = column[i - g][b] - factor * e[b][c]
                rows[i] = rows[i] - factor * pivot_row
        out.append(jnp.where(lane <= sub + 8 * g, rows[g] * lax.rsqrt(pivots), 0.0))
    return out


def dot_t(a, b):
    return lax.dot_general(a, b, (((1,), (1,)), ((), ())), precision=HIGH, preferred_element_type=F32)


def dot(a, b):
    return jnp.dot(a, b, precision=HIGH, preferred_element_type=F32)


def factor_inverse(a_ref, x_ref, between):
    n = a_ref.shape[0]
    x_ref[...] = jnp.zeros_like(x_ref)
    for k in range(n // NB):
        lo, hi = k * NB, (k + 1) * NB
        part = tile_inverse([a_ref[lo + 8 * i:lo + 8 * i + 8, lo:hi] for i in range(NB // 8)])
        for i, rows in enumerate(part):
            x_ref[lo + 8 * i:lo + 8 * i + 8, lo:hi] = rows
        x = x_ref[lo:hi, lo:hi]
        if hi < n:
            low = dot_t(a_ref[hi:, lo:hi], x)
            a_ref[hi:, lo:hi] = low
            a_ref[hi:, hi:] = a_ref[hi:, hi:] - dot_t(low, low)
        between(k)
        if k:
            x_ref[lo:hi, :lo] = -dot(x, dot(a_ref[lo:hi, :lo], x_ref[:lo, :lo]))


def cross(a, b):
    return lax.dot_general(a, b, (((0,), (0,)), ((), ())), preferred_element_type=F32)


def factor_kernel(
    total_rows, full, hid_ref, hp_ref, hcol_ref, hl_ref, x_ref, ridge_ref,
    corner, tr, tc, own_sem, p1s, p1r, p2s, p2r, p3s, p3r, ts, tr_sem, us, ur, hs, hr_sem, qs, qr, ls, lr,
):
    xh, z, core = (lax.axis_index(a) for a in ROW)
    xl, y = (lax.axis_index(a) for a in COL)
    oh, oc = 1 - xh, 1 - core
    zn, zp, zf = (z + 1) % 4, (z + 3) % 4, (z + 2) % 4
    ci, ki = xl * 4 + y, xh * 4 + z
    ri = ki * 2 + core
    to_x, to_core = {"row_0": oh}, {"row_2": oc}
    to_zn, to_zp = {"row_1": zn}, {"row_1": zp}
    mirror = {"row_0": xl, "row_1": y, "col_0": xh, "col_1": z}
    away = jnp.logical_or(xh != xl, z != y)
    rows = hid_ref.shape[0]
    half = rows // 2
    col_steps = [(a, b) for a in range(2) for b in range(4) if a + b]
    row_steps = [(a, b, c) for a in range(2) for b in range(4) for c in range(2) if a + b + c]
    col_peer = {s: {"col_0": (xl + s[0]) % 2, "col_1": (y + s[1]) % 4} for s in col_steps}
    col_from = {s: (xl + s[0]) % 2 * 4 + (y + 4 - s[1]) % 4 for s in col_steps}
    row_peer = {s: {"row_0": (xh + s[0]) % 2, "row_1": (z + s[1]) % 4, "row_2": (core + s[2]) % 2} for s in row_steps}
    row_from = {s: ((xh + s[0]) % 2 * 4 + (z + 4 - s[1]) % 4) * 2 + (core + s[2]) % 2 for s in row_steps}

    barrier = pltpu.get_barrier_semaphore()
    for peer in list(col_peer.values()) + list(row_peer.values()):
        pl.semaphore_signal(barrier, inc=1, device_id=peer, device_id_type=MESH)

    @pl.when(away)
    def _():
        pl.semaphore_signal(barrier, inc=1, device_id=mirror, device_id_type=MESH)

    hcopy = pltpu.make_async_copy(hid_ref, hcol_ref.at[ci], own_sem.at[0])
    hcopy.start()
    squares = jnp.zeros((8, 128), F32)
    for i in range(0, rows, 8):
        for j in range(0, hid_ref.shape[1], 128):
            part = hid_ref[pl.ds(i, 8), pl.ds(j, 128)].astype(F32)
            squares = squares + part * part
    tr[ri] = squares
    peers = len(col_steps) + len(row_steps)

    @pl.when(away)
    def _():
        pl.semaphore_wait(barrier, peers + 1)

    @pl.when(jnp.logical_not(away))
    def _():
        pl.semaphore_wait(barrier, peers)

    started = []

    def send(sems, slot, src, dst, where):
        copy = remote(src, dst, sems, slot, where)
        copy.start()
        started.append(copy)

    def arrive(sems, slot, ref):
        remote(ref, ref, sems, slot, to_core).wait_recv()

    mine = hp_ref.at[ci, pl.ds(pl.multiple_of(core * half, half), half)]
    at_root = jnp.logical_and(xh == 0, z == 0)
    holder = jnp.logical_and(at_root, core == 0)
    one = (p1s, p1r)
    give = remote(hid_ref.at[pl.ds(half, half)], hp_ref.at[ci, pl.ds(half, half)], (p1s, p1r), 0, to_core)
    keep = pltpu.make_async_copy(hid_ref.at[pl.ds(0, half)], hp_ref.at[ci, pl.ds(0, half)], own_sem.at[1])
    hop_x = pltpu.make_async_remote_copy(mine, mine, p1s.at[1], p1r.at[0], device_id=to_x, device_id_type=MESH)
    hop_n = pltpu.make_async_remote_copy(mine, mine, p1s.at[2], p1r.at[0], device_id=to_zn, device_id_type=MESH)
    hop_p = pltpu.make_async_remote_copy(mine, mine, p1s.at[3], p1r.at[0], device_id=to_zp, device_id_type=MESH)

    @pl.when(holder)
    def _():
        give.start()
        keep.start()
        keep.wait()

    @pl.when(jnp.logical_not(holder))
    def _():
        arrive(one, 0, mine)

    @pl.when(at_root)
    def _():
        hop_x.start()

    @pl.when(z <= 1)
    def _():
        hop_n.start()

    @pl.when(z == 0)
    def _():
        hop_p.start()

    two, three = (p2s, p2r), (p3s, p3r)
    for s in col_steps:
        send(two, s[0] * 4 + s[1], mine, mine, col_peer[s])
    send(three, 0, mine, mine, to_core)
    for s in row_steps:
        send((ts, tr_sem), s[0] * 8 + s[1] * 2 + s[2], tr.at[ri], tr.at[ri], row_peer[s])

    across = remote(hid_ref, hl_ref.at[core, ci], (qs, qr), 0, mirror)
    stay = pltpu.make_async_copy(hid_ref, hl_ref.at[core, ci], own_sem.at[2])

    @pl.when(away)
    def _():
        across.start()

    @pl.when(jnp.logical_not(away))
    def _():
        stay.start()

    for s in row_steps:
        arrive((ts, tr_sem), s[0] * 8 + s[1] * 2 + s[2], tr.at[row_from[s]])
    tc[ci] = jnp.sum(tr[...], axis=0)
    order = [(0, 1), (0, 3), (1, 0), (0, 2), (1, 1), (1, 3), (1, 2)]
    for s in order[:3]:
        slot = s[0] * 4 + s[1]
        ref = hp_ref.at[col_from[s], pl.ds(pl.multiple_of(core * half, half), half)]
        arrive(two, slot, ref)
        send(three, slot, ref, ref, to_core)
    for s in col_steps:
        send((us, ur), s[0] * 4 + s[1], tc.at[ci], tc.at[ci], col_peer[s])
    for s in order[3:]:
        slot = s[0] * 4 + s[1]
        ref = hp_ref.at[col_from[s], pl.ds(pl.multiple_of(core * half, half), half)]
        arrive(two, slot, ref)
        send(three, slot, ref, ref, to_core)

    four, five, six = (hs, hr_sem), (qs, qr), (ls, lr)

    def block(h, zz, k, lo=0, n=rows):
        return hl_ref.at[k, h * 4 + zz, pl.ds(lo, n)]

    def pass_on(sems, slot, ref, where):
        send(sems, slot, ref, ref, where)

    @pl.when(away)
    def _():
        across.wait_recv()

    @pl.when(jnp.logical_not(away))
    def _():
        stay.wait()

    pass_on(five, 1, block(xh, z, core), to_x)
    pass_on(five, 2, block(xh, z, core), to_zn)
    pass_on(five, 3, block(xh, z, core), to_zp)
    for s in order:
        send(four, s[0] * 4 + s[1], hid_ref, hcol_ref.at[ci], col_peer[s])

    arrive(three, 0, hp_ref.at[ci, pl.ds(pl.multiple_of(oc * half, half), half)])
    for s in order:
        arrive(three, s[0] * 4 + s[1], hp_ref.at[col_from[s], pl.ds(pl.multiple_of(oc * half, half), half)])
    for s in col_steps:
        arrive((us, ur), s[0] * 4 + s[1], tc.at[col_from[s]])
    total = jnp.sum(jnp.sum(tc[...], axis=0), axis=(0, 1), keepdims=True)
    ridge = damping * total / (total_rows * full)
    ridge_ref[...] = jnp.broadcast_to(ridge, (8, 128))
    panel = corner.shape[0]
    hp = hp_ref[...].reshape(total_rows, panel)
    on_line = lax.broadcasted_iota(jnp.int32, (panel, panel), 0) == lax.broadcasted_iota(jnp.int32, (panel, panel), 1)
    corner[...] = cross(hp, hp) / total_rows + jnp.where(on_line, ridge, 0.0)

    def between(k):
        if k == 0:
            pass_on(six, 0, block(xh, z, core), to_core)
            arrive(five, 2, block(xh, zp, core))
            pass_on(five, 4, block(xh, zp, core, 0, half), to_zn)
            pass_on(six, 1, block(xh, zp, core), to_core)
            arrive(five, 3, block(xh, zn, core))
            pass_on(five, 5, block(xh, zn, core, half, half), to_zp)
            pass_on(six, 2, block(xh, zn, core), to_core)
            arrive(five, 1, block(oh, z, core))
            pass_on(five, 6, block(oh, z, core), to_zn)
            pass_on(five, 7, block(oh, z, core), to_zp)
            pass_on(six, 3, block(oh, z, core), to_core)
        elif k == 1:
            arrive(five, 6, block(oh, zp, core))
            pass_on(five, 8, block(oh, zp, core, 0, half), to_zn)
            pass_on(six, 4, block(oh, zp, core), to_core)
            arrive(five, 7, block(oh, zn, core))
            pass_on(five, 9, block(oh, zn, core, half, half), to_zp)
            pass_on(six, 5, block(oh, zn, core), to_core)
        elif k == 2:
            arrive(five, 4, block(xh, zf, core, 0, half))
            arrive(five, 5, block(xh, zf, core, half, half))
            pass_on(six, 6, block(xh, zf, core), to_core)
            arrive(five, 8, block(oh, zf, core, 0, half))
            arrive(five, 9, block(oh, zf, core, half, half))
            pass_on(six, 7, block(oh, zf, core), to_core)

    factor_inverse(corner, x_ref, between)
    for slot, (h, zz) in enumerate(((xh, z), (xh, zp), (xh, zn), (oh, z), (oh, zp), (oh, zn), (xh, zf), (oh, zf))):
        arrive(six, slot, block(h, zz, oc))
    for s in order:
        arrive(four, s[0] * 4 + s[1], hcol_ref.at[col_from[s]])
    hcopy.wait()
    for copy in started:
        copy.wait_send()

    @pl.when(away)
    def _():
        across.wait_send()

    @pl.when(holder)
    def _():
        give.wait_send()

    @pl.when(at_root)
    def _():
        hop_x.wait_send()

    @pl.when(z <= 1)
    def _():
        hop_n.wait_send()

    @pl.when(z == 0)
    def _():
        hop_p.wait_send()


def factor_of(hidden, rows_all, full):
    rows, own = hidden.shape
    whole = pl.BlockSpec(memory_space=pltpu.VMEM)
    dma = pltpu.SemaphoreType.DMA
    return pl.pallas_call(
        functools.partial(factor_kernel, rows_all, full),
        name="factor",
        out_shape=(
            jax.ShapeDtypeStruct((8, rows, own), BF16),
            jax.ShapeDtypeStruct((8, rows, own), BF16),
            jax.ShapeDtypeStruct((2, 8, rows, own), BF16),
            jax.ShapeDtypeStruct((PANEL, PANEL), F32),
            jax.ShapeDtypeStruct((8, 128), F32),
        ),
        in_specs=[whole],
        out_specs=(whole,) * 5,
        scratch_shapes=[
            pltpu.VMEM((PANEL, PANEL), F32),
            pltpu.VMEM((16, 8, 128), F32),
            pltpu.VMEM((8, 8, 128), F32),
            dma((3,)),
            dma((4,)), dma((1,)),
            dma((8,)), dma((8,)),
            dma((8,)), dma((8,)),
            dma((16,)), dma((16,)),
            dma((8,)), dma((8,)),
            dma((8,)), dma((8,)),
            dma((10,)), dma((10,)),
            dma((8,)), dma((8,)),
        ],
        compiler_params=pltpu.CompilerParams(collective_id=1, has_side_effects=True, vmem_limit_bytes=60 * 2**20),
    )(hidden)


def pair(a):
    high = a.astype(BF16)
    return high, (a - high.astype(F32)).astype(BF16)


def dot3_t(a, b):
    def one(u, v):
        return lax.dot_general(u, v, (((1,), (1,)), ((), ())), preferred_element_type=F32)

    return one(a[0], b[0]) + (one(a[0], b[1]) + one(a[1], b[0]))


def outputs_kernel(hp_ref, hcol_ref, hl_ref, x_ref, ridge_ref, panel_ref, trailing_ref):
    xh, z, core = (lax.axis_index(a) for a in ROW)
    xl, y = (lax.axis_index(a) for a in COL)
    ci, ri = xl * 4 + y, (xh * 4 + z) * 2 + core
    rows_all = hp_ref.shape[0] * hp_ref.shape[1]
    n = x_ref.shape[0]
    ridge = ridge_ref[0:1, 0:1]
    on_line = lax.broadcasted_iota(jnp.int32, (n, n), 0) == lax.broadcasted_iota(jnp.int32, (n, n), 1)
    hp = hp_ref[...].reshape(rows_all, n)
    hcol = hcol_ref[...].reshape(rows_all, n)
    x = pair(x_ref[...])

    def with_ridge(gram, here):
        return gram / rows_all + jnp.where(jnp.logical_and(on_line, here), ridge, 0.0)

    right = pair(dot3_t(pair(with_ridge(cross(hcol, hp), ri == 0)), x))
    for j in range(2):
        left = hl_ref[j].reshape(rows_all, n)
        down = dot3_t(pair(with_ridge(cross(left, hp), ci * 2 + j == 0)), x)
        panel_ref[pl.ds(j * n, n), :] = down
        trailing_ref[pl.ds(j * n, n), :] = with_ridge(cross(left, hcol), ci * 2 + j == ri) - dot3_t(pair(down), right)


def outputs_of(hp, hcol, hl, x, ridge):
    n = x.shape[0]
    whole = pl.BlockSpec(memory_space=pltpu.VMEM)
    return pl.pallas_call(
        outputs_kernel,
        name="outputs",
        out_shape=(jax.ShapeDtypeStruct((2 * n, n), F32), jax.ShapeDtypeStruct((2 * n, n), F32)),
        in_specs=[whole] * 5,
        out_specs=(whole, whole),
        compiler_params=pltpu.CompilerParams(vmem_limit_bytes=60 * 2**20),
    )(hp, hcol, hl, x, ridge)


def per_device(tokens, gate_weight, up_weight, route, live):
    full = gate_weight.shape[1] * lax.axis_size(ROW)
    hidden = hidden_of(tokens, gate_weight, up_weight, route, live)
    return outputs_of(*factor_of(hidden, route.shape[0], full))


def solution(mesh):
    finer = Mesh(mesh.devices.reshape(2, 4, 2, 2, 4), ("row_0", "row_1", "row_2", "col_0", "col_1"))
    placed = (P(ROW, COL), P(COL, ROW), P(COL, ROW), P(), P())
    return jax.shard_map(
        per_device,
        mesh=finer,
        in_specs=placed,
        out_specs=(P(COL, None), P(COL, ROW)),
        check_vma=False,
    )
```

```python
import functools

import jax
import jax.numpy as jnp
from jax import lax
from jax.experimental import pallas as pl
from jax.experimental.pallas import tpu as pltpu
from jax.sharding import Mesh
from jax.sharding import PartitionSpec as P

PANEL = 512
COL = ("col_0", "col_1")
ROW = ("row_0", "row_1", "row_2")
ROW_COL = ("row_0", "row_1", "row_2", "col_0", "col_1")
MESH = pl.DeviceIdType.MESH
F32 = jnp.float32
BF16 = jnp.bfloat16

damping = 0.1


def remote(src, dst, sems, slot, where):
    send, recv = sems
    return pltpu.make_async_remote_copy(
        src_ref=src, dst_ref=dst, send_sem=send.at[slot], recv_sem=recv.at[slot],
        device_id=where, device_id_type=MESH,
    )


NB = 128
HIGH = lax.Precision.HIGHEST


def spread(x):
    return jnp.broadcast_to(x, (8, NB))


def tile_inverse(rows):
    count = len(rows)
    lane = lax.broadcasted_iota(jnp.int32, (8, NB), 1)
    sub = lax.broadcasted_iota(jnp.int32, (8, NB), 0)
    rows = list(rows)
    out = []
    for g in range(count):
        column = [[spread(rows[i][:, 8 * g + c:8 * g + c + 1]) for c in range(8)] for i in range(g, count)]
        e = [[spread(column[0][b][a:a + 1, :]) for b in range(a + 1)] for a in range(8)]
        inside = (lane >= 8 * g) & (lane < 8 * g + 8)
        rows[g] = jnp.where(inside, (lane == sub + 8 * g).astype(F32), rows[g])
        for i in range(g + 1, count):
            rows[i] = jnp.where(inside, 0.0, rows[i])
        pivots = e[0][0]
        for c in range(8):
            if c:
                pivots = jnp.where(sub == c, e[c][c], pivots)
            inverse = 1.0 / e[c][c]
            for a in range(c + 1, 8):
                factor = e[a][c] * inverse
                for b in range(c + 1, a + 1):
                    e[a][b] = e[a][b] - factor * e[b][c]
            pivot_row = spread(rows[g][c:c + 1, :])
            for i in range(g, count):
                factor = column[i - g][c] * inverse
                if i == g:
                    factor = jnp.where(sub > c, factor, 0.0)
                for b in range(c + 1, 8):
                    column[i - g][b] = column[i - g][b] - factor * e[b][c]
                rows[i] = rows[i] - factor * pivot_row
        out.append(jnp.where(lane <= sub + 8 * g, rows[g] * lax.rsqrt(pivots), 0.0))
    return out


def dot_t(a, b):
    return lax.dot_general(a, b, (((1,), (1,)), ((), ())), precision=HIGH, preferred_element_type=F32)


def dot(a, b):
    return jnp.dot(a, b, precision=HIGH, preferred_element_type=F32)


def factor_inverse(a_ref, x_ref, between):
    n = a_ref.shape[0]
    x_ref[...] = jnp.zeros_like(x_ref)
    for k in range(n // NB):
        lo, hi = k * NB, (k + 1) * NB
        part = tile_inverse([a_ref[lo + 8 * i:lo + 8 * i + 8, lo:hi] for i in range(NB // 8)])
        for i, rows in enumerate(part):
            x_ref[lo + 8 * i:lo + 8 * i + 8, lo:hi] = rows
        x = x_ref[lo:hi, lo:hi]
        if hi < n:
            low = dot_t(a_ref[hi:, lo:hi], x)
            a_ref[hi:, lo:hi] = low
            a_ref[hi:, hi:] = a_ref[hi:, hi:] - dot_t(low, low)
        between(k)
        if k:
            x_ref[lo:hi, :lo] = -dot(x, dot(a_ref[lo:hi, :lo], x_ref[:lo, :lo]))


def cross(a, b):
    return lax.dot_general(a, b, (((0,), (0,)), ((), ())), preferred_element_type=F32)


def turned(row):
    return jnp.broadcast_to(row, (128, 128)).astype(F32).T


def main_kernel(
    total_rows, full, tok_ref, gate_ref, up_ref, route_ref, live_ref,
    hp_ref, hcol_ref, hl_ref, x_ref, ridge_ref,
    tk, gw, uw, spots, tg, tu, rgx, rg1, rg2, ru1, ru2, rux, uout, hid, corner, tr, tc, own_sem,
    a_send, a_recv, r_send, r_recv, p1s, p1r, p2s, p2r, p3s, p3r, ts, tq, us, ur, hs, hr_sem, qs, qr, ls, lr,
):
    xh, z, core = (lax.axis_index(a) for a in ROW)
    xl, y = (lax.axis_index(a) for a in COL)
    oh, oc, ol = 1 - xh, 1 - core, 1 - xl
    zn, zp, zf = (z + 1) % 4, (z + 3) % 4, (z + 2) % 4
    yn, yp, yf = (y + 1) % 4, (y + 3) % 4, (y + 2) % 4
    ci, ki = xl * 4 + y, xh * 4 + z
    ri = ki * 2 + core
    to_x, to_core = {"row_0": oh}, {"row_2": oc}
    to_zn, to_zp, to_zf = {"row_1": zn}, {"row_1": zp}, {"row_1": zf}
    to_l, to_yn, to_yp = {"col_0": ol}, {"col_1": yn}, {"col_1": yp}
    mirror = {"row_0": xl, "row_1": y, "col_0": xh, "col_1": z}
    away = jnp.logical_or(xh != xl, z != y)
    m = tok_ref.shape[0]
    cut = m * 5 // 8
    col_steps = [(a, b) for a in range(2) for b in range(4) if a + b]
    row_steps = [(a, b, c) for a in range(2) for b in range(4) for c in range(2) if a + b + c]
    col_peer = {s: {"col_0": (xl + s[0]) % 2, "col_1": (y + s[1]) % 4} for s in col_steps}
    col_from = {s: (xl + s[0]) % 2 * 4 + (y + 4 - s[1]) % 4 for s in col_steps}
    row_peer = {s: {"row_0": (xh + s[0]) % 2, "row_1": (z + s[1]) % 4, "row_2": (core + s[2]) % 2} for s in row_steps}
    row_from = {s: ((xh + s[0]) % 2 * 4 + (z + 4 - s[1]) % 4) * 2 + (core + s[2]) % 2 for s in row_steps}

    own = pltpu.make_async_copy(tok_ref, tk.at[xh, z, core], own_sem.at[0])
    own.start()
    gcopy = pltpu.make_async_copy(gate_ref, gw, own_sem.at[1])
    gcopy.start()
    ucopy = pltpu.make_async_copy(up_ref, uw, own_sem.at[2])
    ucopy.start()
    barrier = pltpu.get_barrier_semaphore()
    for peer in list(col_peer.values()) + list(row_peer.values()):
        pl.semaphore_signal(barrier, inc=1, device_id=peer, device_id_type=MESH)

    @pl.when(away)
    def _():
        pl.semaphore_signal(barrier, inc=1, device_id=mirror, device_id_type=MESH)

    rows = total_rows // 8
    for t in range(8):
        spots[pl.ds(t * rows, rows), :] = turned(route_ref[t:t + 1, :]).astype(jnp.int32)
    own.wait()
    peers = len(col_steps) + len(row_steps)

    @pl.when(away)
    def _():
        pl.semaphore_wait(barrier, peers + 1)

    @pl.when(jnp.logical_not(away))
    def _():
        pl.semaphore_wait(barrier, peers)

    started = []

    def send(sems, slot, src, dst, where):
        copy = remote(src, dst, sems, slot, where)
        copy.start()
        started.append(copy)

    def arrive(sems, slot, ref):
        remote(ref, ref, sems, slot, to_core).wait_recv()

    def pass_on(sems, slot, ref, where):
        send(sems, slot, ref, ref, where)

    A = (a_send, a_recv)

    def block(h, zz, k, lo=0, n=m):
        return tk.at[h, zz, k, pl.ds(lo, n)]

    pass_on(A, 0, block(xh, z, core), to_x)
    pass_on(A, 1, block(xh, z, core), to_zn)
    pass_on(A, 2, block(xh, z, core), to_zp)
    pass_on(A, 3, block(xh, z, core), to_zf)
    pass_on(A, 10, block(xh, z, core), to_core)
    arrive(A, 1, block(xh, zp, core))
    pass_on(A, 7, block(xh, zp, core, cut, m - cut), to_x)
    pass_on(A, 11, block(xh, zp, core), to_core)
    arrive(A, 2, block(xh, zn, core))
    pass_on(A, 8, block(xh, zn, core, cut, m - cut), to_x)
    pass_on(A, 12, block(xh, zn, core), to_core)
    arrive(A, 0, block(oh, z, core))
    pass_on(A, 4, block(oh, z, core, 0, cut), to_zn)
    pass_on(A, 5, block(oh, z, core, 0, cut), to_zp)
    pass_on(A, 6, block(oh, z, core, 0, cut), to_zf)
    pass_on(A, 14, block(oh, z, core), to_core)
    arrive(A, 3, block(xh, zf, core))
    pass_on(A, 9, block(xh, zf, core, cut, m - cut), to_x)
    pass_on(A, 13, block(xh, zf, core), to_core)
    for slot, zz in ((0, zp), (1, zn), (2, zf)):
        arrive(A, 4 + slot, block(oh, zz, core, 0, cut))
        arrive(A, 7 + slot, block(oh, zz, core, cut, m - cut))
        pass_on(A, 15 + slot, block(oh, zz, core), to_core)
    for slot, (h, zz) in enumerate(((xh, z), (xh, zp), (xh, zn), (xh, zf), (oh, z), (oh, zp), (oh, zn), (oh, zf))):
        arrive(A, 10 + slot, block(h, zz, oc))
    gcopy.wait()
    ucopy.wait()

    R = (r_send, r_recv)
    hr = rows // 2
    pool = 16 * m
    width = tk.shape[-1]

    def tile(b):
        spot = jnp.concatenate(
            [spots[pl.ds(pl.multiple_of((e * 4 + b) * rows, rows), rows), :] for e in range(2)], axis=0
        )
        spot = jnp.concatenate([spot] * (pool // 128), axis=1)
        hot = (spot == lax.broadcasted_iota(jnp.int32, (2 * rows, pool), 1)).astype(F32).astype(BF16)
        chosen = jnp.dot(hot, tk[...].reshape(pool, width), preferred_element_type=F32).astype(BF16)
        g = jnp.dot(chosen, gw[...], preferred_element_type=F32)
        u = jnp.dot(chosen, uw[...], preferred_element_type=F32)
        for e in range(2):
            tg[e, b] = g[e * rows:(e + 1) * rows]
            tu[e, b] = u[e * rows:(e + 1) * rows]

    top, bottom = pl.ds(0, hr), pl.ds(hr, hr)
    tile(yf)
    send(R, 0, tg.at[ol, yf], rgx.at[0], to_l)
    send(R, 4, tu.at[0, yf], ru1.at[0], to_yn)
    send(R, 5, tu.at[1, yf], ru1.at[1], to_yp)
    tile(yn)
    send(R, 1, tg.at[ol, yn], rgx.at[1], to_l)
    send(R, 6, tu.at[1, yn], ru2.at[0, 1], to_yn)
    tile(yp)
    send(R, 2, tg.at[ol, yp], rgx.at[2], to_l)
    send(R, 7, tu.at[0, yp], ru2.at[1, 0], to_yp)
    tile(y)
    send(R, 3, tg.at[ol, y], rgx.at[3], to_l)
    arrive(R, 4, ru1.at[0])
    tu[0, yn] = tu[0, yn] + ru1[0]
    send(R, 8, tu.at[0, yn], ru2.at[0, 0], to_yn)
    arrive(R, 5, ru1.at[1])
    tu[1, yp] = tu[1, yp] + ru1[1]
    send(R, 9, tu.at[1, yp], ru2.at[1, 1], to_yp)
    arrive(R, 0, rgx.at[0])
    tg[xl, yf] = tg[xl, yf] + rgx[0]
    send(R, 10, tg.at[xl, yf, top], rg1.at[0], to_yn)
    send(R, 11, tg.at[xl, yf, bottom], rg1.at[1], to_yp)
    arrive(R, 1, rgx.at[1])
    tg[xl, yn] = tg[xl, yn] + rgx[1]
    send(R, 12, tg.at[xl, yn, bottom], rg2.at[0, bottom], to_yn)
    arrive(R, 2, rgx.at[2])
    tg[xl, yp] = tg[xl, yp] + rgx[2]
    send(R, 13, tg.at[xl, yp, top], rg2.at[1, top], to_yp)
    arrive(R, 6, ru2.at[0, 1])
    arrive(R, 8, ru2.at[0, 0])
    arrive(R, 7, ru2.at[1, 0])
    arrive(R, 9, ru2.at[1, 1])
    uout[...] = tu[ol, y] + ru2[0, ol] + ru2[1, ol]
    send(R, 14, uout, rux, to_l)
    arrive(R, 10, rg1.at[0])
    tg[xl, yn, top] = tg[xl, yn, top] + rg1[0]
    send(R, 15, tg.at[xl, yn, top], rg2.at[0, top], to_yn)
    arrive(R, 11, rg1.at[1])
    tg[xl, yp, bottom] = tg[xl, yp, bottom] + rg1[1]
    send(R, 16, tg.at[xl, yp, bottom], rg2.at[1, bottom], to_yp)
    mask = jnp.concatenate([turned(live_ref[pl.ds(ci, 1), :])] * (hid.shape[1] // 128), axis=1)
    arrive(R, 3, rgx.at[3])
    arrive(R, 12, rg2.at[0, bottom])
    arrive(R, 13, rg2.at[1, top])
    arrive(R, 15, rg2.at[0, top])
    arrive(R, 16, rg2.at[1, bottom])
    gate = tg[xl, y] + rgx[3] + rg2[0] + rg2[1]
    part = tu[xl, y] + ru2[0, xl] + ru2[1, xl]
    act = gate / (1.0 + jnp.exp(-gate)) * mask
    arrive(R, 14, rux)
    made = (act * (part + rux[...])).astype(BF16)
    hid[...] = made
    hcol_ref[ci] = made

    half = rows // 2
    at_root = jnp.logical_and(xh == 0, z == 0)
    holder = jnp.logical_and(at_root, core == 0)

    def by_half(c, k):
        return hp_ref.at[c, pl.ds(pl.multiple_of(k * half, half), half)]

    mine = by_half(ci, core)
    give = remote(hid.at[pl.ds(half, half)], hp_ref.at[ci, pl.ds(half, half)], (p1s, p1r), 0, to_core)
    hops = [
        pltpu.make_async_remote_copy(mine, mine, p1s.at[1 + i], p1r.at[0], device_id=where, device_id_type=MESH)
        for i, where in enumerate((to_x, to_zn, to_zp, to_zf))
    ]

    @pl.when(holder)
    def _():
        hp_ref[ci, pl.ds(0, half)] = made[:half]
        give.start()

    wide = made.astype(F32)
    squares = jnp.zeros((8, 128), F32)
    for i in range(0, rows, 8):
        for j in range(0, hid.shape[1], 128):
            piece = wide[i:i + 8, j:j + 128]
            squares = squares + piece * piece
    tr[ri] = squares
    for s in row_steps:
        send((ts, tq), s[0] * 8 + s[1] * 2 + s[2], tr.at[ri], tr.at[ri], row_peer[s])

    @pl.when(jnp.logical_not(holder))
    def _():
        arrive((p1s, p1r), 0, mine)

    @pl.when(at_root)
    def _():
        hops[0].start()

    @pl.when(z == 0)
    def _():
        for hop in hops[1:]:
            hop.start()

    two, three = (p2s, p2r), (p3s, p3r)
    order = [(1, 2), (1, 1), (1, 3), (0, 2), (0, 1), (0, 3), (1, 0)]
    for s in order:
        send(two, s[0] * 4 + s[1], mine, mine, col_peer[s])
    pass_on(three, 0, mine, to_core)
    across = remote(hid, hl_ref.at[core, ci], (qs, qr), 0, mirror)
    stay = pltpu.make_async_copy(hid, hl_ref.at[core, ci], own_sem.at[0])

    @pl.when(away)
    def _():
        across.start()

    @pl.when(jnp.logical_not(away))
    def _():
        stay.start()

    four, five, six = (hs, hr_sem), (qs, qr), (ls, lr)
    for s in order:
        send(four, s[0] * 4 + s[1], hid, hcol_ref.at[ci], col_peer[s])
    for s in row_steps:
        arrive((ts, tq), s[0] * 8 + s[1] * 2 + s[2], tr.at[row_from[s]])
    tc[ci] = jnp.sum(tr[...], axis=0)
    for s in col_steps:
        send((us, ur), s[0] * 4 + s[1], tc.at[ci], tc.at[ci], col_peer[s])
    for s in order[::-1]:
        slot = s[0] * 4 + s[1]
        arrive(two, slot, by_half(col_from[s], core))
        pass_on(three, slot, by_half(col_from[s], core), to_core)

    def spread_block(h, zz, k):
        return hl_ref.at[k, h * 4 + zz]

    here = spread_block(xh, z, core)

    @pl.when(away)
    def _():
        across.wait_recv()

    @pl.when(jnp.logical_not(away))
    def _():
        stay.wait()

    for slot, where in ((1, to_x), (2, to_zn), (3, to_zp), (4, to_zf)):
        pass_on(five, slot, here, where)
    arrive(three, 0, by_half(ci, oc))
    for s in order[::-1]:
        arrive(three, s[0] * 4 + s[1], by_half(col_from[s], oc))
    panel = corner.shape[0]
    hp = hp_ref[...].reshape(total_rows, panel)
    on_line = lax.broadcasted_iota(jnp.int32, (panel, panel), 0) == lax.broadcasted_iota(jnp.int32, (panel, panel), 1)
    gram = cross(hp, hp) / total_rows
    for s in col_steps:
        arrive((us, ur), s[0] * 4 + s[1], tc.at[col_from[s]])
    total = jnp.sum(jnp.sum(tc[...], axis=0), axis=(0, 1), keepdims=True)
    ridge = damping * total / (total_rows * full)
    ridge_ref[...] = jnp.broadcast_to(ridge, (8, 128))
    corner[...] = gram + jnp.where(on_line, ridge, 0.0)

    def between(k):
        if k == 0:
            pass_on(six, 0, here, to_core)
            arrive(five, 1, spread_block(oh, z, core))
            for slot, where in ((5, to_zn), (6, to_zp), (7, to_zf)):
                pass_on(five, slot, spread_block(oh, z, core), where)
            pass_on(six, 1, spread_block(oh, z, core), to_core)
        elif k == 1:
            for slot, zz in ((2, zp), (3, zn), (4, zf)):
                arrive(five, slot, spread_block(xh, zz, core))
                pass_on(six, slot, spread_block(xh, zz, core), to_core)
        elif k == 2:
            for slot, zz in ((5, zp), (6, zn), (7, zf)):
                arrive(five, slot, spread_block(oh, zz, core))
                pass_on(six, slot, spread_block(oh, zz, core), to_core)

    factor_inverse(corner, x_ref, between)
    for slot, (h, zz) in enumerate(((xh, z), (oh, z), (xh, zp), (xh, zn), (xh, zf), (oh, zp), (oh, zn), (oh, zf))):
        arrive(six, slot, spread_block(h, zz, oc))
    for s in order:
        arrive(four, s[0] * 4 + s[1], hcol_ref.at[col_from[s]])
    for copy in started:
        copy.wait_send()

    @pl.when(away)
    def _():
        across.wait_send()

    @pl.when(holder)
    def _():
        give.wait_send()

    @pl.when(at_root)
    def _():
        hops[0].wait_send()

    @pl.when(z == 0)
    def _():
        for hop in hops[1:]:
            hop.wait_send()


def main_of(tokens, gate_weight, up_weight, route, live, full):
    m, width = tokens.shape
    own = gate_weight.shape[1]
    rows_all = route.shape[0]
    rows = rows_all // 8
    hr = rows // 2
    vm = pltpu.VMEM
    dma = pltpu.SemaphoreType.DMA
    hbm = pl.BlockSpec(memory_space=pl.ANY)
    whole = pl.BlockSpec(memory_space=pltpu.VMEM)
    return pl.pallas_call(
        functools.partial(main_kernel, rows_all, full),
        name="hidden_factor",
        out_shape=(
            jax.ShapeDtypeStruct((8, rows, own), BF16),
            jax.ShapeDtypeStruct((8, rows, own), BF16),
            jax.ShapeDtypeStruct((2, 8, rows, own), BF16),
            jax.ShapeDtypeStruct((PANEL, PANEL), F32),
            jax.ShapeDtypeStruct((8, 128), F32),
        ),
        in_specs=[hbm, hbm, hbm, whole, whole],
        out_specs=(whole,) * 5,
        scratch_shapes=[
            vm((2, 4, 2, m, width), BF16),
            vm(gate_weight.shape, BF16),
            vm(up_weight.shape, BF16),
            vm((rows_all, 128), jnp.int32),
            vm((2, 4, rows, own), F32),
            vm((2, 4, rows, own), F32),
            vm((4, rows, own), F32),
            vm((2, hr, own), F32),
            vm((2, rows, own), F32),
            vm((2, rows, own), F32),
            vm((2, 2, rows, own), F32),
            vm((rows, own), F32),
            vm((rows, own), F32),
            vm((rows, own), BF16),
            vm((PANEL, PANEL), F32),
            vm((16, 8, 128), F32),
            vm((8, 8, 128), F32),
            dma((3,)),
            dma((18,)), dma((18,)),
            dma((17,)), dma((17,)),
            dma((5,)), dma((1,)),
            dma((8,)), dma((8,)),
            dma((8,)), dma((8,)),
            dma((16,)), dma((16,)),
            dma((8,)), dma((8,)),
            dma((8,)), dma((8,)),
            dma((8,)), dma((8,)),
            dma((8,)), dma((8,)),
        ],
        compiler_params=pltpu.CompilerParams(collective_id=0, has_side_effects=True, vmem_limit_bytes=60 * 2**20),
    )(tokens, gate_weight, up_weight, route.reshape(8, rows), live.reshape(8, rows))


def pair(a):
    high = a.astype(BF16)
    return high, (a - high.astype(F32)).astype(BF16)


def dot3_t(a, b):
    def one(u, v):
        return lax.dot_general(u, v, (((1,), (1,)), ((), ())), preferred_element_type=F32)

    return one(a[0], b[0]) + (one(a[0], b[1]) + one(a[1], b[0]))


def outputs_kernel(hp_ref, hcol_ref, hl_ref, x_ref, ridge_ref, panel_ref, trailing_ref):
    xh, z, core = (lax.axis_index(a) for a in ROW)
    xl, y = (lax.axis_index(a) for a in COL)
    ci, ri = xl * 4 + y, (xh * 4 + z) * 2 + core
    rows_all = hp_ref.shape[0] * hp_ref.shape[1]
    n = x_ref.shape[0]
    ridge = ridge_ref[0:1, 0:1]
    on_line = lax.broadcasted_iota(jnp.int32, (n, n), 0) == lax.broadcasted_iota(jnp.int32, (n, n), 1)
    hp = hp_ref[...].reshape(rows_all, n)
    hcol = hcol_ref[...].reshape(rows_all, n)
    x = pair(x_ref[...])

    def with_ridge(gram, here):
        return gram / rows_all + jnp.where(jnp.logical_and(on_line, here), ridge, 0.0)

    right = pair(dot3_t(pair(with_ridge(cross(hcol, hp), ri == 0)), x))
    for j in range(2):
        left = hl_ref[j].reshape(rows_all, n)
        down = dot3_t(pair(with_ridge(cross(left, hp), ci * 2 + j == 0)), x)
        panel_ref[pl.ds(j * n, n), :] = down
        trailing_ref[pl.ds(j * n, n), :] = with_ridge(cross(left, hcol), ci * 2 + j == ri) - dot3_t(pair(down), right)


def outputs_of(hp, hcol, hl, x, ridge):
    n = x.shape[0]
    whole = pl.BlockSpec(memory_space=pltpu.VMEM)
    return pl.pallas_call(
        outputs_kernel,
        name="outputs",
        out_shape=(jax.ShapeDtypeStruct((2 * n, n), F32), jax.ShapeDtypeStruct((2 * n, n), F32)),
        in_specs=[whole] * 5,
        out_specs=(whole, whole),
        compiler_params=pltpu.CompilerParams(vmem_limit_bytes=60 * 2**20),
    )(hp, hcol, hl, x, ridge)


def per_device(tokens, gate_weight, up_weight, route, live):
    full = gate_weight.shape[1] * lax.axis_size(ROW)
    return outputs_of(*main_of(tokens, gate_weight, up_weight, route, live, full))


def solution(mesh):
    finer = Mesh(mesh.devices.reshape(2, 4, 2, 2, 4), ("row_0", "row_1", "row_2", "col_0", "col_1"))
    placed = (P(ROW, COL), P(COL, ROW), P(COL, ROW), P(), P())
    return jax.shard_map(
        per_device,
        mesh=finer,
        in_specs=placed,
        out_specs=(P(COL, None), P(COL, ROW)),
        check_vma=False,
    )
```

```python
import functools

import jax
import jax.numpy as jnp
from jax import lax
from jax.experimental import pallas as pl
from jax.experimental.pallas import tpu as pltpu
from jax.sharding import Mesh
from jax.sharding import PartitionSpec as P

PANEL = 512
COL = ("col_0", "col_1")
ROW = ("row_0", "row_1", "row_2")
ROW_COL = ("row_0", "row_1", "row_2", "col_0", "col_1")
MESH = pl.DeviceIdType.MESH
F32 = jnp.float32
BF16 = jnp.bfloat16

damping = 0.1


def remote(src, dst, sems, slot, where):
    send, recv = sems
    return pltpu.make_async_remote_copy(
        src_ref=src, dst_ref=dst, send_sem=send.at[slot], recv_sem=recv.at[slot],
        device_id=where, device_id_type=MESH,
    )


NB = 128
HIGH = lax.Precision.HIGHEST


def spread(x):
    return jnp.broadcast_to(x, (8, NB))


def tile_inverse(rows, halfway):
    count = len(rows)
    lane = lax.broadcasted_iota(jnp.int32, (8, NB), 1)
    sub = lax.broadcasted_iota(jnp.int32, (8, NB), 0)
    rows = list(rows)
    out = []
    for g in range(count):
        column = [[spread(rows[i][:, 8 * g + c:8 * g + c + 1]) for c in range(8)] for i in range(g, count)]
        e = [[spread(column[0][b][a:a + 1, :]) for b in range(a + 1)] for a in range(8)]
        inside = (lane >= 8 * g) & (lane < 8 * g + 8)
        rows[g] = jnp.where(inside, (lane == sub + 8 * g).astype(F32), rows[g])
        for i in range(g + 1, count):
            rows[i] = jnp.where(inside, 0.0, rows[i])
        pivots = e[0][0]
        for c in range(8):
            if c:
                pivots = jnp.where(sub == c, e[c][c], pivots)
            if c % 2 == 0:
                inverse = 1.0 / e[c][c]
                later = e[c][c] / (e[c][c] * e[c + 1][c + 1] - e[c + 1][c] * e[c + 1][c])
            else:
                inverse = later
            for a in range(c + 1, 8):
                factor = e[a][c] * inverse
                for b in range(c + 1, a + 1):
                    e[a][b] = e[a][b] - factor * e[b][c]
            pivot_row = spread(rows[g][c:c + 1, :])
            for i in range(g, count):
                factor = column[i - g][c] * inverse
                if i == g:
                    factor = jnp.where(sub > c, factor, 0.0)
                for b in range(c + 1, 8):
                    column[i - g][b] = column[i - g][b] - factor * e[b][c]
                rows[i] = rows[i] - factor * pivot_row
        out.append(jnp.where(lane <= sub + 8 * g, rows[g] * lax.rsqrt(pivots), 0.0))
        if g == count // 2 - 1:
            halfway()
    return out


def dot_t(a, b):
    return lax.dot_general(a, b, (((1,), (1,)), ((), ())), precision=HIGH, preferred_element_type=F32)


def dot(a, b):
    return jnp.dot(a, b, precision=HIGH, preferred_element_type=F32)


def factor_inverse(a_ref, x_ref, between):
    n = a_ref.shape[0]
    x_ref[...] = jnp.zeros_like(x_ref)
    for k in range(n // NB):
        lo, hi = k * NB, (k + 1) * NB
        part = tile_inverse(
            [a_ref[lo + 8 * i:lo + 8 * i + 8, lo:hi] for i in range(NB // 8)], lambda: between(2 * k)
        )
        for i, rows in enumerate(part):
            x_ref[lo + 8 * i:lo + 8 * i + 8, lo:hi] = rows
        x = x_ref[lo:hi, lo:hi]
        if hi < n:
            low = dot_t(a_ref[hi:, lo:hi], x)
            a_ref[hi:, lo:hi] = low
            a_ref[hi:, hi:] = a_ref[hi:, hi:] - dot_t(low, low)
        between(2 * k + 1)
        if k:
            x_ref[lo:hi, :lo] = -dot(x, dot(a_ref[lo:hi, :lo], x_ref[:lo, :lo]))


def cross(a, b):
    return lax.dot_general(a, b, (((0,), (0,)), ((), ())), preferred_element_type=F32)


def turned(row):
    return jnp.broadcast_to(row, (128, 128)).astype(F32).T


def main_kernel(
    total_rows, full, tok_ref, gate_ref, up_ref, route_ref, live_ref,
    hp_ref, hcol_ref, hl_ref, x_ref, ridge_ref,
    tk, gw, uw, spots, tg, tu, rgx, rg1, rg2, ru1, ru2, rux, uout, hid, corner, tr, tc, own_sem,
    a_send, a_recv, r_send, r_recv, p1s, p1r, p2s, p2r, p3s, p3r, ts, tq, us, ur, hs, hr_sem, qs, qr, ls, lr,
):
    xh, z, core = (lax.axis_index(a) for a in ROW)
    xl, y = (lax.axis_index(a) for a in COL)
    oh, oc, ol = 1 - xh, 1 - core, 1 - xl
    zn, zp, zf = (z + 1) % 4, (z + 3) % 4, (z + 2) % 4
    yn, yp, yf = (y + 1) % 4, (y + 3) % 4, (y + 2) % 4
    ci, ki = xl * 4 + y, xh * 4 + z
    ri = ki * 2 + core
    to_x, to_core = {"row_0": oh}, {"row_2": oc}
    to_zn, to_zp, to_zf = {"row_1": zn}, {"row_1": zp}, {"row_1": zf}
    to_l, to_yn, to_yp = {"col_0": ol}, {"col_1": yn}, {"col_1": yp}
    mirror = {"row_0": xl, "row_1": y, "col_0": xh, "col_1": z}
    away = jnp.logical_or(xh != xl, z != y)
    m = tok_ref.shape[0]
    cut = m * 5 // 8
    col_steps = [(a, b) for a in range(2) for b in range(4) if a + b]
    row_steps = [(a, b, c) for a in range(2) for b in range(4) for c in range(2) if a + b + c]
    col_peer = {s: {"col_0": (xl + s[0]) % 2, "col_1": (y + s[1]) % 4} for s in col_steps}
    col_from = {s: (xl + s[0]) % 2 * 4 + (y + 4 - s[1]) % 4 for s in col_steps}
    row_peer = {s: {"row_0": (xh + s[0]) % 2, "row_1": (z + s[1]) % 4, "row_2": (core + s[2]) % 2} for s in row_steps}
    row_from = {s: ((xh + s[0]) % 2 * 4 + (z + 4 - s[1]) % 4) * 2 + (core + s[2]) % 2 for s in row_steps}

    own = pltpu.make_async_copy(tok_ref, tk.at[xh, z, core], own_sem.at[0])
    own.start()
    gcopy = pltpu.make_async_copy(gate_ref, gw, own_sem.at[1])
    gcopy.start()
    ucopy = pltpu.make_async_copy(up_ref, uw, own_sem.at[2])
    ucopy.start()
    barrier = pltpu.get_barrier_semaphore()
    for peer in list(col_peer.values()) + list(row_peer.values()):
        pl.semaphore_signal(barrier, inc=1, device_id=peer, device_id_type=MESH)

    @pl.when(away)
    def _():
        pl.semaphore_signal(barrier, inc=1, device_id=mirror, device_id_type=MESH)

    rows = total_rows // 8
    for t in range(8):
        spots[pl.ds(t * rows, rows), :] = turned(route_ref[t:t + 1, :]).astype(jnp.int32)
    own.wait()
    peers = len(col_steps) + len(row_steps)

    @pl.when(away)
    def _():
        pl.semaphore_wait(barrier, peers + 1)

    @pl.when(jnp.logical_not(away))
    def _():
        pl.semaphore_wait(barrier, peers)

    started = []

    def send(sems, slot, src, dst, where):
        copy = remote(src, dst, sems, slot, where)
        copy.start()
        started.append(copy)

    def arrive(sems, slot, ref):
        remote(ref, ref, sems, slot, to_core).wait_recv()

    def pass_on(sems, slot, ref, where):
        send(sems, slot, ref, ref, where)

    A = (a_send, a_recv)

    def block(h, zz, k, lo=0, n=m):
        return tk.at[h, zz, k, pl.ds(lo, n)]

    pass_on(A, 0, block(xh, z, core), to_x)
    pass_on(A, 1, block(xh, z, core), to_zn)
    pass_on(A, 2, block(xh, z, core), to_zp)
    pass_on(A, 3, block(xh, z, core), to_zf)
    pass_on(A, 10, block(xh, z, core), to_core)
    arrive(A, 1, block(xh, zp, core))
    pass_on(A, 7, block(xh, zp, core, cut, m - cut), to_x)
    pass_on(A, 11, block(xh, zp, core), to_core)
    arrive(A, 2, block(xh, zn, core))
    pass_on(A, 8, block(xh, zn, core, cut, m - cut), to_x)
    pass_on(A, 12, block(xh, zn, core), to_core)
    arrive(A, 0, block(oh, z, core))
    pass_on(A, 4, block(oh, z, core, 0, cut), to_zn)
    pass_on(A, 5, block(oh, z, core, 0, cut), to_zp)
    pass_on(A, 6, block(oh, z, core, 0, cut), to_zf)
    pass_on(A, 14, block(oh, z, core), to_core)
    arrive(A, 3, block(xh, zf, core))
    pass_on(A, 9, block(xh, zf, core, cut, m - cut), to_x)
    pass_on(A, 13, block(xh, zf, core), to_core)
    for slot, zz in ((0, zp), (1, zn), (2, zf)):
        arrive(A, 4 + slot, block(oh, zz, core, 0, cut))
        pass_on(A, 15 + slot, block(oh, zz, core, 0, cut), to_core)
        arrive(A, 7 + slot, block(oh, zz, core, cut, m - cut))
        pass_on(A, 18 + slot, block(oh, zz, core, cut, m - cut), to_core)
    for slot, (h, zz) in enumerate(((xh, z), (xh, zp), (xh, zn), (xh, zf), (oh, z))):
        arrive(A, 10 + slot, block(h, zz, oc))
    for slot, zz in ((0, zp), (1, zn), (2, zf)):
        arrive(A, 15 + slot, block(oh, zz, oc, 0, cut))
        arrive(A, 18 + slot, block(oh, zz, oc, cut, m - cut))
    gcopy.wait()
    ucopy.wait()

    R = (r_send, r_recv)
    hr = rows // 2
    pool = 16 * m
    width = tk.shape[-1]

    def tile(b):
        spot = jnp.concatenate(
            [spots[pl.ds(pl.multiple_of((e * 4 + b) * rows, rows), rows), :] for e in range(2)], axis=0
        )
        spot = jnp.concatenate([spot] * (pool // 128), axis=1)
        hot = (spot == lax.broadcasted_iota(jnp.int32, (2 * rows, pool), 1)).astype(F32).astype(BF16)
        chosen = jnp.dot(hot, tk[...].reshape(pool, width), preferred_element_type=F32).astype(BF16)
        g = jnp.dot(chosen, gw[...], preferred_element_type=F32)
        u = jnp.dot(chosen, uw[...], preferred_element_type=F32)
        for e in range(2):
            tg[e, b] = g[e * rows:(e + 1) * rows]
            tu[e, b] = u[e * rows:(e + 1) * rows]

    top, bottom = pl.ds(0, hr), pl.ds(hr, hr)
    tile(yf)
    send(R, 0, tg.at[ol, yf], rgx.at[0], to_l)
    send(R, 4, tu.at[0, yf], ru1.at[0], to_yn)
    send(R, 5, tu.at[1, yf], ru1.at[1], to_yp)
    tile(yn)
    send(R, 1, tg.at[ol, yn], rgx.at[1], to_l)
    send(R, 6, tu.at[1, yn], ru2.at[0, 1], to_yn)
    tile(yp)
    send(R, 2, tg.at[ol, yp], rgx.at[2], to_l)
    send(R, 7, tu.at[0, yp], ru2.at[1, 0], to_yp)
    tile(y)
    send(R, 3, tg.at[ol, y], rgx.at[3], to_l)
    arrive(R, 4, ru1.at[0])
    tu[0, yn] = tu[0, yn] + ru1[0]
    send(R, 8, tu.at[0, yn], ru2.at[0, 0], to_yn)
    arrive(R, 5, ru1.at[1])
    tu[1, yp] = tu[1, yp] + ru1[1]
    send(R, 9, tu.at[1, yp], ru2.at[1, 1], to_yp)
    arrive(R, 0, rgx.at[0])
    tg[xl, yf] = tg[xl, yf] + rgx[0]
    send(R, 10, tg.at[xl, yf, top], rg1.at[0], to_yn)
    send(R, 11, tg.at[xl, yf, bottom], rg1.at[1], to_yp)
    arrive(R, 1, rgx.at[1])
    tg[xl, yn] = tg[xl, yn] + rgx[1]
    send(R, 12, tg.at[xl, yn, bottom], rg2.at[0, bottom], to_yn)
    arrive(R, 2, rgx.at[2])
    tg[xl, yp] = tg[xl, yp] + rgx[2]
    send(R, 13, tg.at[xl, yp, top], rg2.at[1, top], to_yp)
    arrive(R, 6, ru2.at[0, 1])
    arrive(R, 8, ru2.at[0, 0])
    arrive(R, 7, ru2.at[1, 0])
    arrive(R, 9, ru2.at[1, 1])
    uout[...] = tu[ol, y] + ru2[0, ol] + ru2[1, ol]
    send(R, 14, uout, rux, to_l)
    arrive(R, 10, rg1.at[0])
    tg[xl, yn, top] = tg[xl, yn, top] + rg1[0]
    send(R, 15, tg.at[xl, yn, top], rg2.at[0, top], to_yn)
    arrive(R, 11, rg1.at[1])
    tg[xl, yp, bottom] = tg[xl, yp, bottom] + rg1[1]
    send(R, 16, tg.at[xl, yp, bottom], rg2.at[1, bottom], to_yp)
    mask = jnp.concatenate([turned(live_ref[pl.ds(ci, 1), :])] * (hid.shape[1] // 128), axis=1)
    arrive(R, 3, rgx.at[3])
    arrive(R, 12, rg2.at[0, bottom])
    arrive(R, 13, rg2.at[1, top])
    arrive(R, 15, rg2.at[0, top])
    arrive(R, 16, rg2.at[1, bottom])
    gate = tg[xl, y] + rgx[3] + rg2[0] + rg2[1]
    part = tu[xl, y] + ru2[0, xl] + ru2[1, xl]
    act = gate / (1.0 + jnp.exp(-gate)) * mask
    arrive(R, 14, rux)
    made = (act * (part + rux[...])).astype(BF16)
    hid[...] = made
    hcol_ref[ci] = made

    half = rows // 2
    at_root = jnp.logical_and(xh == 0, z == 0)
    holder = jnp.logical_and(at_root, core == 0)

    def by_half(c, k):
        return hp_ref.at[c, pl.ds(pl.multiple_of(k * half, half), half)]

    mine = by_half(ci, core)
    give = remote(hid.at[pl.ds(half, half)], hp_ref.at[ci, pl.ds(half, half)], (p1s, p1r), 0, to_core)
    hops = [
        pltpu.make_async_remote_copy(mine, mine, p1s.at[1 + i], p1r.at[0], device_id=where, device_id_type=MESH)
        for i, where in enumerate((to_x, to_zn, to_zp, to_zf))
    ]

    @pl.when(holder)
    def _():
        hp_ref[ci, pl.ds(0, half)] = made[:half]
        give.start()

    wide = made.astype(F32)
    squares = jnp.zeros((8, 128), F32)
    for i in range(0, rows, 8):
        for j in range(0, hid.shape[1], 128):
            piece = wide[i:i + 8, j:j + 128]
            squares = squares + piece * piece
    tr[ri] = squares
    for s in row_steps:
        send((ts, tq), s[0] * 8 + s[1] * 2 + s[2], tr.at[ri], tr.at[ri], row_peer[s])

    @pl.when(jnp.logical_not(holder))
    def _():
        arrive((p1s, p1r), 0, mine)

    @pl.when(at_root)
    def _():
        hops[0].start()

    @pl.when(z == 0)
    def _():
        for hop in hops[1:]:
            hop.start()

    two, three = (p2s, p2r), (p3s, p3r)
    along = ((1, to_yn), (3, to_yp), (2, {"col_1": yf}))
    across = remote(hid, hl_ref.at[core, ci], (qs, qr), 0, mirror)
    stay = pltpu.make_async_copy(hid, hl_ref.at[core, ci], own_sem.at[0])
    four, five, six = (hs, hr_sem), (qs, qr), (ls, lr)
    cp = ol * 4 + y
    pass_on(two, 4, mine, to_l)
    for d, where in along:
        pass_on(two, d, mine, where)
    pass_on(three, 0, mine, to_core)
    arrive(two, 4, by_half(cp, core))
    for d, where in along:
        pass_on(two, 4 + d, by_half(cp, core), where)
    pass_on(three, 4, by_half(cp, core), to_core)
    send(four, 4, hid, hcol_ref.at[ci], to_l)

    @pl.when(away)
    def _():
        across.start()

    @pl.when(jnp.logical_not(away))
    def _():
        stay.start()

    for s in row_steps:
        arrive((ts, tq), s[0] * 8 + s[1] * 2 + s[2], tr.at[row_from[s]])
    tc[ci] = jnp.sum(tr[...], axis=0)
    for s in col_steps:
        send((us, ur), s[0] * 4 + s[1], tc.at[ci], tc.at[ci], col_peer[s])
    for d, where in along:
        send(four, d, hid, hcol_ref.at[ci], where)
    order = [(0, 1), (0, 3), (0, 2), (1, 1), (1, 3), (1, 2)]
    for s in order:
        slot = s[0] * 4 + s[1]
        arrive(two, slot, by_half(col_from[s], core))
        pass_on(three, slot, by_half(col_from[s], core), to_core)

    def spread_block(h, zz, k):
        return hl_ref.at[k, h * 4 + zz]

    here = spread_block(xh, z, core)
    arrive(three, 0, by_half(ci, oc))
    arrive(three, 4, by_half(cp, oc))
    for s in order:
        arrive(three, s[0] * 4 + s[1], by_half(col_from[s], oc))
    panel = corner.shape[0]
    hp = hp_ref[...].reshape(total_rows, panel)
    on_line = lax.broadcasted_iota(jnp.int32, (panel, panel), 0) == lax.broadcasted_iota(jnp.int32, (panel, panel), 1)
    gram = cross(hp, hp) / total_rows
    for s in col_steps:
        arrive((us, ur), s[0] * 4 + s[1], tc.at[col_from[s]])
    total = jnp.sum(jnp.sum(tc[...], axis=0), axis=(0, 1), keepdims=True)
    ridge = damping * total / (total_rows * full)
    ridge_ref[...] = jnp.broadcast_to(ridge, (8, 128))
    scale = 1.0 / ridge
    corner[...] = (gram + jnp.where(on_line, ridge, 0.0)) * scale

    def between(k):
        if k == 0:
            arrive(four, 4, hcol_ref.at[cp])
            for d, where in along:
                pass_on(four, 4 + d, hcol_ref.at[cp], where)

            @pl.when(away)
            def _():
                across.wait_recv()

            @pl.when(jnp.logical_not(away))
            def _():
                stay.wait()

            for slot, where in ((1, to_x), (2, to_zn), (3, to_zp), (4, to_zf)):
                pass_on(five, slot, here, where)
            pass_on(six, 0, here, to_core)
        elif k == 3:
            arrive(five, 1, spread_block(oh, z, core))
            for slot, where in ((5, to_zn), (6, to_zp), (7, to_zf)):
                pass_on(five, slot, spread_block(oh, z, core), where)
            pass_on(six, 1, spread_block(oh, z, core), to_core)
        elif k == 4:
            for slot, zz in ((2, zp), (3, zn), (4, zf)):
                arrive(five, slot, spread_block(xh, zz, core))
                pass_on(six, slot, spread_block(xh, zz, core), to_core)
        elif k == 6:
            for slot, zz in ((5, zp), (6, zn), (7, zf)):
                arrive(five, slot, spread_block(oh, zz, core))
                pass_on(six, slot, spread_block(oh, zz, core), to_core)

    factor_inverse(corner, x_ref, between)
    x_ref[...] = x_ref[...] * jnp.sqrt(scale)
    for slot, (h, zz) in enumerate(((xh, z), (oh, z), (xh, zp), (xh, zn), (xh, zf), (oh, zp), (oh, zn), (oh, zf))):
        arrive(six, slot, spread_block(h, zz, oc))
    for s in order:
        arrive(four, s[0] * 4 + s[1], hcol_ref.at[col_from[s]])
    for copy in started:
        copy.wait_send()

    @pl.when(away)
    def _():
        across.wait_send()

    @pl.when(holder)
    def _():
        give.wait_send()

    @pl.when(at_root)
    def _():
        hops[0].wait_send()

    @pl.when(z == 0)
    def _():
        for hop in hops[1:]:
            hop.wait_send()


def main_of(tokens, gate_weight, up_weight, route, live, full):
    m, width = tokens.shape
    own = gate_weight.shape[1]
    rows_all = route.shape[0]
    rows = rows_all // 8
    hr = rows // 2
    vm = pltpu.VMEM
    dma = pltpu.SemaphoreType.DMA
    hbm = pl.BlockSpec(memory_space=pltpu.HBM)
    whole = pl.BlockSpec(memory_space=pltpu.VMEM)
    return pl.pallas_call(
        functools.partial(main_kernel, rows_all, full),
        name="hidden_factor",
        out_shape=(
            jax.ShapeDtypeStruct((8, rows, own), BF16),
            jax.ShapeDtypeStruct((8, rows, own), BF16),
            jax.ShapeDtypeStruct((2, 8, rows, own), BF16),
            jax.ShapeDtypeStruct((PANEL, PANEL), F32),
            jax.ShapeDtypeStruct((8, 128), F32),
        ),
        in_specs=[hbm, hbm, hbm, whole, whole],
        out_specs=(whole,) * 5,
        scratch_shapes=[
            vm((2, 4, 2, m, width), BF16),
            vm(gate_weight.shape, BF16),
            vm(up_weight.shape, BF16),
            vm((rows_all, 128), jnp.int32),
            vm((2, 4, rows, own), F32),
            vm((2, 4, rows, own), F32),
            vm((4, rows, own), F32),
            vm((2, hr, own), F32),
            vm((2, rows, own), F32),
            vm((2, rows, own), F32),
            vm((2, 2, rows, own), F32),
            vm((rows, own), F32),
            vm((rows, own), F32),
            vm((rows, own), BF16),
            vm((PANEL, PANEL), F32),
            vm((16, 8, 128), F32),
            vm((8, 8, 128), F32),
            dma((3,)),
            dma((21,)), dma((21,)),
            dma((17,)), dma((17,)),
            dma((5,)), dma((1,)),
            dma((8,)), dma((8,)),
            dma((8,)), dma((8,)),
            dma((16,)), dma((16,)),
            dma((8,)), dma((8,)),
            dma((8,)), dma((8,)),
            dma((8,)), dma((8,)),
            dma((8,)), dma((8,)),
        ],
        compiler_params=pltpu.CompilerParams(collective_id=0, has_side_effects=True, vmem_limit_bytes=36 * 2**20),
    )(tokens, gate_weight, up_weight, route.reshape(8, rows), live.reshape(8, rows))


def pair(a):
    high = a.astype(BF16)
    return high, (a - high.astype(F32)).astype(BF16)


def dot3_t(a, b):
    def one(u, v):
        return lax.dot_general(u, v, (((1,), (1,)), ((), ())), preferred_element_type=F32)

    return one(a[0], b[0]) + (one(a[0], b[1]) + one(a[1], b[0]))


def outputs_kernel(hp_ref, hcol_ref, hl_ref, x_ref, ridge_ref, panel_ref, trailing_ref, panel, trailing, sems):
    xh, z, core = (lax.axis_index(a) for a in ROW)
    xl, y = (lax.axis_index(a) for a in COL)
    ci, ri = xl * 4 + y, (xh * 4 + z) * 2 + core
    rows_all = hp_ref.shape[0] * hp_ref.shape[1]
    n = x_ref.shape[0]
    ridge = ridge_ref[0:1, 0:1]
    on_line = lax.broadcasted_iota(jnp.int32, (n, n), 0) == lax.broadcasted_iota(jnp.int32, (n, n), 1)
    hp = hp_ref[...].reshape(rows_all, n)
    hcol = hcol_ref[...].reshape(rows_all, n)
    x = pair(x_ref[...])

    def with_ridge(gram, here):
        return gram / rows_all + jnp.where(jnp.logical_and(on_line, here), ridge, 0.0)

    right = pair(dot3_t(pair(with_ridge(cross(hcol, hp), ri == 0)), x))
    copies = []
    for j in range(2):
        here = pl.ds(j * n, n)
        left = hl_ref[j].reshape(rows_all, n)
        down = dot3_t(pair(with_ridge(cross(left, hp), ci * 2 + j == 0)), x)
        panel[here, :] = down
        copies.append(pltpu.make_async_copy(panel.at[here], panel_ref.at[here], sems.at[j]))
        copies[-1].start()
        trailing[here, :] = with_ridge(cross(left, hcol), ci * 2 + j == ri) - dot3_t(pair(down), right)
        copies.append(pltpu.make_async_copy(trailing.at[here], trailing_ref.at[here], sems.at[2 + j]))
        copies[-1].start()
    for copy in copies:
        copy.wait()


def outputs_of(hp, hcol, hl, x, ridge):
    n = x.shape[0]
    hbm = pl.BlockSpec(memory_space=pl.ANY)
    whole = pl.BlockSpec(memory_space=pltpu.VMEM)
    return pl.pallas_call(
        outputs_kernel,
        name="outputs",
        out_shape=(jax.ShapeDtypeStruct((2 * n, n), F32), jax.ShapeDtypeStruct((2 * n, n), F32)),
        in_specs=[whole] * 5,
        out_specs=(hbm, hbm),
        scratch_shapes=[pltpu.VMEM((2 * n, n), F32), pltpu.VMEM((2 * n, n), F32), pltpu.SemaphoreType.DMA((4,))],
        compiler_params=pltpu.CompilerParams(vmem_limit_bytes=28 * 2**20),
    )(hp, hcol, hl, x, ridge)


def per_device(tokens, gate_weight, up_weight, route, live):
    full = gate_weight.shape[1] * lax.axis_size(ROW)
    return outputs_of(*main_of(tokens, gate_weight, up_weight, route, live, full))


def solution(mesh):
    finer = Mesh(mesh.devices.reshape(2, 4, 2, 2, 4), ("row_0", "row_1", "row_2", "col_0", "col_1"))
    placed = (P(ROW, COL), P(COL, ROW), P(COL, ROW), P(), P())
    return jax.shard_map(
        per_device,
        mesh=finer,
        in_specs=placed,
        out_specs=(P(COL, None), P(COL, ROW)),
        check_vma=False,
    )
```

```python
import functools

import jax
import jax.numpy as jnp
from jax import lax
from jax.experimental import pallas as pl
from jax.experimental.pallas import tpu as pltpu
from jax.sharding import Mesh
from jax.sharding import PartitionSpec as P

PANEL = 512
COL = ("col_0", "col_1")
ROW = ("row_0", "row_1", "row_2")
ROW_COL = ("row_0", "row_1", "row_2", "col_0", "col_1")
MESH = pl.DeviceIdType.MESH
F32 = jnp.float32
BF16 = jnp.bfloat16

damping = 0.1


def remote(src, dst, sems, slot, where):
    send, recv = sems
    return pltpu.make_async_remote_copy(
        src_ref=src, dst_ref=dst, send_sem=send.at[slot], recv_sem=recv.at[slot],
        device_id=where, device_id_type=MESH,
    )


NB = 128
HIGH = lax.Precision.HIGHEST


def spread(x):
    return jnp.broadcast_to(x, (8, NB))


def tile_inverse(rows, halfway):
    count = len(rows)
    lane = lax.broadcasted_iota(jnp.int32, (8, NB), 1)
    sub = lax.broadcasted_iota(jnp.int32, (8, NB), 0)
    rows = list(rows)
    out = []
    for g in range(count):
        column = [[spread(rows[i][:, 8 * g + c:8 * g + c + 1]) for c in range(8)] for i in range(g, count)]
        e = [[spread(column[0][b][a:a + 1, :]) for b in range(a + 1)] for a in range(8)]
        inside = (lane >= 8 * g) & (lane < 8 * g + 8)
        rows[g] = jnp.where(inside, (lane == sub + 8 * g).astype(F32), rows[g])
        for i in range(g + 1, count):
            rows[i] = jnp.where(inside, 0.0, rows[i])
        pivots = e[0][0]
        for c in range(8):
            if c:
                pivots = jnp.where(sub == c, e[c][c], pivots)
            if c % 2 == 0:
                inverse = 1.0 / e[c][c]
                later = e[c][c] / (e[c][c] * e[c + 1][c + 1] - e[c + 1][c] * e[c + 1][c])
            else:
                inverse = later
            for a in range(c + 1, 8):
                factor = e[a][c] * inverse
                for b in range(c + 1, a + 1):
                    e[a][b] = e[a][b] - factor * e[b][c]
            pivot_row = spread(rows[g][c:c + 1, :])
            for i in range(g, count):
                factor = column[i - g][c] * inverse
                if i == g:
                    factor = jnp.where(sub > c, factor, 0.0)
                for b in range(c + 1, 8):
                    column[i - g][b] = column[i - g][b] - factor * e[b][c]
                rows[i] = rows[i] - factor * pivot_row
        out.append(jnp.where(lane <= sub + 8 * g, rows[g] * lax.rsqrt(pivots), 0.0))
        if g == count // 2 - 1:
            halfway()
    return out


def dot_t(a, b):
    return lax.dot_general(a, b, (((1,), (1,)), ((), ())), precision=HIGH, preferred_element_type=F32)


def dot(a, b):
    return jnp.dot(a, b, precision=HIGH, preferred_element_type=F32)


def factor_inverse(a_ref, x_ref, between):
    n = a_ref.shape[0]
    x_ref[...] = jnp.zeros_like(x_ref)
    for k in range(n // NB):
        lo, hi = k * NB, (k + 1) * NB
        part = tile_inverse(
            [a_ref[lo + 8 * i:lo + 8 * i + 8, lo:hi] for i in range(NB // 8)], lambda: between(2 * k)
        )
        for i, rows in enumerate(part):
            x_ref[lo + 8 * i:lo + 8 * i + 8, lo:hi] = rows
        x = x_ref[lo:hi, lo:hi]
        if hi < n:
            low = dot_t(a_ref[hi:, lo:hi], x)
            a_ref[hi:, lo:hi] = low
            a_ref[hi:, hi:] = a_ref[hi:, hi:] - dot_t(low, low)
        between(2 * k + 1)
        if k:
            x_ref[lo:hi, :lo] = -dot(x, dot(a_ref[lo:hi, :lo], x_ref[:lo, :lo]))


def cross(a, b):
    return lax.dot_general(a, b, (((0,), (0,)), ((), ())), preferred_element_type=F32)


def turned(row):
    return jnp.broadcast_to(row, (128, 128)).astype(F32).T


def main_kernel(
    total_rows, full, tok_ref, gate_ref, up_ref, route_in, live_in,
    hp_ref, hcol_ref, hl_ref, x_ref, ridge_ref,
    tk, gw, uw, route_ref, live_ref, spots, tg, tu, rgx, rg1, rg2, ru1, ru2, rux, uout, hid, corner, tr, tc, own_sem,
    a_send, a_recv, r_send, r_recv, p1s, p1r, p2s, p2r, p3s, p3r, ts, tq, us, ur, hs, hr_sem, qs, qr, ls, lr,
):
    xh, z, core = (lax.axis_index(a) for a in ROW)
    xl, y = (lax.axis_index(a) for a in COL)
    oh, oc, ol = 1 - xh, 1 - core, 1 - xl
    zn, zp, zf = (z + 1) % 4, (z + 3) % 4, (z + 2) % 4
    yn, yp, yf = (y + 1) % 4, (y + 3) % 4, (y + 2) % 4
    ci, ki = xl * 4 + y, xh * 4 + z
    ri = ki * 2 + core
    to_x, to_core = {"row_0": oh}, {"row_2": oc}
    to_zn, to_zp, to_zf = {"row_1": zn}, {"row_1": zp}, {"row_1": zf}
    to_l, to_yn, to_yp = {"col_0": ol}, {"col_1": yn}, {"col_1": yp}
    mirror = {"row_0": xl, "row_1": y, "col_0": xh, "col_1": z}
    away = jnp.logical_or(xh != xl, z != y)
    m = tok_ref.shape[0]
    cut = m * 5 // 8
    col_steps = [(a, b) for a in range(2) for b in range(4) if a + b]
    row_steps = [(a, b, c) for a in range(2) for b in range(4) for c in range(2) if a + b + c]
    col_peer = {s: {"col_0": (xl + s[0]) % 2, "col_1": (y + s[1]) % 4} for s in col_steps}
    col_from = {s: (xl + s[0]) % 2 * 4 + (y + 4 - s[1]) % 4 for s in col_steps}
    row_peer = {s: {"row_0": (xh + s[0]) % 2, "row_1": (z + s[1]) % 4, "row_2": (core + s[2]) % 2} for s in row_steps}
    row_from = {s: ((xh + s[0]) % 2 * 4 + (z + 4 - s[1]) % 4) * 2 + (core + s[2]) % 2 for s in row_steps}

    own = pltpu.make_async_copy(tok_ref, tk.at[xh, z, core], own_sem.at[0])
    own.start()
    lists = [
        pltpu.make_async_copy(src, dst, own_sem.at[3 + i])
        for i, (src, dst) in enumerate(((route_in, route_ref), (live_in, live_ref)))
    ]
    for copy in lists:
        copy.start()
    gcopy = pltpu.make_async_copy(gate_ref, gw, own_sem.at[1])
    gcopy.start()
    ucopy = pltpu.make_async_copy(up_ref, uw, own_sem.at[2])
    ucopy.start()
    barrier = pltpu.get_barrier_semaphore()
    for peer in list(col_peer.values()) + list(row_peer.values()):
        pl.semaphore_signal(barrier, inc=1, device_id=peer, device_id_type=MESH)

    @pl.when(away)
    def _():
        pl.semaphore_signal(barrier, inc=1, device_id=mirror, device_id_type=MESH)

    rows = total_rows // 8
    for copy in lists:
        copy.wait()
    for t in range(8):
        spots[pl.ds(t * rows, rows), :] = turned(route_ref[t:t + 1, :]).astype(jnp.int32)
    own.wait()
    peers = len(col_steps) + len(row_steps)

    @pl.when(away)
    def _():
        pl.semaphore_wait(barrier, peers + 1)

    @pl.when(jnp.logical_not(away))
    def _():
        pl.semaphore_wait(barrier, peers)

    started = []

    def send(sems, slot, src, dst, where):
        copy = remote(src, dst, sems, slot, where)
        copy.start()
        started.append(copy)

    def arrive(sems, slot, ref):
        remote(ref, ref, sems, slot, to_core).wait_recv()

    def pass_on(sems, slot, ref, where):
        send(sems, slot, ref, ref, where)

    A = (a_send, a_recv)

    def block(h, zz, k, lo=0, n=m):
        return tk.at[h, zz, k, pl.ds(lo, n)]

    pass_on(A, 0, block(xh, z, core), to_x)
    pass_on(A, 1, block(xh, z, core), to_zn)
    pass_on(A, 2, block(xh, z, core), to_zp)
    pass_on(A, 3, block(xh, z, core), to_zf)
    pass_on(A, 10, block(xh, z, core), to_core)
    arrive(A, 1, block(xh, zp, core))
    pass_on(A, 7, block(xh, zp, core, cut, m - cut), to_x)
    pass_on(A, 11, block(xh, zp, core), to_core)
    arrive(A, 2, block(xh, zn, core))
    pass_on(A, 8, block(xh, zn, core, cut, m - cut), to_x)
    pass_on(A, 12, block(xh, zn, core), to_core)
    arrive(A, 0, block(oh, z, core))
    pass_on(A, 4, block(oh, z, core, 0, cut), to_zn)
    pass_on(A, 5, block(oh, z, core, 0, cut), to_zp)
    pass_on(A, 6, block(oh, z, core, 0, cut), to_zf)
    pass_on(A, 14, block(oh, z, core), to_core)
    arrive(A, 3, block(xh, zf, core))
    pass_on(A, 9, block(xh, zf, core, cut, m - cut), to_x)
    pass_on(A, 13, block(xh, zf, core), to_core)
    for slot, zz in ((0, zp), (1, zn), (2, zf)):
        arrive(A, 4 + slot, block(oh, zz, core, 0, cut))
        pass_on(A, 15 + slot, block(oh, zz, core, 0, cut), to_core)
        arrive(A, 7 + slot, block(oh, zz, core, cut, m - cut))
        pass_on(A, 18 + slot, block(oh, zz, core, cut, m - cut), to_core)
    for slot, (h, zz) in enumerate(((xh, z), (xh, zp), (xh, zn), (xh, zf), (oh, z))):
        arrive(A, 10 + slot, block(h, zz, oc))
    for slot, zz in ((0, zp), (1, zn), (2, zf)):
        arrive(A, 15 + slot, block(oh, zz, oc, 0, cut))
        arrive(A, 18 + slot, block(oh, zz, oc, cut, m - cut))
    gcopy.wait()
    ucopy.wait()

    R = (r_send, r_recv)
    hr = rows // 2
    pool = 16 * m
    width = tk.shape[-1]

    def tile(b):
        spot = jnp.concatenate(
            [spots[pl.ds(pl.multiple_of((e * 4 + b) * rows, rows), rows), :] for e in range(2)], axis=0
        )
        spot = jnp.concatenate([spot] * (pool // 128), axis=1)
        hot = (spot == lax.broadcasted_iota(jnp.int32, (2 * rows, pool), 1)).astype(F32).astype(BF16)
        chosen = jnp.dot(hot, tk[...].reshape(pool, width), preferred_element_type=F32).astype(BF16)
        g = jnp.dot(chosen, gw[...], preferred_element_type=F32)
        u = jnp.dot(chosen, uw[...], preferred_element_type=F32)
        for e in range(2):
            tg[e, b] = g[e * rows:(e + 1) * rows]
            tu[e, b] = u[e * rows:(e + 1) * rows]

    top, bottom = pl.ds(0, hr), pl.ds(hr, hr)
    tile(yf)
    send(R, 0, tg.at[ol, yf], rgx.at[0], to_l)
    send(R, 4, tu.at[0, yf], ru1.at[0], to_yn)
    send(R, 5, tu.at[1, yf], ru1.at[1], to_yp)
    tile(yn)
    send(R, 1, tg.at[ol, yn], rgx.at[1], to_l)
    send(R, 6, tu.at[1, yn], ru2.at[0, 1], to_yn)
    tile(yp)
    send(R, 2, tg.at[ol, yp], rgx.at[2], to_l)
    send(R, 7, tu.at[0, yp], ru2.at[1, 0], to_yp)
    tile(y)
    send(R, 3, tg.at[ol, y], rgx.at[3], to_l)
    arrive(R, 4, ru1.at[0])
    tu[0, yn] = tu[0, yn] + ru1[0]
    send(R, 8, tu.at[0, yn], ru2.at[0, 0], to_yn)
    arrive(R, 5, ru1.at[1])
    tu[1, yp] = tu[1, yp] + ru1[1]
    send(R, 9, tu.at[1, yp], ru2.at[1, 1], to_yp)
    arrive(R, 0, rgx.at[0])
    tg[xl, yf] = tg[xl, yf] + rgx[0]
    send(R, 10, tg.at[xl, yf, top], rg1.at[0], to_yn)
    send(R, 11, tg.at[xl, yf, bottom], rg1.at[1], to_yp)
    arrive(R, 1, rgx.at[1])
    tg[xl, yn] = tg[xl, yn] + rgx[1]
    send(R, 12, tg.at[xl, yn, bottom], rg2.at[0, bottom], to_yn)
    arrive(R, 2, rgx.at[2])
    tg[xl, yp] = tg[xl, yp] + rgx[2]
    send(R, 13, tg.at[xl, yp, top], rg2.at[1, top], to_yp)
    arrive(R, 6, ru2.at[0, 1])
    arrive(R, 8, ru2.at[0, 0])
    arrive(R, 7, ru2.at[1, 0])
    arrive(R, 9, ru2.at[1, 1])
    uout[...] = tu[ol, y] + ru2[0, ol] + ru2[1, ol]
    send(R, 14, uout, rux, to_l)
    arrive(R, 10, rg1.at[0])
    tg[xl, yn, top] = tg[xl, yn, top] + rg1[0]
    send(R, 15, tg.at[xl, yn, top], rg2.at[0, top], to_yn)
    arrive(R, 11, rg1.at[1])
    tg[xl, yp, bottom] = tg[xl, yp, bottom] + rg1[1]
    send(R, 16, tg.at[xl, yp, bottom], rg2.at[1, bottom], to_yp)
    mask = jnp.concatenate([turned(live_ref[pl.ds(ci, 1), :])] * (hid.shape[1] // 128), axis=1)
    arrive(R, 3, rgx.at[3])
    arrive(R, 12, rg2.at[0, bottom])
    arrive(R, 13, rg2.at[1, top])
    arrive(R, 15, rg2.at[0, top])
    arrive(R, 16, rg2.at[1, bottom])
    gate = tg[xl, y] + rgx[3] + rg2[0] + rg2[1]
    part = tu[xl, y] + ru2[0, xl] + ru2[1, xl]
    act = gate / (1.0 + jnp.exp(-gate)) * mask
    arrive(R, 14, rux)
    made = (act * (part + rux[...])).astype(BF16)
    hid[...] = made
    hcol_ref[ci] = made

    half = rows // 2
    at_root = jnp.logical_and(xh == 0, z == 0)
    holder = jnp.logical_and(at_root, core == 0)

    def by_half(c, k):
        return hp_ref.at[c, pl.ds(pl.multiple_of(k * half, half), half)]

    mine = by_half(ci, core)
    give = remote(hid.at[pl.ds(half, half)], hp_ref.at[ci, pl.ds(half, half)], (p1s, p1r), 0, to_core)
    hops = [
        pltpu.make_async_remote_copy(mine, mine, p1s.at[1 + i], p1r.at[0], device_id=where, device_id_type=MESH)
        for i, where in enumerate((to_x, to_zn, to_zp, to_zf))
    ]

    @pl.when(holder)
    def _():
        hp_ref[ci, pl.ds(0, half)] = made[:half]
        give.start()
        for hop in hops:
            hop.start()

    along = ((1, to_yn), (3, to_yp), (2, {"col_1": yf}))
    across = remote(hid, hl_ref.at[core, ci], (qs, qr), 0, mirror)
    stay = pltpu.make_async_copy(hid, hl_ref.at[core, ci], own_sem.at[0])
    four, five, six = (hs, hr_sem), (qs, qr), (ls, lr)
    cp = ol * 4 + y

    @pl.when(away)
    def _():
        across.start()

    @pl.when(jnp.logical_not(away))
    def _():
        stay.start()

    wide = made.astype(F32)
    squares = jnp.zeros((8, 128), F32)
    for i in range(0, rows, 8):
        for j in range(0, hid.shape[1], 128):
            piece = wide[i:i + 8, j:j + 128]
            squares = squares + piece * piece
    tr[ri] = squares
    for s in row_steps:
        send((ts, tq), s[0] * 8 + s[1] * 2 + s[2], tr.at[ri], tr.at[ri], row_peer[s])

    @pl.when(jnp.logical_not(holder))
    def _():
        arrive((p1s, p1r), 0, mine)

    @pl.when(jnp.logical_and(at_root, core == 1))
    def _():
        hops[0].start()

    @pl.when(jnp.logical_and(z == 0, jnp.logical_not(holder)))
    def _():
        for hop in hops[1:]:
            hop.start()

    two, three = (p2s, p2r), (p3s, p3r)
    pass_on(two, 4, mine, to_l)
    for d, where in along:
        pass_on(two, d, mine, where)
    pass_on(three, 0, mine, to_core)

    def spread_block(h, zz, k):
        return hl_ref.at[k, h * 4 + zz]

    here = spread_block(xh, z, core)

    @pl.when(away)
    def _():
        across.wait_recv()

    @pl.when(jnp.logical_not(away))
    def _():
        stay.wait()

    for slot, where in ((1, to_x), (2, to_zn), (3, to_zp), (4, to_zf)):
        pass_on(five, slot, here, where)
    arrive(two, 4, by_half(cp, core))
    for d, where in along:
        pass_on(two, 4 + d, by_half(cp, core), where)
    pass_on(three, 4, by_half(cp, core), to_core)
    send(four, 4, hid, hcol_ref.at[ci], to_l)
    for s in row_steps:
        arrive((ts, tq), s[0] * 8 + s[1] * 2 + s[2], tr.at[row_from[s]])
    tc[ci] = jnp.sum(tr[...], axis=0)
    for s in col_steps:
        send((us, ur), s[0] * 4 + s[1], tc.at[ci], tc.at[ci], col_peer[s])
    for d, where in along:
        send(four, d, hid, hcol_ref.at[ci], where)
    order = [(0, 1), (0, 3), (0, 2), (1, 1), (1, 3), (1, 2)]
    for s in order:
        slot = s[0] * 4 + s[1]
        arrive(two, slot, by_half(col_from[s], core))
        pass_on(three, slot, by_half(col_from[s], core), to_core)
    arrive(five, 1, spread_block(oh, z, core))
    for slot, where in ((5, to_zn), (6, to_zp), (7, to_zf)):
        pass_on(five, slot, spread_block(oh, z, core), where)
    pass_on(six, 0, here, to_core)
    pass_on(six, 1, spread_block(oh, z, core), to_core)
    arrive(three, 0, by_half(ci, oc))
    arrive(three, 4, by_half(cp, oc))
    for s in order:
        arrive(three, s[0] * 4 + s[1], by_half(col_from[s], oc))
    panel = corner.shape[0]
    hp = hp_ref[...].reshape(total_rows, panel)
    on_line = lax.broadcasted_iota(jnp.int32, (panel, panel), 0) == lax.broadcasted_iota(jnp.int32, (panel, panel), 1)
    gram = cross(hp, hp) / total_rows
    for s in col_steps:
        arrive((us, ur), s[0] * 4 + s[1], tc.at[col_from[s]])
    total = jnp.sum(jnp.sum(tc[...], axis=0), axis=(0, 1), keepdims=True)
    ridge = damping * total / (total_rows * full)
    ridge_ref[...] = jnp.broadcast_to(ridge, (8, 128))
    scale = 1.0 / ridge
    corner[...] = (gram + jnp.where(on_line, ridge, 0.0)) * scale

    def between(k):
        if k == 0:
            arrive(four, 4, hcol_ref.at[cp])
            for d, where in along:
                pass_on(four, 4 + d, hcol_ref.at[cp], where)

        elif k == 2:
            for slot, zz in ((2, zp), (3, zn), (4, zf)):
                arrive(five, slot, spread_block(xh, zz, core))
                pass_on(six, slot, spread_block(xh, zz, core), to_core)
        elif k == 5:
            for slot, zz in ((5, zp), (6, zn), (7, zf)):
                arrive(five, slot, spread_block(oh, zz, core))
                pass_on(six, slot, spread_block(oh, zz, core), to_core)

    factor_inverse(corner, x_ref, between)
    x_ref[...] = x_ref[...] * jnp.sqrt(scale)
    for slot, (h, zz) in enumerate(((xh, z), (oh, z), (xh, zp), (xh, zn), (xh, zf), (oh, zp), (oh, zn), (oh, zf))):
        arrive(six, slot, spread_block(h, zz, oc))
    for s in order:
        arrive(four, s[0] * 4 + s[1], hcol_ref.at[col_from[s]])
    for copy in started:
        copy.wait_send()

    @pl.when(away)
    def _():
        across.wait_send()

    @pl.when(holder)
    def _():
        give.wait_send()

    @pl.when(at_root)
    def _():
        hops[0].wait_send()

    @pl.when(z == 0)
    def _():
        for hop in hops[1:]:
            hop.wait_send()


def main_of(tokens, gate_weight, up_weight, route, live, full):
    m, width = tokens.shape
    own = gate_weight.shape[1]
    rows_all = route.shape[0]
    rows = rows_all // 8
    hr = rows // 2
    vm = pltpu.VMEM
    dma = pltpu.SemaphoreType.DMA
    hbm = pl.BlockSpec(memory_space=pltpu.HBM)
    whole = pl.BlockSpec(memory_space=pltpu.VMEM)
    operands = (tokens, gate_weight, up_weight, route.reshape(8, rows), live.reshape(8, rows))
    return pl.pallas_call(
        functools.partial(main_kernel, rows_all, full),
        name="hidden_factor",
        out_shape=(
            jax.ShapeDtypeStruct((8, rows, own), BF16),
            jax.ShapeDtypeStruct((8, rows, own), BF16),
            jax.ShapeDtypeStruct((2, 8, rows, own), BF16),
            jax.ShapeDtypeStruct((PANEL, PANEL), F32),
            jax.ShapeDtypeStruct((8, 128), F32),
        ),
        in_specs=[hbm] * 5,
        out_specs=(whole,) * 5,
        scratch_shapes=[
            vm((2, 4, 2, m, width), BF16),
            vm(gate_weight.shape, BF16),
            vm(up_weight.shape, BF16),
            vm((8, rows), jnp.int32),
            vm((8, rows), jnp.int32),
            vm((rows_all, 128), jnp.int32),
            vm((2, 4, rows, own), F32),
            vm((2, 4, rows, own), F32),
            vm((4, rows, own), F32),
            vm((2, hr, own), F32),
            vm((2, rows, own), F32),
            vm((2, rows, own), F32),
            vm((2, 2, rows, own), F32),
            vm((rows, own), F32),
            vm((rows, own), F32),
            vm((rows, own), BF16),
            vm((PANEL, PANEL), F32),
            vm((16, 8, 128), F32),
            vm((8, 8, 128), F32),
            dma((5,)),
            dma((21,)), dma((21,)),
            dma((17,)), dma((17,)),
            dma((5,)), dma((1,)),
            dma((8,)), dma((8,)),
            dma((8,)), dma((8,)),
            dma((16,)), dma((16,)),
            dma((8,)), dma((8,)),
            dma((8,)), dma((8,)),
            dma((8,)), dma((8,)),
            dma((8,)), dma((8,)),
        ],
        compiler_params=pltpu.CompilerParams(collective_id=0, has_side_effects=True, vmem_limit_bytes=46000 * 2**10),
    )(*(pltpu.with_memory_space_constraint(a, pltpu.HBM) for a in operands))


def pair(a):
    high = a.astype(BF16)
    return high, (a - high.astype(F32)).astype(BF16)


def dot3_t(a, b):
    def one(u, v):
        return lax.dot_general(u, v, (((1,), (1,)), ((), ())), preferred_element_type=F32)

    return one(a[0], b[0]) + (one(a[0], b[1]) + one(a[1], b[0]))


def outputs_kernel(hp_ref, hcol_ref, hl_ref, x_ref, ridge_ref, panel_ref, trailing_ref, panel, trailing, sems):
    xh, z, core = (lax.axis_index(a) for a in ROW)
    xl, y = (lax.axis_index(a) for a in COL)
    ci, ri = xl * 4 + y, (xh * 4 + z) * 2 + core
    rows_all = hp_ref.shape[0] * hp_ref.shape[1]
    n = x_ref.shape[0]
    ridge = ridge_ref[0:1, 0:1]
    on_line = lax.broadcasted_iota(jnp.int32, (n, n), 0) == lax.broadcasted_iota(jnp.int32, (n, n), 1)
    hp = hp_ref[...].reshape(rows_all, n)
    hcol = hcol_ref[...].reshape(rows_all, n)
    x = pair(x_ref[...])

    def with_ridge(gram, here):
        return gram / rows_all + jnp.where(jnp.logical_and(on_line, here), ridge, 0.0)

    right = pair(dot3_t(pair(with_ridge(cross(hcol, hp), ri == 0)), x))
    copies = []
    for j in range(2):
        here = pl.ds(j * n, n)
        left = hl_ref[j].reshape(rows_all, n)
        down = dot3_t(pair(with_ridge(cross(left, hp), ci * 2 + j == 0)), x)
        panel[here, :] = down
        copies.append(pltpu.make_async_copy(panel.at[here], panel_ref.at[here], sems.at[j]))
        copies[-1].start()
        trailing[here, :] = with_ridge(cross(left, hcol), ci * 2 + j == ri) - dot3_t(pair(down), right)
        copies.append(pltpu.make_async_copy(trailing.at[here], trailing_ref.at[here], sems.at[2 + j]))
        copies[-1].start()
    for copy in copies:
        copy.wait()


def outputs_of(hp, hcol, hl, x, ridge):
    n = x.shape[0]
    hbm = pl.BlockSpec(memory_space=pl.ANY)
    whole = pl.BlockSpec(memory_space=pltpu.VMEM)
    return pl.pallas_call(
        outputs_kernel,
        name="outputs",
        out_shape=(jax.ShapeDtypeStruct((2 * n, n), F32), jax.ShapeDtypeStruct((2 * n, n), F32)),
        in_specs=[whole] * 5,
        out_specs=(hbm, hbm),
        scratch_shapes=[pltpu.VMEM((2 * n, n), F32), pltpu.VMEM((2 * n, n), F32), pltpu.SemaphoreType.DMA((4,))],
        compiler_params=pltpu.CompilerParams(vmem_limit_bytes=28 * 2**20),
    )(hp, hcol, hl, x, ridge)


def per_device(tokens, gate_weight, up_weight, route, live):
    full = gate_weight.shape[1] * lax.axis_size(ROW)
    return outputs_of(*main_of(tokens, gate_weight, up_weight, route, live, full))


def solution(mesh):
    finer = Mesh(mesh.devices.reshape(2, 4, 2, 2, 4), ("row_0", "row_1", "row_2", "col_0", "col_1"))
    placed = (P(ROW, COL), P(COL, ROW), P(COL, ROW), P(), P())
    return jax.shard_map(
        per_device,
        mesh=finer,
        in_specs=placed,
        out_specs=(P(COL, None), P(COL, ROW)),
        check_vma=False,
    )
```

```python
import functools

import jax
import jax.numpy as jnp
from jax import lax
from jax.experimental import pallas as pl
from jax.experimental.pallas import tpu as pltpu
from jax.sharding import Mesh
from jax.sharding import PartitionSpec as P

PANEL = 512
COL = ("col_0", "col_1")
ROW = ("row_0", "row_1", "row_2")
ROW_COL = ("row_0", "row_1", "row_2", "col_0", "col_1")
MESH = pl.DeviceIdType.MESH
F32 = jnp.float32
BF16 = jnp.bfloat16

damping = 0.1


def remote(src, dst, sems, slot, where):
    send, recv = sems
    return pltpu.make_async_remote_copy(
        src_ref=src, dst_ref=dst, send_sem=send.at[slot], recv_sem=recv.at[slot],
        device_id=where, device_id_type=MESH,
    )


NB = 128
HIGH = lax.Precision.HIGHEST


def spread(x):
    return jnp.broadcast_to(x, (8, NB))


def tile_inverse(rows, halfway):
    count = len(rows)
    lane = lax.broadcasted_iota(jnp.int32, (8, NB), 1)
    sub = lax.broadcasted_iota(jnp.int32, (8, NB), 0)
    rows = list(rows)
    out = []
    for g in range(count):
        top = [spread(rows[g][:, 8 * g + c:8 * g + c + 1]) for c in range(8)]
        e = [[spread(top[b][a:a + 1, :]) for b in range(a + 1)] for a in range(8)]
        inside = (lane >= 8 * g) & (lane < 8 * g + 8)
        group = jnp.where(inside, (lane == sub + 8 * g).astype(F32), rows[g])
        own = [spread(group[c:c + 1, :]) for c in range(8)]
        inverse = [None] * 8
        m = [[None] * 8 for _ in range(8)]
        for c in range(8):
            if c % 2 == 0:
                inverse[c] = 1.0 / e[c][c]
                inverse[c + 1] = e[c][c] / (e[c][c] * e[c + 1][c + 1] - e[c + 1][c] * e[c + 1][c])
            for a in range(c + 1, 8):
                m[a][c] = e[a][c] * inverse[c]
                for b in range(c + 1, a + 1):
                    e[a][b] = e[a][b] - m[a][c] * e[b][c]
                own[a] = own[a] - m[a][c] * own[c]
        back = [own[c] * inverse[c] for c in range(8)]
        for b in range(7, 0, -1):
            for c in range(b):
                back[c] = back[c] - m[b][c] * back[b]
        for i in range(g + 1, count):
            terms = [spread(rows[i][:, 8 * g + c:8 * g + c + 1]) * back[c] for c in range(8)]
            while len(terms) > 1:
                terms = [terms[k] + terms[k + 1] for k in range(0, len(terms), 2)]
            rows[i] = jnp.where(inside, 0.0, rows[i]) - terms[0]
        pivots, done = e[0][0], own[0]
        for c in range(1, 8):
            pivots = jnp.where(sub == c, e[c][c], pivots)
            done = jnp.where(sub == c, own[c], done)
        out.append(jnp.where(lane <= sub + 8 * g, done * lax.rsqrt(pivots), 0.0))
        if g == count // 2 - 1:
            halfway()
    return out


def dot_t(a, b):
    return lax.dot_general(a, b, (((1,), (1,)), ((), ())), precision=HIGH, preferred_element_type=F32)


def dot(a, b):
    return jnp.dot(a, b, precision=HIGH, preferred_element_type=F32)


def factor_inverse(a_ref, x_ref, between):
    n = a_ref.shape[0]
    x_ref[...] = jnp.zeros_like(x_ref)
    for k in range(n // NB):
        lo, hi = k * NB, (k + 1) * NB
        part = tile_inverse(
            [a_ref[lo + 8 * i:lo + 8 * i + 8, lo:hi] for i in range(NB // 8)], lambda: between(2 * k)
        )
        for i, rows in enumerate(part):
            x_ref[lo + 8 * i:lo + 8 * i + 8, lo:hi] = rows
        x = x_ref[lo:hi, lo:hi]
        if hi < n:
            low = dot_t(a_ref[hi:, lo:hi], x)
            a_ref[hi:, lo:hi] = low
            a_ref[hi:, hi:] = a_ref[hi:, hi:] - dot_t(low, low)
        between(2 * k + 1)
        if k:
            x_ref[lo:hi, :lo] = -dot(x, dot(a_ref[lo:hi, :lo], x_ref[:lo, :lo]))


def cross(a, b):
    return lax.dot_general(a, b, (((0,), (0,)), ((), ())), preferred_element_type=F32)


def turned(row):
    return jnp.broadcast_to(row, (128, 128)).astype(F32).T


def main_kernel(
    total_rows, full, tok_ref, gate_ref, up_ref, route_in, live_in,
    hp_ref, hcol_ref, hl_ref, x_ref, ridge_ref,
    tk, gw, uw, route_ref, live_ref, spots, tg, tu, rgx, rg1, rg2, ru1, ru2, rux, uout, hid, corner, tr, tz, ty, own_sem,
    a_send, a_recv, r_send, r_recv, p1s, p1r, p2s, p2r, p3s, p3r, ts, tq, hs, hr_sem, qs, qr, ls, lr,
):
    xh, z, core = (lax.axis_index(a) for a in ROW)
    xl, y = (lax.axis_index(a) for a in COL)
    oh, oc, ol = 1 - xh, 1 - core, 1 - xl
    zn, zp, zf = (z + 1) % 4, (z + 3) % 4, (z + 2) % 4
    yn, yp, yf = (y + 1) % 4, (y + 3) % 4, (y + 2) % 4
    ci, ki = xl * 4 + y, xh * 4 + z
    ri = ki * 2 + core
    to_x, to_core = {"row_0": oh}, {"row_2": oc}
    to_zn, to_zp, to_zf = {"row_1": zn}, {"row_1": zp}, {"row_1": zf}
    to_l, to_yn, to_yp = {"col_0": ol}, {"col_1": yn}, {"col_1": yp}
    mirror = {"row_0": xl, "row_1": y, "col_0": xh, "col_1": z}
    away = jnp.logical_or(xh != xl, z != y)
    m = tok_ref.shape[0]
    cut = m * 5 // 8
    to_yf = {"col_1": yf}
    peers = [to_x, to_core, to_zn, to_zp, to_zf, to_l, to_yn, to_yp, to_yf]
    col_from = {(a, b): (xl + a) % 2 * 4 + (y + 4 - b) % 4 for a in range(2) for b in range(4)}

    own = pltpu.make_async_copy(tok_ref, tk.at[xh, z, core], own_sem.at[0])
    own.start()
    lists = [
        pltpu.make_async_copy(src, dst, own_sem.at[3 + i])
        for i, (src, dst) in enumerate(((route_in, route_ref), (live_in, live_ref)))
    ]
    for copy in lists:
        copy.start()
    gcopy = pltpu.make_async_copy(gate_ref, gw, own_sem.at[1])
    gcopy.start()
    ucopy = pltpu.make_async_copy(up_ref, uw, own_sem.at[2])
    ucopy.start()
    barrier = pltpu.get_barrier_semaphore()
    for peer in peers:
        pl.semaphore_signal(barrier, inc=1, device_id=peer, device_id_type=MESH)

    @pl.when(away)
    def _():
        pl.semaphore_signal(barrier, inc=1, device_id=mirror, device_id_type=MESH)

    rows = total_rows // 8
    for copy in lists:
        copy.wait()
    for t in range(8):
        spots[pl.ds(t * rows, rows), :] = turned(route_ref[t:t + 1, :]).astype(jnp.int32)
    own.wait()

    @pl.when(away)
    def _():
        pl.semaphore_wait(barrier, len(peers) + 1)

    @pl.when(jnp.logical_not(away))
    def _():
        pl.semaphore_wait(barrier, len(peers))

    started = []

    def send(sems, slot, src, dst, where):
        copy = remote(src, dst, sems, slot, where)
        copy.start()
        started.append(copy)

    def arrive(sems, slot, ref):
        remote(ref, ref, sems, slot, to_core).wait_recv()

    def pass_on(sems, slot, ref, where):
        send(sems, slot, ref, ref, where)

    A = (a_send, a_recv)

    def block(h, zz, k, lo=0, n=m):
        return tk.at[h, zz, k, pl.ds(lo, n)]

    pass_on(A, 0, block(xh, z, core), to_x)
    pass_on(A, 1, block(xh, z, core), to_zn)
    pass_on(A, 2, block(xh, z, core), to_zp)
    pass_on(A, 3, block(xh, z, core), to_zf)
    pass_on(A, 10, block(xh, z, core), to_core)
    arrive(A, 1, block(xh, zp, core))
    pass_on(A, 7, block(xh, zp, core, cut, m - cut), to_x)
    pass_on(A, 11, block(xh, zp, core), to_core)
    arrive(A, 2, block(xh, zn, core))
    pass_on(A, 8, block(xh, zn, core, cut, m - cut), to_x)
    pass_on(A, 12, block(xh, zn, core), to_core)
    arrive(A, 0, block(oh, z, core))
    pass_on(A, 4, block(oh, z, core, 0, cut), to_zn)
    pass_on(A, 5, block(oh, z, core, 0, cut), to_zp)
    pass_on(A, 6, block(oh, z, core, 0, cut), to_zf)
    pass_on(A, 14, block(oh, z, core), to_core)
    arrive(A, 3, block(xh, zf, core))
    pass_on(A, 9, block(xh, zf, core, cut, m - cut), to_x)
    pass_on(A, 13, block(xh, zf, core), to_core)
    for slot, zz in ((0, zp), (1, zn), (2, zf)):
        arrive(A, 4 + slot, block(oh, zz, core, 0, cut))
        pass_on(A, 15 + slot, block(oh, zz, core, 0, cut), to_core)
        arrive(A, 7 + slot, block(oh, zz, core, cut, m - cut))
        pass_on(A, 18 + slot, block(oh, zz, core, cut, m - cut), to_core)
    for slot, (h, zz) in enumerate(((xh, z), (xh, zp), (xh, zn), (xh, zf), (oh, z))):
        arrive(A, 10 + slot, block(h, zz, oc))
    for slot, zz in ((0, zp), (1, zn), (2, zf)):
        arrive(A, 15 + slot, block(oh, zz, oc, 0, cut))
        arrive(A, 18 + slot, block(oh, zz, oc, cut, m - cut))
    gcopy.wait()
    ucopy.wait()

    R = (r_send, r_recv)
    hr = rows // 2
    pool = 16 * m
    width = tk.shape[-1]

    def tile(b):
        spot = jnp.concatenate(
            [spots[pl.ds(pl.multiple_of((e * 4 + b) * rows, rows), rows), :] for e in range(2)], axis=0
        )
        spot = jnp.concatenate([spot] * (pool // 128), axis=1)
        hot = (spot == lax.broadcasted_iota(jnp.int32, (2 * rows, pool), 1)).astype(F32).astype(BF16)
        chosen = jnp.dot(hot, tk[...].reshape(pool, width), preferred_element_type=F32).astype(BF16)
        g = jnp.dot(chosen, gw[...], preferred_element_type=F32)
        u = jnp.dot(chosen, uw[...], preferred_element_type=F32)
        for e in range(2):
            tg[e, b] = g[e * rows:(e + 1) * rows]
            tu[e, b] = u[e * rows:(e + 1) * rows]

    top, bottom = pl.ds(0, hr), pl.ds(hr, hr)
    tile(yf)
    send(R, 0, tg.at[ol, yf], rgx.at[0], to_l)
    send(R, 4, tu.at[0, yf], ru1.at[0], to_yn)
    send(R, 5, tu.at[1, yf], ru1.at[1], to_yp)
    tile(yn)
    send(R, 1, tg.at[ol, yn], rgx.at[1], to_l)
    send(R, 6, tu.at[1, yn], ru2.at[0, 1], to_yn)
    tile(yp)
    send(R, 2, tg.at[ol, yp], rgx.at[2], to_l)
    send(R, 7, tu.at[0, yp], ru2.at[1, 0], to_yp)
    tile(y)
    send(R, 3, tg.at[ol, y], rgx.at[3], to_l)
    arrive(R, 4, ru1.at[0])
    tu[0, yn] = tu[0, yn] + ru1[0]
    send(R, 8, tu.at[0, yn], ru2.at[0, 0], to_yn)
    arrive(R, 5, ru1.at[1])
    tu[1, yp] = tu[1, yp] + ru1[1]
    send(R, 9, tu.at[1, yp], ru2.at[1, 1], to_yp)
    arrive(R, 0, rgx.at[0])
    tg[xl, yf] = tg[xl, yf] + rgx[0]
    send(R, 10, tg.at[xl, yf, top], rg1.at[0], to_yn)
    send(R, 11, tg.at[xl, yf, bottom], rg1.at[1], to_yp)
    arrive(R, 1, rgx.at[1])
    tg[xl, yn] = tg[xl, yn] + rgx[1]
    send(R, 12, tg.at[xl, yn, bottom], rg2.at[0, bottom], to_yn)
    arrive(R, 2, rgx.at[2])
    tg[xl, yp] = tg[xl, yp] + rgx[2]
    send(R, 13, tg.at[xl, yp, top], rg2.at[1, top], to_yp)
    arrive(R, 6, ru2.at[0, 1])
    arrive(R, 8, ru2.at[0, 0])
    arrive(R, 7, ru2.at[1, 0])
    arrive(R, 9, ru2.at[1, 1])
    uout[...] = tu[ol, y] + ru2[0, ol] + ru2[1, ol]
    send(R, 14, uout, rux, to_l)
    arrive(R, 10, rg1.at[0])
    tg[xl, yn, top] = tg[xl, yn, top] + rg1[0]
    send(R, 15, tg.at[xl, yn, top], rg2.at[0, top], to_yn)
    arrive(R, 11, rg1.at[1])
    tg[xl, yp, bottom] = tg[xl, yp, bottom] + rg1[1]
    send(R, 16, tg.at[xl, yp, bottom], rg2.at[1, bottom], to_yp)
    mask = jnp.concatenate([turned(live_ref[pl.ds(ci, 1), :])] * (hid.shape[1] // 128), axis=1)
    arrive(R, 3, rgx.at[3])
    arrive(R, 12, rg2.at[0, bottom])
    arrive(R, 13, rg2.at[1, top])
    arrive(R, 15, rg2.at[0, top])
    arrive(R, 16, rg2.at[1, bottom])
    gate = tg[xl, y] + rgx[3] + rg2[0] + rg2[1]
    part = tu[xl, y] + ru2[0, xl] + ru2[1, xl]
    act = gate / (1.0 + jnp.exp(-gate)) * mask
    arrive(R, 14, rux)
    made = (act * (part + rux[...])).astype(BF16)
    hid[...] = made
    hcol_ref[ci] = made

    half = rows // 2
    at_root = jnp.logical_and(xh == 0, z == 0)
    holder = jnp.logical_and(at_root, core == 0)

    def by_half(c, k):
        return hp_ref.at[c, pl.ds(pl.multiple_of(k * half, half), half)]

    mine = by_half(ci, core)
    give = remote(hid.at[pl.ds(half, half)], hp_ref.at[ci, pl.ds(half, half)], (p1s, p1r), 0, to_core)
    hops = [
        pltpu.make_async_remote_copy(mine, mine, p1s.at[1 + i], p1r.at[0], device_id=where, device_id_type=MESH)
        for i, where in enumerate((to_x, to_zn, to_zp, to_zf))
    ]

    @pl.when(holder)
    def _():
        hp_ref[ci, pl.ds(0, half)] = made[:half]
        give.start()
        for hop in hops:
            hop.start()

    along = ((1, to_yn), (3, to_yp), (2, to_yf))
    across = remote(hid, hl_ref.at[core, ci], (qs, qr), 0, mirror)
    stay = pltpu.make_async_copy(hid, hl_ref.at[core, ci], own_sem.at[0])
    four, five, six = (hs, hr_sem), (qs, qr), (ls, lr)
    cp = ol * 4 + y

    @pl.when(away)
    def _():
        across.start()

    @pl.when(jnp.logical_not(away))
    def _():
        stay.start()

    wide = made.astype(F32)
    squares = jnp.zeros((8, 128), F32)
    for i in range(0, rows, 8):
        for j in range(0, hid.shape[1], 128):
            piece = wide[i:i + 8, j:j + 128]
            squares = squares + piece * piece
    seven = (ts, tq)
    tr[0] = squares
    send(seven, 0, tr.at[0], tr.at[1], to_core)

    @pl.when(jnp.logical_not(holder))
    def _():
        arrive((p1s, p1r), 0, mine)

    arrive(seven, 0, tr.at[1])
    tr[2] = tr[0] + tr[1]
    send(seven, 1, tr.at[2], tr.at[3], to_x)

    @pl.when(jnp.logical_and(at_root, core == 1))
    def _():
        hops[0].start()

    @pl.when(jnp.logical_and(z == 0, jnp.logical_not(holder)))
    def _():
        for hop in hops[1:]:
            hop.start()

    two, three = (p2s, p2r), (p3s, p3r)
    pass_on(two, 4, mine, to_l)
    for d, where in along:
        pass_on(two, d, mine, where)
    pass_on(three, 0, mine, to_core)

    def spread_block(h, zz, k):
        return hl_ref.at[k, h * 4 + zz]

    here = spread_block(xh, z, core)

    @pl.when(away)
    def _():
        across.wait_recv()

    @pl.when(jnp.logical_not(away))
    def _():
        stay.wait()

    for slot, where in ((1, to_x), (2, to_zn), (3, to_zp), (4, to_zf)):
        pass_on(five, slot, here, where)
    arrive(seven, 1, tr.at[3])
    tz[z] = tr[2] + tr[3]
    for d, where in ((1, to_zn), (3, to_zp), (2, to_zf)):
        pass_on(seven, 1 + d, tz.at[z], where)
    arrive(two, 4, by_half(cp, core))
    for d, where in along:
        pass_on(two, 4 + d, by_half(cp, core), where)
    pass_on(three, 4, by_half(cp, core), to_core)
    send(four, 4, hid, hcol_ref.at[ci], to_l)
    for d, zz in ((1, zp), (3, zn), (2, zf)):
        arrive(seven, 1 + d, tz.at[zz])
    tr[4] = jnp.sum(tz[...], axis=0)
    send(seven, 5, tr.at[4], tr.at[5], to_l)
    for d, where in along:
        send(four, d, hid, hcol_ref.at[ci], where)
    order = [(0, 1), (0, 3), (0, 2), (1, 1), (1, 3), (1, 2)]
    for s in order:
        slot = s[0] * 4 + s[1]
        arrive(two, slot, by_half(col_from[s], core))
        pass_on(three, slot, by_half(col_from[s], core), to_core)
        if s == (0, 2):
            arrive(seven, 5, tr.at[5])
            ty[y] = tr[4] + tr[5]
            for d, where in along:
                pass_on(seven, 5 + d, ty.at[y], where)
    arrive(five, 1, spread_block(oh, z, core))
    for slot, where in ((5, to_zn), (6, to_zp), (7, to_zf)):
        pass_on(five, slot, spread_block(oh, z, core), where)
    pass_on(six, 0, here, to_core)
    pass_on(six, 1, spread_block(oh, z, core), to_core)
    arrive(three, 0, by_half(ci, oc))
    arrive(three, 4, by_half(cp, oc))
    for s in order:
        arrive(three, s[0] * 4 + s[1], by_half(col_from[s], oc))
    panel = corner.shape[0]
    hp = hp_ref[...].reshape(total_rows, panel)
    on_line = lax.broadcasted_iota(jnp.int32, (panel, panel), 0) == lax.broadcasted_iota(jnp.int32, (panel, panel), 1)
    gram = cross(hp, hp) / total_rows
    for d, yy in ((1, yp), (3, yn), (2, yf)):
        arrive(seven, 5 + d, ty.at[yy])
    total = jnp.sum(jnp.sum(ty[...], axis=0), axis=(0, 1), keepdims=True)
    ridge = damping * total / (total_rows * full)
    ridge_ref[...] = jnp.broadcast_to(ridge, (8, 128))
    scale = 1.0 / ridge
    corner[...] = (gram + jnp.where(on_line, ridge, 0.0)) * scale

    def between(k):
        if k == 0:
            arrive(four, 4, hcol_ref.at[cp])
            for d, where in along:
                pass_on(four, 4 + d, hcol_ref.at[cp], where)

        elif k == 2:
            for slot, zz in ((2, zp), (3, zn), (4, zf)):
                arrive(five, slot, spread_block(xh, zz, core))
                pass_on(six, slot, spread_block(xh, zz, core), to_core)
        elif k == 5:
            for slot, zz in ((5, zp), (6, zn), (7, zf)):
                arrive(five, slot, spread_block(oh, zz, core))
                pass_on(six, slot, spread_block(oh, zz, core), to_core)

    factor_inverse(corner, x_ref, between)
    x_ref[...] = x_ref[...] * jnp.sqrt(scale)
    for slot, (h, zz) in enumerate(((xh, z), (oh, z), (xh, zp), (xh, zn), (xh, zf), (oh, zp), (oh, zn), (oh, zf))):
        arrive(six, slot, spread_block(h, zz, oc))
    for s in order:
        arrive(four, s[0] * 4 + s[1], hcol_ref.at[col_from[s]])
    for copy in started:
        copy.wait_send()

    @pl.when(away)
    def _():
        across.wait_send()

    @pl.when(holder)
    def _():
        give.wait_send()

    @pl.when(at_root)
    def _():
        hops[0].wait_send()

    @pl.when(z == 0)
    def _():
        for hop in hops[1:]:
            hop.wait_send()


def main_of(tokens, gate_weight, up_weight, route, live, full):
    m, width = tokens.shape
    own = gate_weight.shape[1]
    rows_all = route.shape[0]
    rows = rows_all // 8
    hr = rows // 2
    vm = pltpu.VMEM
    dma = pltpu.SemaphoreType.DMA
    hbm = pl.BlockSpec(memory_space=pltpu.HBM)
    whole = pl.BlockSpec(memory_space=pltpu.VMEM)
    operands = (tokens, gate_weight, up_weight, route.reshape(8, rows), live.reshape(8, rows))
    return pl.pallas_call(
        functools.partial(main_kernel, rows_all, full),
        name="hidden_factor",
        out_shape=(
            jax.ShapeDtypeStruct((8, rows, own), BF16),
            jax.ShapeDtypeStruct((8, rows, own), BF16),
            jax.ShapeDtypeStruct((2, 8, rows, own), BF16),
            jax.ShapeDtypeStruct((PANEL, PANEL), F32),
            jax.ShapeDtypeStruct((8, 128), F32),
        ),
        in_specs=[hbm] * 5,
        out_specs=(whole,) * 5,
        scratch_shapes=[
            vm((2, 4, 2, m, width), BF16),
            vm(gate_weight.shape, BF16),
            vm(up_weight.shape, BF16),
            vm((8, rows), jnp.int32),
            vm((8, rows), jnp.int32),
            vm((rows_all, 128), jnp.int32),
            vm((2, 4, rows, own), F32),
            vm((2, 4, rows, own), F32),
            vm((4, rows, own), F32),
            vm((2, hr, own), F32),
            vm((2, rows, own), F32),
            vm((2, rows, own), F32),
            vm((2, 2, rows, own), F32),
            vm((rows, own), F32),
            vm((rows, own), F32),
            vm((rows, own), BF16),
            vm((PANEL, PANEL), F32),
            vm((6, 8, 128), F32),
            vm((4, 8, 128), F32),
            vm((4, 8, 128), F32),
            dma((5,)),
            dma((21,)), dma((21,)),
            dma((17,)), dma((17,)),
            dma((5,)), dma((1,)),
            dma((8,)), dma((8,)),
            dma((8,)), dma((8,)),
            dma((9,)), dma((9,)),
            dma((8,)), dma((8,)),
            dma((8,)), dma((8,)),
            dma((8,)), dma((8,)),
        ],
        compiler_params=pltpu.CompilerParams(collective_id=0, has_side_effects=True, vmem_limit_bytes=46000 * 2**10),
    )(*(pltpu.with_memory_space_constraint(a, pltpu.HBM) for a in operands))


def pair(a):
    high = a.astype(BF16)
    return high, (a - high.astype(F32)).astype(BF16)


def dot3_t(a, b):
    def one(u, v):
        return lax.dot_general(u, v, (((1,), (1,)), ((), ())), preferred_element_type=F32)

    return one(a[0], b[0]) + (one(a[0], b[1]) + one(a[1], b[0]))


def outputs_kernel(hp_ref, hcol_ref, hl_ref, x_ref, ridge_ref, panel_ref, trailing_ref, panel, trailing, sems):
    xh, z, core = (lax.axis_index(a) for a in ROW)
    xl, y = (lax.axis_index(a) for a in COL)
    ci, ri = xl * 4 + y, (xh * 4 + z) * 2 + core
    rows_all = hp_ref.shape[0] * hp_ref.shape[1]
    n = x_ref.shape[0]
    ridge = ridge_ref[0:1, 0:1]
    on_line = lax.broadcasted_iota(jnp.int32, (n, n), 0) == lax.broadcasted_iota(jnp.int32, (n, n), 1)
    hp = hp_ref[...].reshape(rows_all, n)
    hcol = hcol_ref[...].reshape(rows_all, n)
    x = pair(x_ref[...])

    def with_ridge(gram, here):
        return gram / rows_all + jnp.where(jnp.logical_and(on_line, here), ridge, 0.0)

    right = pair(dot3_t(pair(with_ridge(cross(hcol, hp), ri == 0)), x))
    copies = []
    for j in range(2):
        here = pl.ds(j * n, n)
        left = hl_ref[j].reshape(rows_all, n)
        down = dot3_t(pair(with_ridge(cross(left, hp), ci * 2 + j == 0)), x)
        panel[here, :] = down
        copies.append(pltpu.make_async_copy(panel.at[here], panel_ref.at[here], sems.at[j]))
        copies[-1].start()
        trailing[here, :] = with_ridge(cross(left, hcol), ci * 2 + j == ri) - dot3_t(pair(down), right)
        copies.append(pltpu.make_async_copy(trailing.at[here], trailing_ref.at[here], sems.at[2 + j]))
        copies[-1].start()
    for copy in copies:
        copy.wait()


def outputs_of(hp, hcol, hl, x, ridge):
    n = x.shape[0]
    hbm = pl.BlockSpec(memory_space=pl.ANY)
    whole = pl.BlockSpec(memory_space=pltpu.VMEM)
    return pl.pallas_call(
        outputs_kernel,
        name="outputs",
        out_shape=(jax.ShapeDtypeStruct((2 * n, n), F32), jax.ShapeDtypeStruct((2 * n, n), F32)),
        in_specs=[whole] * 5,
        out_specs=(hbm, hbm),
        scratch_shapes=[pltpu.VMEM((2 * n, n), F32), pltpu.VMEM((2 * n, n), F32), pltpu.SemaphoreType.DMA((4,))],
        compiler_params=pltpu.CompilerParams(vmem_limit_bytes=28 * 2**20),
    )(hp, hcol, hl, x, ridge)


def per_device(tokens, gate_weight, up_weight, route, live):
    full = gate_weight.shape[1] * lax.axis_size(ROW)
    return outputs_of(*main_of(tokens, gate_weight, up_weight, route, live, full))


def solution(mesh):
    finer = Mesh(mesh.devices.reshape(2, 4, 2, 2, 4), ("row_0", "row_1", "row_2", "col_0", "col_1"))
    placed = (P(ROW, COL), P(COL, ROW), P(COL, ROW), P(), P())
    return jax.shard_map(
        per_device,
        mesh=finer,
        in_specs=placed,
        out_specs=(P(COL, None), P(COL, ROW)),
        check_vma=False,
    )
```

```python
import functools

import jax
import jax.numpy as jnp
from jax import lax
from jax.experimental import pallas as pl
from jax.experimental.pallas import tpu as pltpu
from jax.sharding import Mesh
from jax.sharding import PartitionSpec as P

PANEL = 512
COL = ("col_0", "col_1")
ROW = ("row_0", "row_1", "row_2")
ROW_COL = ("row_0", "row_1", "row_2", "col_0", "col_1")
MESH = pl.DeviceIdType.MESH
F32 = jnp.float32
BF16 = jnp.bfloat16

damping = 0.1


def remote(src, dst, sems, slot, where):
    send, recv = sems
    return pltpu.make_async_remote_copy(
        src_ref=src, dst_ref=dst, send_sem=send.at[slot], recv_sem=recv.at[slot],
        device_id=where, device_id_type=MESH,
    )


NB = 128
HIGH = lax.Precision.HIGHEST


def spread(x):
    return jnp.broadcast_to(x, (8, NB))


def tile_inverse(rows, halfway):
    count = len(rows)
    lane = lax.broadcasted_iota(jnp.int32, (8, NB), 1)
    sub = lax.broadcasted_iota(jnp.int32, (8, NB), 0)
    rows = list(rows)
    out = []
    for g in range(count):
        top = [spread(rows[g][:, 8 * g + c:8 * g + c + 1]) for c in range(8)]
        e = [[spread(top[b][a:a + 1, :]) for b in range(a + 1)] for a in range(8)]
        inside = (lane >= 8 * g) & (lane < 8 * g + 8)
        group = jnp.where(inside, (lane == sub + 8 * g).astype(F32), rows[g])
        own = [spread(group[c:c + 1, :]) for c in range(8)]
        inverse = [None] * 8
        m = [[None] * 8 for _ in range(8)]
        for c in range(8):
            if c % 2 == 0:
                inverse[c] = 1.0 / e[c][c]
                inverse[c + 1] = e[c][c] / (e[c][c] * e[c + 1][c + 1] - e[c + 1][c] * e[c + 1][c])
            for a in range(c + 1, 8):
                m[a][c] = e[a][c] * inverse[c]
                for b in range(c + 1, a + 1):
                    e[a][b] = e[a][b] - m[a][c] * e[b][c]
                own[a] = own[a] - m[a][c] * own[c]
        back = [own[c] * inverse[c] for c in range(8)]
        for b in range(7, 0, -1):
            for c in range(b):
                back[c] = back[c] - m[b][c] * back[b]
        for i in range(g + 1, count):
            terms = [spread(rows[i][:, 8 * g + c:8 * g + c + 1]) * back[c] for c in range(8)]
            while len(terms) > 1:
                terms = [terms[k] + terms[k + 1] for k in range(0, len(terms), 2)]
            rows[i] = jnp.where(inside, 0.0, rows[i]) - terms[0]
        pivots, done = e[0][0], own[0]
        for c in range(1, 8):
            pivots = jnp.where(sub == c, e[c][c], pivots)
            done = jnp.where(sub == c, own[c], done)
        out.append(jnp.where(lane <= sub + 8 * g, done * lax.rsqrt(pivots), 0.0))
        if g == count // 2 - 1:
            halfway()
    return out


def dot_t(a, b):
    return lax.dot_general(a, b, (((1,), (1,)), ((), ())), precision=HIGH, preferred_element_type=F32)


def dot(a, b):
    return jnp.dot(a, b, precision=HIGH, preferred_element_type=F32)


def factor_inverse(a_ref, x_ref, between):
    n = a_ref.shape[0]
    x_ref[...] = jnp.zeros_like(x_ref)
    for k in range(n // NB):
        lo, hi = k * NB, (k + 1) * NB
        part = tile_inverse(
            [a_ref[lo + 8 * i:lo + 8 * i + 8, lo:hi] for i in range(NB // 8)], lambda: between(2 * k)
        )
        for i, rows in enumerate(part):
            x_ref[lo + 8 * i:lo + 8 * i + 8, lo:hi] = rows
        x = x_ref[lo:hi, lo:hi]
        if hi < n:
            low = dot_t(a_ref[hi:, lo:hi], x)
            a_ref[hi:, lo:hi] = low
            a_ref[hi:, hi:] = a_ref[hi:, hi:] - dot_t(low, low)
        between(2 * k + 1)
        if k:
            x_ref[lo:hi, :lo] = -dot(x, dot(a_ref[lo:hi, :lo], x_ref[:lo, :lo]))


def cross(a, b):
    return lax.dot_general(a, b, (((0,), (0,)), ((), ())), preferred_element_type=F32)


def turned(row):
    return jnp.broadcast_to(row, (128, 128)).astype(F32).T


def main_kernel(
    total_rows, full, tok_ref, gate_ref, up_ref, route_in, live_in,
    hp_ref, hcol_ref, hl_ref, x_ref, ridge_ref,
    tk, gw, uw, route_ref, live_ref, spots, tg, tu, rgx, rg1, rg2, ru1, ru2, rux, uout, hid, corner, tr, tz, ty, own_sem,
    a_send, a_recv, r_send, r_recv, p1s, p1r, p2s, p2r, p3s, p3r, ts, tq, hs, hr_sem, qs, qr, ls, lr,
):
    xh, z, core = (lax.axis_index(a) for a in ROW)
    xl, y = (lax.axis_index(a) for a in COL)
    oh, oc, ol = 1 - xh, 1 - core, 1 - xl
    zn, zp, zf = (z + 1) % 4, (z + 3) % 4, (z + 2) % 4
    yn, yp, yf = (y + 1) % 4, (y + 3) % 4, (y + 2) % 4
    ci, ki = xl * 4 + y, xh * 4 + z
    ri = ki * 2 + core
    to_x, to_core = {"row_0": oh}, {"row_2": oc}
    to_zn, to_zp, to_zf = {"row_1": zn}, {"row_1": zp}, {"row_1": zf}
    to_l, to_yn, to_yp = {"col_0": ol}, {"col_1": yn}, {"col_1": yp}
    mirror = {"row_0": xl, "row_1": y, "col_0": xh, "col_1": z}
    away = jnp.logical_or(xh != xl, z != y)
    m = tok_ref.shape[0]
    cut = m * 5 // 8
    to_yf = {"col_1": yf}
    peers = [to_x, to_core, to_zn, to_zp, to_zf, to_l, to_yn, to_yp, to_yf]
    col_from = {(a, b): (xl + a) % 2 * 4 + (y + 4 - b) % 4 for a in range(2) for b in range(4)}

    own = pltpu.make_async_copy(tok_ref, tk.at[xh, z, core], own_sem.at[0])
    own.start()
    lists = [
        pltpu.make_async_copy(src, dst, own_sem.at[3 + i])
        for i, (src, dst) in enumerate(((route_in, route_ref), (live_in, live_ref)))
    ]
    for copy in lists:
        copy.start()
    gcopy = pltpu.make_async_copy(gate_ref, gw, own_sem.at[1])
    gcopy.start()
    ucopy = pltpu.make_async_copy(up_ref, uw, own_sem.at[2])
    ucopy.start()
    barrier = pltpu.get_barrier_semaphore()
    for peer in peers:
        pl.semaphore_signal(barrier, inc=1, device_id=peer, device_id_type=MESH)

    @pl.when(away)
    def _():
        pl.semaphore_signal(barrier, inc=1, device_id=mirror, device_id_type=MESH)

    rows = total_rows // 8
    for copy in lists:
        copy.wait()
    for t in range(8):
        spots[pl.ds(t * rows, rows), :] = turned(route_ref[t:t + 1, :]).astype(jnp.int32)
    own.wait()

    @pl.when(away)
    def _():
        pl.semaphore_wait(barrier, len(peers) + 1)

    @pl.when(jnp.logical_not(away))
    def _():
        pl.semaphore_wait(barrier, len(peers))

    started = []

    def send(sems, slot, src, dst, where):
        copy = remote(src, dst, sems, slot, where)
        copy.start()
        started.append(copy)

    def arrive(sems, slot, ref):
        remote(ref, ref, sems, slot, to_core).wait_recv()

    def pass_on(sems, slot, ref, where):
        send(sems, slot, ref, ref, where)

    A = (a_send, a_recv)

    def block(h, zz, k, lo=0, n=m):
        return tk.at[h, zz, k, pl.ds(lo, n)]

    pass_on(A, 0, block(xh, z, core), to_x)
    pass_on(A, 1, block(xh, z, core), to_zn)
    pass_on(A, 2, block(xh, z, core), to_zp)
    pass_on(A, 3, block(xh, z, core), to_zf)
    pass_on(A, 10, block(xh, z, core), to_core)
    arrive(A, 1, block(xh, zp, core))
    pass_on(A, 7, block(xh, zp, core, cut, m - cut), to_x)
    pass_on(A, 11, block(xh, zp, core), to_core)
    arrive(A, 2, block(xh, zn, core))
    pass_on(A, 8, block(xh, zn, core, cut, m - cut), to_x)
    pass_on(A, 12, block(xh, zn, core), to_core)
    arrive(A, 0, block(oh, z, core))
    pass_on(A, 4, block(oh, z, core, 0, cut), to_zn)
    pass_on(A, 5, block(oh, z, core, 0, cut), to_zp)
    pass_on(A, 6, block(oh, z, core, 0, cut), to_zf)
    pass_on(A, 14, block(oh, z, core), to_core)
    arrive(A, 3, block(xh, zf, core))
    pass_on(A, 9, block(xh, zf, core, cut, m - cut), to_x)
    pass_on(A, 13, block(xh, zf, core), to_core)
    for slot, zz in ((0, zp), (1, zn), (2, zf)):
        arrive(A, 4 + slot, block(oh, zz, core, 0, cut))
        pass_on(A, 15 + slot, block(oh, zz, core, 0, cut), to_core)
        arrive(A, 7 + slot, block(oh, zz, core, cut, m - cut))
        pass_on(A, 18 + slot, block(oh, zz, core, cut, m - cut), to_core)
    for slot, (h, zz) in enumerate(((xh, z), (xh, zp), (xh, zn), (xh, zf), (oh, z))):
        arrive(A, 10 + slot, block(h, zz, oc))
    for slot, zz in ((0, zp), (1, zn), (2, zf)):
        arrive(A, 15 + slot, block(oh, zz, oc, 0, cut))
        arrive(A, 18 + slot, block(oh, zz, oc, cut, m - cut))
    gcopy.wait()
    ucopy.wait()

    R = (r_send, r_recv)
    hr = rows // 2
    pool = 16 * m
    width = tk.shape[-1]

    def tile(b):
        spot = jnp.concatenate(
            [spots[pl.ds(pl.multiple_of((e * 4 + b) * rows, rows), rows), :] for e in range(2)], axis=0
        )
        spot = jnp.concatenate([spot] * (pool // 128), axis=1)
        hot = (spot == lax.broadcasted_iota(jnp.int32, (2 * rows, pool), 1)).astype(F32).astype(BF16)
        chosen = jnp.dot(hot, tk[...].reshape(pool, width), preferred_element_type=F32).astype(BF16)
        g = jnp.dot(chosen, gw[...], preferred_element_type=F32)
        u = jnp.dot(chosen, uw[...], preferred_element_type=F32)
        for e in range(2):
            tg[e, b] = g[e * rows:(e + 1) * rows]
            tu[e, b] = u[e * rows:(e + 1) * rows]

    top, bottom = pl.ds(0, hr), pl.ds(hr, hr)
    tile(yf)
    send(R, 0, tg.at[ol, yf], rgx.at[0], to_l)
    send(R, 4, tu.at[0, yf], ru1.at[0], to_yn)
    send(R, 5, tu.at[1, yf], ru1.at[1], to_yp)
    tile(yn)
    send(R, 1, tg.at[ol, yn], rgx.at[1], to_l)
    send(R, 6, tu.at[1, yn], ru2.at[0, 1], to_yn)
    tile(yp)
    send(R, 2, tg.at[ol, yp], rgx.at[2], to_l)
    send(R, 7, tu.at[0, yp], ru2.at[1, 0], to_yp)
    tile(y)
    send(R, 3, tg.at[ol, y], rgx.at[3], to_l)
    arrive(R, 4, ru1.at[0])
    tu[0, yn] = tu[0, yn] + ru1[0]
    send(R, 8, tu.at[0, yn], ru2.at[0, 0], to_yn)
    arrive(R, 5, ru1.at[1])
    tu[1, yp] = tu[1, yp] + ru1[1]
    send(R, 9, tu.at[1, yp], ru2.at[1, 1], to_yp)
    arrive(R, 0, rgx.at[0])
    tg[xl, yf] = tg[xl, yf] + rgx[0]
    send(R, 10, tg.at[xl, yf, top], rg1.at[0], to_yn)
    send(R, 11, tg.at[xl, yf, bottom], rg1.at[1], to_yp)
    arrive(R, 1, rgx.at[1])
    tg[xl, yn] = tg[xl, yn] + rgx[1]
    send(R, 12, tg.at[xl, yn, bottom], rg2.at[0, bottom], to_yn)
    arrive(R, 2, rgx.at[2])
    tg[xl, yp] = tg[xl, yp] + rgx[2]
    send(R, 13, tg.at[xl, yp, top], rg2.at[1, top], to_yp)
    arrive(R, 6, ru2.at[0, 1])
    arrive(R, 8, ru2.at[0, 0])
    arrive(R, 7, ru2.at[1, 0])
    arrive(R, 9, ru2.at[1, 1])
    uout[...] = tu[ol, y] + ru2[0, ol] + ru2[1, ol]
    send(R, 14, uout, rux, to_l)
    arrive(R, 10, rg1.at[0])
    tg[xl, yn, top] = tg[xl, yn, top] + rg1[0]
    send(R, 15, tg.at[xl, yn, top], rg2.at[0, top], to_yn)
    arrive(R, 11, rg1.at[1])
    tg[xl, yp, bottom] = tg[xl, yp, bottom] + rg1[1]
    send(R, 16, tg.at[xl, yp, bottom], rg2.at[1, bottom], to_yp)
    mask = jnp.concatenate([turned(live_ref[pl.ds(ci, 1), :])] * (hid.shape[1] // 128), axis=1)
    arrive(R, 3, rgx.at[3])
    arrive(R, 12, rg2.at[0, bottom])
    arrive(R, 13, rg2.at[1, top])
    arrive(R, 15, rg2.at[0, top])
    arrive(R, 16, rg2.at[1, bottom])
    gate = tg[xl, y] + rgx[3] + rg2[0] + rg2[1]
    part = tu[xl, y] + ru2[0, xl] + ru2[1, xl]
    act = gate / (1.0 + jnp.exp(-gate)) * mask
    arrive(R, 14, rux)
    made = (act * (part + rux[...])).astype(BF16)
    hid[...] = made
    hcol_ref[ci] = made

    half = rows // 2
    at_root = jnp.logical_and(xh == 0, z == 0)
    holder = jnp.logical_and(at_root, core == 0)

    def by_half(c, k):
        return hp_ref.at[c, pl.ds(pl.multiple_of(k * half, half), half)]

    mine = by_half(ci, core)
    give = remote(hid.at[pl.ds(half, half)], hp_ref.at[ci, pl.ds(half, half)], (p1s, p1r), 0, to_core)
    hops = [
        pltpu.make_async_remote_copy(mine, mine, p1s.at[1 + i], p1r.at[0], device_id=where, device_id_type=MESH)
        for i, where in enumerate((to_x, to_zn, to_zp, to_zf))
    ]

    @pl.when(holder)
    def _():
        hp_ref[ci, pl.ds(0, half)] = made[:half]
        give.start()
        for hop in hops:
            hop.start()

    along = ((1, to_yn), (3, to_yp), (2, to_yf))
    across = remote(hid, hl_ref.at[core, ci], (qs, qr), 0, mirror)
    stay = pltpu.make_async_copy(hid, hl_ref.at[core, ci], own_sem.at[0])
    four, five, six = (hs, hr_sem), (qs, qr), (ls, lr)
    cp = ol * 4 + y

    @pl.when(away)
    def _():
        across.start()

    @pl.when(jnp.logical_not(away))
    def _():
        stay.start()

    wide = made.astype(F32)
    squares = jnp.zeros((8, 128), F32)
    for i in range(0, rows, 8):
        for j in range(0, hid.shape[1], 128):
            piece = wide[i:i + 8, j:j + 128]
            squares = squares + piece * piece
    seven = (ts, tq)
    tr[0] = squares
    send(seven, 0, tr.at[0], tr.at[1], to_core)
    arrive(seven, 0, tr.at[1])
    tr[2] = tr[0] + tr[1]
    send(seven, 1, tr.at[2], tr.at[3], to_x)

    @pl.when(jnp.logical_not(holder))
    def _():
        arrive((p1s, p1r), 0, mine)

    @pl.when(jnp.logical_and(at_root, core == 1))
    def _():
        hops[0].start()

    @pl.when(jnp.logical_and(z == 0, jnp.logical_not(holder)))
    def _():
        for hop in hops[1:]:
            hop.start()

    two, three = (p2s, p2r), (p3s, p3r)
    pass_on(two, 4, mine, to_l)
    for d, where in along:
        pass_on(two, d, mine, where)
    pass_on(three, 0, mine, to_core)

    def spread_block(h, zz, k):
        return hl_ref.at[k, h * 4 + zz]

    arrive(seven, 1, tr.at[3])
    tz[z] = tr[2] + tr[3]
    for d, where in ((1, to_zn), (3, to_zp), (2, to_zf)):
        pass_on(seven, 1 + d, tz.at[z], where)
    here = spread_block(xh, z, core)

    @pl.when(away)
    def _():
        across.wait_recv()

    @pl.when(jnp.logical_not(away))
    def _():
        stay.wait()

    for slot, where in ((1, to_x), (2, to_zn), (3, to_zp), (4, to_zf)):
        pass_on(five, slot, here, where)
    arrive(two, 4, by_half(cp, core))
    for d, where in along:
        pass_on(two, 4 + d, by_half(cp, core), where)
    pass_on(three, 4, by_half(cp, core), to_core)
    for d, zz in ((1, zp), (3, zn), (2, zf)):
        arrive(seven, 1 + d, tz.at[zz])
    tr[4] = jnp.sum(tz[...], axis=0)
    send(seven, 5, tr.at[4], tr.at[5], to_l)
    send(four, 4, hid, hcol_ref.at[ci], to_l)
    order = [(0, 1), (0, 3), (0, 2), (1, 1), (1, 3), (1, 2)]
    for s in order:
        slot = s[0] * 4 + s[1]
        arrive(two, slot, by_half(col_from[s], core))
        pass_on(three, slot, by_half(col_from[s], core), to_core)
        if s == (0, 2):
            arrive(seven, 5, tr.at[5])
            ty[y] = tr[4] + tr[5]
            for d, where in along:
                pass_on(seven, 5 + d, ty.at[y], where)
            for d, where in along:
                send(four, d, hid, hcol_ref.at[ci], where)
    arrive(five, 1, spread_block(oh, z, core))
    for slot, where in ((5, to_zn), (6, to_zp), (7, to_zf)):
        pass_on(five, slot, spread_block(oh, z, core), where)
    pass_on(six, 0, here, to_core)
    pass_on(six, 1, spread_block(oh, z, core), to_core)
    arrive(three, 0, by_half(ci, oc))
    arrive(three, 4, by_half(cp, oc))
    for s in order:
        arrive(three, s[0] * 4 + s[1], by_half(col_from[s], oc))
    panel = corner.shape[0]
    hp = hp_ref[...].reshape(total_rows, panel)
    on_line = lax.broadcasted_iota(jnp.int32, (panel, panel), 0) == lax.broadcasted_iota(jnp.int32, (panel, panel), 1)
    gram = cross(hp, hp) / total_rows
    for d, yy in ((1, yp), (3, yn), (2, yf)):
        arrive(seven, 5 + d, ty.at[yy])
    total = jnp.sum(jnp.sum(ty[...], axis=0), axis=(0, 1), keepdims=True)
    ridge = damping * total / (total_rows * full)
    ridge_ref[...] = jnp.broadcast_to(ridge, (8, 128))
    scale = 1.0 / ridge
    corner[...] = (gram + jnp.where(on_line, ridge, 0.0)) * scale

    def between(k):
        if k == 0:
            arrive(four, 4, hcol_ref.at[cp])
            for d, where in along:
                pass_on(four, 4 + d, hcol_ref.at[cp], where)

        elif k == 2:
            for slot, zz in ((2, zp), (3, zn), (4, zf)):
                arrive(five, slot, spread_block(xh, zz, core))
                pass_on(six, slot, spread_block(xh, zz, core), to_core)
        elif k == 5:
            for slot, zz in ((5, zp), (6, zn), (7, zf)):
                arrive(five, slot, spread_block(oh, zz, core))
                pass_on(six, slot, spread_block(oh, zz, core), to_core)

    factor_inverse(corner, x_ref, between)
    x_ref[...] = x_ref[...] * jnp.sqrt(scale)
    for slot, (h, zz) in enumerate(((xh, z), (oh, z), (xh, zp), (xh, zn), (xh, zf), (oh, zp), (oh, zn), (oh, zf))):
        arrive(six, slot, spread_block(h, zz, oc))
    for s in order:
        arrive(four, s[0] * 4 + s[1], hcol_ref.at[col_from[s]])
    for copy in started:
        copy.wait_send()

    @pl.when(away)
    def _():
        across.wait_send()

    @pl.when(holder)
    def _():
        give.wait_send()

    @pl.when(at_root)
    def _():
        hops[0].wait_send()

    @pl.when(z == 0)
    def _():
        for hop in hops[1:]:
            hop.wait_send()


def main_of(tokens, gate_weight, up_weight, route, live, full):
    m, width = tokens.shape
    own = gate_weight.shape[1]
    rows_all = route.shape[0]
    rows = rows_all // 8
    hr = rows // 2
    vm = pltpu.VMEM
    dma = pltpu.SemaphoreType.DMA
    hbm = pl.BlockSpec(memory_space=pltpu.HBM)
    whole = pl.BlockSpec(memory_space=pltpu.VMEM)
    operands = (tokens, gate_weight, up_weight, route.reshape(8, rows), live.reshape(8, rows))
    return pl.pallas_call(
        functools.partial(main_kernel, rows_all, full),
        name="hidden_factor",
        out_shape=(
            jax.ShapeDtypeStruct((8, rows, own), BF16),
            jax.ShapeDtypeStruct((8, rows, own), BF16),
            jax.ShapeDtypeStruct((2, 8, rows, own), BF16),
            jax.ShapeDtypeStruct((PANEL, PANEL), F32),
            jax.ShapeDtypeStruct((8, 128), F32),
        ),
        in_specs=[hbm] * 5,
        out_specs=(whole,) * 5,
        scratch_shapes=[
            vm((2, 4, 2, m, width), BF16),
            vm(gate_weight.shape, BF16),
            vm(up_weight.shape, BF16),
            vm((8, rows), jnp.int32),
            vm((8, rows), jnp.int32),
            vm((rows_all, 128), jnp.int32),
            vm((2, 4, rows, own), F32),
            vm((2, 4, rows, own), F32),
            vm((4, rows, own), F32),
            vm((2, hr, own), F32),
            vm((2, rows, own), F32),
            vm((2, rows, own), F32),
            vm((2, 2, rows, own), F32),
            vm((rows, own), F32),
            vm((rows, own), F32),
            vm((rows, own), BF16),
            vm((PANEL, PANEL), F32),
            vm((6, 8, 128), F32),
            vm((4, 8, 128), F32),
            vm((4, 8, 128), F32),
            dma((5,)),
            dma((21,)), dma((21,)),
            dma((17,)), dma((17,)),
            dma((5,)), dma((1,)),
            dma((8,)), dma((8,)),
            dma((8,)), dma((8,)),
            dma((9,)), dma((9,)),
            dma((8,)), dma((8,)),
            dma((8,)), dma((8,)),
            dma((8,)), dma((8,)),
        ],
        compiler_params=pltpu.CompilerParams(collective_id=0, has_side_effects=True, vmem_limit_bytes=46000 * 2**10),
    )(*(pltpu.with_memory_space_constraint(a, pltpu.HBM) for a in operands))


def pair(a):
    high = a.astype(BF16)
    return high, (a - high.astype(F32)).astype(BF16)


def dot3_t(a, b):
    def one(u, v):
        return lax.dot_general(u, v, (((1,), (1,)), ((), ())), preferred_element_type=F32)

    return one(a[0], b[0]) + (one(a[0], b[1]) + one(a[1], b[0]))


def outputs_kernel(hp_ref, hcol_ref, hl_ref, x_ref, ridge_ref, panel_ref, trailing_ref, panel, trailing, sems):
    xh, z, core = (lax.axis_index(a) for a in ROW)
    xl, y = (lax.axis_index(a) for a in COL)
    ci, ri = xl * 4 + y, (xh * 4 + z) * 2 + core
    rows_all = hp_ref.shape[0] * hp_ref.shape[1]
    n = x_ref.shape[0]
    ridge = ridge_ref[0:1, 0:1]
    on_line = lax.broadcasted_iota(jnp.int32, (n, n), 0) == lax.broadcasted_iota(jnp.int32, (n, n), 1)
    hp = hp_ref[...].reshape(rows_all, n)
    hcol = hcol_ref[...].reshape(rows_all, n)
    x = pair(x_ref[...])

    def with_ridge(gram, here):
        return gram / rows_all + jnp.where(jnp.logical_and(on_line, here), ridge, 0.0)

    right = pair(dot3_t(pair(with_ridge(cross(hcol, hp), ri == 0)), x))
    copies = []
    for j in range(2):
        here = pl.ds(j * n, n)
        left = hl_ref[j].reshape(rows_all, n)
        down = dot3_t(pair(with_ridge(cross(left, hp), ci * 2 + j == 0)), x)
        panel[here, :] = down
        copies.append(pltpu.make_async_copy(panel.at[here], panel_ref.at[here], sems.at[j]))
        copies[-1].start()
        trailing[here, :] = with_ridge(cross(left, hcol), ci * 2 + j == ri) - dot3_t(pair(down), right)
        copies.append(pltpu.make_async_copy(trailing.at[here], trailing_ref.at[here], sems.at[2 + j]))
        copies[-1].start()
    for copy in copies:
        copy.wait()


def outputs_of(hp, hcol, hl, x, ridge):
    n = x.shape[0]
    hbm = pl.BlockSpec(memory_space=pl.ANY)
    whole = pl.BlockSpec(memory_space=pltpu.VMEM)
    return pl.pallas_call(
        outputs_kernel,
        name="outputs",
        out_shape=(jax.ShapeDtypeStruct((2 * n, n), F32), jax.ShapeDtypeStruct((2 * n, n), F32)),
        in_specs=[whole] * 5,
        out_specs=(hbm, hbm),
        scratch_shapes=[pltpu.VMEM((2 * n, n), F32), pltpu.VMEM((2 * n, n), F32), pltpu.SemaphoreType.DMA((4,))],
        compiler_params=pltpu.CompilerParams(vmem_limit_bytes=28 * 2**20),
    )(hp, hcol, hl, x, ridge)


def per_device(tokens, gate_weight, up_weight, route, live):
    full = gate_weight.shape[1] * lax.axis_size(ROW)
    return outputs_of(*main_of(tokens, gate_weight, up_weight, route, live, full))


def solution(mesh):
    finer = Mesh(mesh.devices.reshape(2, 4, 2, 2, 4), ("row_0", "row_1", "row_2", "col_0", "col_1"))
    placed = (P(ROW, COL), P(COL, ROW), P(COL, ROW), P(), P())
    return jax.shard_map(
        per_device,
        mesh=finer,
        in_specs=placed,
        out_specs=(P(COL, None), P(COL, ROW)),
        check_vma=False,
    )
```

```python
import functools

import jax
import jax.numpy as jnp
from jax import lax
from jax.experimental import pallas as pl
from jax.experimental.pallas import tpu as pltpu
from jax.sharding import Mesh
from jax.sharding import PartitionSpec as P

PANEL = 512
COL = ("col_0", "col_1")
ROW = ("row_0", "row_1", "row_2")
ROW_COL = ("row_0", "row_1", "row_2", "col_0", "col_1")
MESH = pl.DeviceIdType.MESH
F32 = jnp.float32
BF16 = jnp.bfloat16

damping = 0.1


def remote(src, dst, sems, slot, where):
    send, recv = sems
    return pltpu.make_async_remote_copy(
        src_ref=src, dst_ref=dst, send_sem=send.at[slot], recv_sem=recv.at[slot],
        device_id=where, device_id_type=MESH,
    )


NB = 128
HIGH = lax.Precision.HIGHEST


def spread(x):
    return jnp.broadcast_to(x, (8, NB))


def tile_inverse(rows, halfway):
    count = len(rows)
    lane = lax.broadcasted_iota(jnp.int32, (8, NB), 1)
    sub = lax.broadcasted_iota(jnp.int32, (8, NB), 0)
    rows = list(rows)
    out = []
    for g in range(count):
        top = [spread(rows[g][:, 8 * g + c:8 * g + c + 1]) for c in range(8)]
        e = [[spread(top[b][a:a + 1, :]) for b in range(a + 1)] for a in range(8)]
        inside = (lane >= 8 * g) & (lane < 8 * g + 8)
        group = jnp.where(inside, (lane == sub + 8 * g).astype(F32), rows[g])
        own = [spread(group[c:c + 1, :]) for c in range(8)]
        inverse = [None] * 8
        m = [[None] * 8 for _ in range(8)]
        for c in range(8):
            if c % 2 == 0:
                inverse[c] = 1.0 / e[c][c]
                inverse[c + 1] = e[c][c] / (e[c][c] * e[c + 1][c + 1] - e[c + 1][c] * e[c + 1][c])
            for a in range(c + 1, 8):
                m[a][c] = e[a][c] * inverse[c]
                for b in range(c + 1, a + 1):
                    e[a][b] = e[a][b] - m[a][c] * e[b][c]
                own[a] = own[a] - m[a][c] * own[c]
        back = [own[c] * inverse[c] for c in range(8)]
        for b in range(7, 0, -1):
            for c in range(b):
                back[c] = back[c] - m[b][c] * back[b]
        for i in range(g + 1, count):
            terms = [spread(rows[i][:, 8 * g + c:8 * g + c + 1]) * back[c] for c in range(8)]
            while len(terms) > 1:
                terms = [terms[k] + terms[k + 1] for k in range(0, len(terms), 2)]
            rows[i] = jnp.where(inside, 0.0, rows[i]) - terms[0]
        pivots, done = e[0][0], own[0]
        for c in range(1, 8):
            pivots = jnp.where(sub == c, e[c][c], pivots)
            done = jnp.where(sub == c, own[c], done)
        out.append(jnp.where(lane <= sub + 8 * g, done * lax.rsqrt(pivots), 0.0))
        if g == count // 2 - 1:
            halfway()
    return out


def dot_t(a, b):
    return lax.dot_general(a, b, (((1,), (1,)), ((), ())), precision=HIGH, preferred_element_type=F32)


def dot(a, b):
    return jnp.dot(a, b, precision=HIGH, preferred_element_type=F32)


def factor_inverse(a_ref, x_ref, between):
    n = a_ref.shape[0]
    x_ref[...] = jnp.zeros_like(x_ref)
    for k in range(n // NB):
        lo, hi = k * NB, (k + 1) * NB
        part = tile_inverse(
            [a_ref[lo + 8 * i:lo + 8 * i + 8, lo:hi] for i in range(NB // 8)], lambda: between(2 * k)
        )
        for i, rows in enumerate(part):
            x_ref[lo + 8 * i:lo + 8 * i + 8, lo:hi] = rows
        x = x_ref[lo:hi, lo:hi]
        if hi < n:
            low = dot_t(a_ref[hi:, lo:hi], x)
            a_ref[hi:, lo:hi] = low
            a_ref[hi:, hi:] = a_ref[hi:, hi:] - dot_t(low, low)
        between(2 * k + 1)
        if k:
            x_ref[lo:hi, :lo] = -dot(x, dot(a_ref[lo:hi, :lo], x_ref[:lo, :lo]))


def cross(a, b):
    return lax.dot_general(a, b, (((0,), (0,)), ((), ())), preferred_element_type=F32)


def turned(row):
    return jnp.broadcast_to(row, (128, 128)).astype(F32).T


def main_kernel(
    total_rows, full, tok_ref, gate_ref, up_ref, route_in, live_in,
    hp_ref, hcol_ref, hl_ref, x_ref, ridge_ref,
    tk, gw, uw, route_ref, live_ref, spots, tg, tu, rgx, rg1, rg2, ru1, ru2, rux, uout, hid, corner, tr, tz, ty, own_sem,
    a_send, a_recv, r_send, r_recv, p1s, p1r, p2s, p2r, p3s, p3r, ts, tq, hs, hr_sem, qs, qr, ls, lr,
):
    xh, z, core = (lax.axis_index(a) for a in ROW)
    xl, y = (lax.axis_index(a) for a in COL)
    oh, oc, ol = 1 - xh, 1 - core, 1 - xl
    zn, zp, zf = (z + 1) % 4, (z + 3) % 4, (z + 2) % 4
    yn, yp, yf = (y + 1) % 4, (y + 3) % 4, (y + 2) % 4
    ci, ki = xl * 4 + y, xh * 4 + z
    ri = ki * 2 + core
    to_x, to_core = {"row_0": oh}, {"row_2": oc}
    to_zn, to_zp, to_zf = {"row_1": zn}, {"row_1": zp}, {"row_1": zf}
    to_l, to_yn, to_yp = {"col_0": ol}, {"col_1": yn}, {"col_1": yp}
    mirror = {"row_0": xl, "row_1": y, "col_0": xh, "col_1": z}
    away = jnp.logical_or(xh != xl, z != y)
    m = tok_ref.shape[0]
    cut = m * 5 // 8
    to_yf = {"col_1": yf}
    peers = [to_x, to_core, to_zn, to_zp, to_zf, to_l, to_yn, to_yp, to_yf]
    col_from = {(a, b): (xl + a) % 2 * 4 + (y + 4 - b) % 4 for a in range(2) for b in range(4)}

    own = pltpu.make_async_copy(tok_ref, tk.at[xh, z, core], own_sem.at[0])
    own.start()
    lists = [
        pltpu.make_async_copy(src, dst, own_sem.at[3 + i])
        for i, (src, dst) in enumerate(((route_in, route_ref), (live_in, live_ref)))
    ]
    for copy in lists:
        copy.start()
    gcopy = pltpu.make_async_copy(gate_ref, gw, own_sem.at[1])
    gcopy.start()
    ucopy = pltpu.make_async_copy(up_ref, uw, own_sem.at[2])
    ucopy.start()
    barrier = pltpu.get_barrier_semaphore()
    for peer in peers:
        pl.semaphore_signal(barrier, inc=1, device_id=peer, device_id_type=MESH)

    @pl.when(away)
    def _():
        pl.semaphore_signal(barrier, inc=1, device_id=mirror, device_id_type=MESH)

    rows = total_rows // 8
    for copy in lists:
        copy.wait()
    for t in range(8):
        spots[pl.ds(t * rows, rows), :] = turned(route_ref[t:t + 1, :]).astype(jnp.int32)
    own.wait()

    @pl.when(away)
    def _():
        pl.semaphore_wait(barrier, len(peers) + 1)

    @pl.when(jnp.logical_not(away))
    def _():
        pl.semaphore_wait(barrier, len(peers))

    started = []

    def send(sems, slot, src, dst, where):
        copy = remote(src, dst, sems, slot, where)
        copy.start()
        started.append(copy)

    def arrive(sems, slot, ref):
        remote(ref, ref, sems, slot, to_core).wait_recv()

    def pass_on(sems, slot, ref, where):
        send(sems, slot, ref, ref, where)

    A = (a_send, a_recv)

    def block(h, zz, k, lo=0, n=m):
        return tk.at[h, zz, k, pl.ds(lo, n)]

    pass_on(A, 0, block(xh, z, core), to_x)
    pass_on(A, 1, block(xh, z, core), to_zn)
    pass_on(A, 2, block(xh, z, core), to_zp)
    pass_on(A, 3, block(xh, z, core), to_zf)
    pass_on(A, 10, block(xh, z, core), to_core)
    arrive(A, 1, block(xh, zp, core))
    pass_on(A, 7, block(xh, zp, core, cut, m - cut), to_x)
    pass_on(A, 11, block(xh, zp, core), to_core)
    arrive(A, 2, block(xh, zn, core))
    pass_on(A, 8, block(xh, zn, core, cut, m - cut), to_x)
    pass_on(A, 12, block(xh, zn, core), to_core)
    arrive(A, 0, block(oh, z, core))
    pass_on(A, 4, block(oh, z, core, 0, cut), to_zn)
    pass_on(A, 5, block(oh, z, core, 0, cut), to_zp)
    pass_on(A, 6, block(oh, z, core, 0, cut), to_zf)
    pass_on(A, 14, block(oh, z, core), to_core)
    arrive(A, 3, block(xh, zf, core))
    pass_on(A, 9, block(xh, zf, core, cut, m - cut), to_x)
    pass_on(A, 13, block(xh, zf, core), to_core)
    for slot, zz in ((0, zp), (1, zn), (2, zf)):
        arrive(A, 4 + slot, block(oh, zz, core, 0, cut))
        pass_on(A, 15 + slot, block(oh, zz, core, 0, cut), to_core)
        arrive(A, 7 + slot, block(oh, zz, core, cut, m - cut))
        pass_on(A, 18 + slot, block(oh, zz, core, cut, m - cut), to_core)
    for slot, (h, zz) in enumerate(((xh, z), (xh, zp), (xh, zn), (xh, zf), (oh, z))):
        arrive(A, 10 + slot, block(h, zz, oc))
    for slot, zz in ((0, zp), (1, zn), (2, zf)):
        arrive(A, 15 + slot, block(oh, zz, oc, 0, cut))
        arrive(A, 18 + slot, block(oh, zz, oc, cut, m - cut))
    gcopy.wait()
    ucopy.wait()

    R = (r_send, r_recv)
    hr = rows // 2
    pool = 16 * m
    width = tk.shape[-1]

    def tile(b):
        spot = jnp.concatenate(
            [spots[pl.ds(pl.multiple_of((e * 4 + b) * rows, rows), rows), :] for e in range(2)], axis=0
        )
        spot = jnp.concatenate([spot] * (pool // 128), axis=1)
        hot = (spot == lax.broadcasted_iota(jnp.int32, (2 * rows, pool), 1)).astype(F32).astype(BF16)
        chosen = jnp.dot(hot, tk[...].reshape(pool, width), preferred_element_type=F32).astype(BF16)
        g = jnp.dot(chosen, gw[...], preferred_element_type=F32)
        u = jnp.dot(chosen, uw[...], preferred_element_type=F32)
        for e in range(2):
            tg[e, b] = g[e * rows:(e + 1) * rows]
            tu[e, b] = u[e * rows:(e + 1) * rows]

    top, bottom = pl.ds(0, hr), pl.ds(hr, hr)
    tile(yf)
    send(R, 0, tg.at[ol, yf], rgx.at[0], to_l)
    send(R, 4, tu.at[0, yf], ru1.at[0], to_yn)
    send(R, 5, tu.at[1, yf], ru1.at[1], to_yp)
    tile(yn)
    send(R, 1, tg.at[ol, yn], rgx.at[1], to_l)
    send(R, 6, tu.at[1, yn], ru2.at[0, 1], to_yn)
    tile(yp)
    send(R, 2, tg.at[ol, yp], rgx.at[2], to_l)
    send(R, 7, tu.at[0, yp], ru2.at[1, 0], to_yp)
    tile(y)
    send(R, 3, tg.at[ol, y], rgx.at[3], to_l)
    arrive(R, 4, ru1.at[0])
    tu[0, yn] = tu[0, yn] + ru1[0]
    send(R, 8, tu.at[0, yn], ru2.at[0, 0], to_yn)
    arrive(R, 5, ru1.at[1])
    tu[1, yp] = tu[1, yp] + ru1[1]
    send(R, 9, tu.at[1, yp], ru2.at[1, 1], to_yp)
    arrive(R, 0, rgx.at[0])
    tg[xl, yf] = tg[xl, yf] + rgx[0]
    send(R, 10, tg.at[xl, yf, top], rg1.at[0], to_yn)
    send(R, 11, tg.at[xl, yf, bottom], rg1.at[1], to_yp)
    arrive(R, 1, rgx.at[1])
    tg[xl, yn] = tg[xl, yn] + rgx[1]
    send(R, 12, tg.at[xl, yn, bottom], rg2.at[0, bottom], to_yn)
    arrive(R, 2, rgx.at[2])
    tg[xl, yp] = tg[xl, yp] + rgx[2]
    send(R, 13, tg.at[xl, yp, top], rg2.at[1, top], to_yp)
    arrive(R, 6, ru2.at[0, 1])
    arrive(R, 8, ru2.at[0, 0])
    arrive(R, 7, ru2.at[1, 0])
    arrive(R, 9, ru2.at[1, 1])
    uout[...] = tu[ol, y] + ru2[0, ol] + ru2[1, ol]
    send(R, 14, uout, rux, to_l)
    arrive(R, 10, rg1.at[0])
    tg[xl, yn, top] = tg[xl, yn, top] + rg1[0]
    send(R, 15, tg.at[xl, yn, top], rg2.at[0, top], to_yn)
    arrive(R, 11, rg1.at[1])
    tg[xl, yp, bottom] = tg[xl, yp, bottom] + rg1[1]
    send(R, 16, tg.at[xl, yp, bottom], rg2.at[1, bottom], to_yp)
    mask = jnp.concatenate([turned(live_ref[pl.ds(ci, 1), :])] * (hid.shape[1] // 128), axis=1)
    arrive(R, 3, rgx.at[3])
    arrive(R, 12, rg2.at[0, bottom])
    arrive(R, 13, rg2.at[1, top])
    arrive(R, 15, rg2.at[0, top])
    arrive(R, 16, rg2.at[1, bottom])
    gate = tg[xl, y] + rgx[3] + rg2[0] + rg2[1]
    part = tu[xl, y] + ru2[0, xl] + ru2[1, xl]
    act = gate / (1.0 + jnp.exp(-gate)) * mask
    arrive(R, 14, rux)
    made = (act * (part + rux[...])).astype(BF16)
    hid[...] = made
    hcol_ref[ci] = made

    half = rows // 2
    at_root = jnp.logical_and(xh == 0, z == 0)
    holder = jnp.logical_and(at_root, core == 0)

    def by_half(c, k):
        return hp_ref.at[c, pl.ds(pl.multiple_of(k * half, half), half)]

    mine = by_half(ci, core)
    give = remote(hid.at[pl.ds(half, half)], hp_ref.at[ci, pl.ds(half, half)], (p1s, p1r), 0, to_core)
    hops = [
        pltpu.make_async_remote_copy(mine, mine, p1s.at[1 + i], p1r.at[0], device_id=where, device_id_type=MESH)
        for i, where in enumerate((to_x, to_zn, to_zp, to_zf))
    ]

    @pl.when(holder)
    def _():
        hp_ref[ci, pl.ds(0, half)] = made[:half]
        give.start()
        for hop in hops:
            hop.start()

    along = ((1, to_yn), (3, to_yp), (2, to_yf))
    across = remote(hid, hl_ref.at[core, ci], (qs, qr), 0, mirror)
    stay = pltpu.make_async_copy(hid, hl_ref.at[core, ci], own_sem.at[0])
    four, five, six = (hs, hr_sem), (qs, qr), (ls, lr)
    cp = ol * 4 + y

    @pl.when(away)
    def _():
        across.start()

    @pl.when(jnp.logical_not(away))
    def _():
        stay.start()

    wide = made.astype(F32)
    squares = jnp.zeros((8, 128), F32)
    for i in range(0, rows, 8):
        for j in range(0, hid.shape[1], 128):
            piece = wide[i:i + 8, j:j + 128]
            squares = squares + piece * piece
    seven = (ts, tq)
    tr[0] = squares
    send(seven, 0, tr.at[0], tr.at[1], to_core)
    arrive(seven, 0, tr.at[1])
    tr[2] = tr[0] + tr[1]
    send(seven, 1, tr.at[2], tr.at[3], to_x)

    @pl.when(jnp.logical_not(holder))
    def _():
        arrive((p1s, p1r), 0, mine)

    @pl.when(jnp.logical_and(at_root, core == 1))
    def _():
        hops[0].start()

    @pl.when(jnp.logical_and(z == 0, jnp.logical_not(holder)))
    def _():
        for hop in hops[1:]:
            hop.start()

    two, three = (p2s, p2r), (p3s, p3r)
    pass_on(two, 4, mine, to_l)
    for d, where in along:
        pass_on(two, d, mine, where)
    pass_on(three, 0, mine, to_core)

    def spread_block(h, zz, k):
        return hl_ref.at[k, h * 4 + zz]

    arrive(seven, 1, tr.at[3])
    tz[z] = tr[2] + tr[3]
    for d, where in ((1, to_zn), (3, to_zp), (2, to_zf)):
        pass_on(seven, 1 + d, tz.at[z], where)
    here = spread_block(xh, z, core)

    @pl.when(away)
    def _():
        across.wait_recv()

    @pl.when(jnp.logical_not(away))
    def _():
        stay.wait()

    for slot, where in ((1, to_x), (2, to_zn), (3, to_zp), (4, to_zf)):
        pass_on(five, slot, here, where)
    arrive(two, 4, by_half(cp, core))
    for d, where in along:
        pass_on(two, 4 + d, by_half(cp, core), where)
    pass_on(three, 4, by_half(cp, core), to_core)
    for d, zz in ((1, zp), (3, zn), (2, zf)):
        arrive(seven, 1 + d, tz.at[zz])
    tr[4] = jnp.sum(tz[...], axis=0)
    send(seven, 5, tr.at[4], tr.at[5], to_l)
    send(four, 4, hid, hcol_ref.at[ci], to_l)
    order = [(0, 1), (0, 3), (0, 2), (1, 1), (1, 3), (1, 2)]
    for s in order:
        slot = s[0] * 4 + s[1]
        arrive(two, slot, by_half(col_from[s], core))
        pass_on(three, slot, by_half(col_from[s], core), to_core)
        if s == (0, 2):
            arrive(seven, 5, tr.at[5])
            ty[y] = tr[4] + tr[5]
            for d, where in along:
                pass_on(seven, 5 + d, ty.at[y], where)
            for d, where in along:
                send(four, d, hid, hcol_ref.at[ci], where)
    arrive(three, 0, by_half(ci, oc))
    arrive(three, 4, by_half(cp, oc))
    for s in order:
        arrive(three, s[0] * 4 + s[1], by_half(col_from[s], oc))
    panel = corner.shape[0]
    hp = hp_ref[...].reshape(total_rows, panel)
    on_line = lax.broadcasted_iota(jnp.int32, (panel, panel), 0) == lax.broadcasted_iota(jnp.int32, (panel, panel), 1)
    gram = cross(hp, hp) / total_rows
    for d, yy in ((1, yp), (3, yn), (2, yf)):
        arrive(seven, 5 + d, ty.at[yy])
    total = jnp.sum(jnp.sum(ty[...], axis=0), axis=(0, 1), keepdims=True)
    ridge = damping * total / (total_rows * full)
    ridge_ref[...] = jnp.broadcast_to(ridge, (8, 128))
    scale = 1.0 / ridge
    corner[...] = (gram + jnp.where(on_line, ridge, 0.0)) * scale

    def between(k):
        if k == 0:
            arrive(five, 1, spread_block(oh, z, core))
            for slot, where in ((5, to_zn), (6, to_zp), (7, to_zf)):
                pass_on(five, slot, spread_block(oh, z, core), where)
            pass_on(six, 0, here, to_core)
            pass_on(six, 1, spread_block(oh, z, core), to_core)
            arrive(four, 4, hcol_ref.at[cp])
            for d, where in along:
                pass_on(four, 4 + d, hcol_ref.at[cp], where)

        elif k == 2:
            for slot, zz in ((2, zp), (3, zn), (4, zf)):
                arrive(five, slot, spread_block(xh, zz, core))
                pass_on(six, slot, spread_block(xh, zz, core), to_core)
        elif k == 5:
            for slot, zz in ((5, zp), (6, zn), (7, zf)):
                arrive(five, slot, spread_block(oh, zz, core))
                pass_on(six, slot, spread_block(oh, zz, core), to_core)

    factor_inverse(corner, x_ref, between)
    x_ref[...] = x_ref[...] * jnp.sqrt(scale)
    for slot, (h, zz) in enumerate(((xh, z), (oh, z), (xh, zp), (xh, zn), (xh, zf), (oh, zp), (oh, zn), (oh, zf))):
        arrive(six, slot, spread_block(h, zz, oc))
    for s in order:
        arrive(four, s[0] * 4 + s[1], hcol_ref.at[col_from[s]])
    for copy in started:
        copy.wait_send()

    @pl.when(away)
    def _():
        across.wait_send()

    @pl.when(holder)
    def _():
        give.wait_send()

    @pl.when(at_root)
    def _():
        hops[0].wait_send()

    @pl.when(z == 0)
    def _():
        for hop in hops[1:]:
            hop.wait_send()


def main_of(tokens, gate_weight, up_weight, route, live, full):
    m, width = tokens.shape
    own = gate_weight.shape[1]
    rows_all = route.shape[0]
    rows = rows_all // 8
    hr = rows // 2
    vm = pltpu.VMEM
    dma = pltpu.SemaphoreType.DMA
    hbm = pl.BlockSpec(memory_space=pltpu.HBM)
    whole = pl.BlockSpec(memory_space=pltpu.VMEM)
    operands = (tokens, gate_weight, up_weight, route.reshape(8, rows), live.reshape(8, rows))
    return pl.pallas_call(
        functools.partial(main_kernel, rows_all, full),
        name="hidden_factor",
        out_shape=(
            jax.ShapeDtypeStruct((8, rows, own), BF16),
            jax.ShapeDtypeStruct((8, rows, own), BF16),
            jax.ShapeDtypeStruct((2, 8, rows, own), BF16),
            jax.ShapeDtypeStruct((PANEL, PANEL), F32),
            jax.ShapeDtypeStruct((8, 128), F32),
        ),
        in_specs=[hbm] * 5,
        out_specs=(whole,) * 5,
        scratch_shapes=[
            vm((2, 4, 2, m, width), BF16),
            vm(gate_weight.shape, BF16),
            vm(up_weight.shape, BF16),
            vm((8, rows), jnp.int32),
            vm((8, rows), jnp.int32),
            vm((rows_all, 128), jnp.int32),
            vm((2, 4, rows, own), F32),
            vm((2, 4, rows, own), F32),
            vm((4, rows, own), F32),
            vm((2, hr, own), F32),
            vm((2, rows, own), F32),
            vm((2, rows, own), F32),
            vm((2, 2, rows, own), F32),
            vm((rows, own), F32),
            vm((rows, own), F32),
            vm((rows, own), BF16),
            vm((PANEL, PANEL), F32),
            vm((6, 8, 128), F32),
            vm((4, 8, 128), F32),
            vm((4, 8, 128), F32),
            dma((5,)),
            dma((21,)), dma((21,)),
            dma((17,)), dma((17,)),
            dma((5,)), dma((1,)),
            dma((8,)), dma((8,)),
            dma((8,)), dma((8,)),
            dma((9,)), dma((9,)),
            dma((8,)), dma((8,)),
            dma((8,)), dma((8,)),
            dma((8,)), dma((8,)),
        ],
        compiler_params=pltpu.CompilerParams(collective_id=0, has_side_effects=True, vmem_limit_bytes=46000 * 2**10),
    )(*(pltpu.with_memory_space_constraint(a, pltpu.HBM) for a in operands))


def pair(a):
    high = a.astype(BF16)
    return high, (a - high.astype(F32)).astype(BF16)


def dot3_t(a, b):
    def one(u, v):
        return lax.dot_general(u, v, (((1,), (1,)), ((), ())), preferred_element_type=F32)

    return one(a[0], b[0]) + (one(a[0], b[1]) + one(a[1], b[0]))


def outputs_kernel(hp_ref, hcol_ref, hl_ref, x_ref, ridge_ref, panel_ref, trailing_ref, panel, trailing, sems):
    xh, z, core = (lax.axis_index(a) for a in ROW)
    xl, y = (lax.axis_index(a) for a in COL)
    ci, ri = xl * 4 + y, (xh * 4 + z) * 2 + core
    rows_all = hp_ref.shape[0] * hp_ref.shape[1]
    n = x_ref.shape[0]
    ridge = ridge_ref[0:1, 0:1]
    on_line = lax.broadcasted_iota(jnp.int32, (n, n), 0) == lax.broadcasted_iota(jnp.int32, (n, n), 1)
    hp = hp_ref[...].reshape(rows_all, n)
    hcol = hcol_ref[...].reshape(rows_all, n)
    x = pair(x_ref[...])

    def with_ridge(gram, here):
        return gram / rows_all + jnp.where(jnp.logical_and(on_line, here), ridge, 0.0)

    right = pair(dot3_t(pair(with_ridge(cross(hcol, hp), ri == 0)), x))
    copies = []
    for j in range(2):
        here = pl.ds(j * n, n)
        left = hl_ref[j].reshape(rows_all, n)
        down = dot3_t(pair(with_ridge(cross(left, hp), ci * 2 + j == 0)), x)
        panel[here, :] = down
        copies.append(pltpu.make_async_copy(panel.at[here], panel_ref.at[here], sems.at[j]))
        copies[-1].start()
        trailing[here, :] = with_ridge(cross(left, hcol), ci * 2 + j == ri) - dot3_t(pair(down), right)
        copies.append(pltpu.make_async_copy(trailing.at[here], trailing_ref.at[here], sems.at[2 + j]))
        copies[-1].start()
    for copy in copies:
        copy.wait()


def outputs_of(hp, hcol, hl, x, ridge):
    n = x.shape[0]
    hbm = pl.BlockSpec(memory_space=pl.ANY)
    whole = pl.BlockSpec(memory_space=pltpu.VMEM)
    return pl.pallas_call(
        outputs_kernel,
        name="outputs",
        out_shape=(jax.ShapeDtypeStruct((2 * n, n), F32), jax.ShapeDtypeStruct((2 * n, n), F32)),
        in_specs=[whole] * 5,
        out_specs=(hbm, hbm),
        scratch_shapes=[pltpu.VMEM((2 * n, n), F32), pltpu.VMEM((2 * n, n), F32), pltpu.SemaphoreType.DMA((4,))],
        compiler_params=pltpu.CompilerParams(vmem_limit_bytes=28 * 2**20),
    )(hp, hcol, hl, x, ridge)


def per_device(tokens, gate_weight, up_weight, route, live):
    full = gate_weight.shape[1] * lax.axis_size(ROW)
    return outputs_of(*main_of(tokens, gate_weight, up_weight, route, live, full))


def solution(mesh):
    finer = Mesh(mesh.devices.reshape(2, 4, 2, 2, 4), ("row_0", "row_1", "row_2", "col_0", "col_1"))
    placed = (P(ROW, COL), P(COL, ROW), P(COL, ROW), P(), P())
    return jax.shard_map(
        per_device,
        mesh=finer,
        in_specs=placed,
        out_specs=(P(COL, None), P(COL, ROW)),
        check_vma=False,
    )
```

```python
import functools

import jax
import jax.numpy as jnp
from jax import lax
from jax.experimental import pallas as pl
from jax.experimental.pallas import tpu as pltpu
from jax.sharding import Mesh
from jax.sharding import PartitionSpec as P

PANEL = 512
COL = ("col_0", "col_1")
ROW = ("row_0", "row_1", "row_2")
ROW_COL = ("row_0", "row_1", "row_2", "col_0", "col_1")
MESH = pl.DeviceIdType.MESH
F32 = jnp.float32
BF16 = jnp.bfloat16

damping = 0.1


def remote(src, dst, sems, slot, where):
    send, recv = sems
    return pltpu.make_async_remote_copy(
        src_ref=src, dst_ref=dst, send_sem=send.at[slot], recv_sem=recv.at[slot],
        device_id=where, device_id_type=MESH,
    )


NB = 128
HIGH = lax.Precision.HIGHEST


def spread(x):
    return jnp.broadcast_to(x, (8, NB))


def tile_inverse(rows, halfway):
    count = len(rows)
    lane = lax.broadcasted_iota(jnp.int32, (8, NB), 1)
    sub = lax.broadcasted_iota(jnp.int32, (8, NB), 0)
    rows = list(rows)
    out = []
    for g in range(count):
        top = [spread(rows[g][:, 8 * g + c:8 * g + c + 1]) for c in range(8)]
        e = [[spread(top[b][a:a + 1, :]) for b in range(a + 1)] for a in range(8)]
        inside = (lane >= 8 * g) & (lane < 8 * g + 8)
        group = jnp.where(inside, (lane == sub + 8 * g).astype(F32), rows[g])
        own = [spread(group[c:c + 1, :]) for c in range(8)]
        inverse = [None] * 8
        m = [[None] * 8 for _ in range(8)]
        for c in range(8):
            if c % 2 == 0:
                inverse[c] = 1.0 / e[c][c]
                inverse[c + 1] = e[c][c] / (e[c][c] * e[c + 1][c + 1] - e[c + 1][c] * e[c + 1][c])
            for a in range(c + 1, 8):
                m[a][c] = e[a][c] * inverse[c]
                for b in range(c + 1, a + 1):
                    e[a][b] = e[a][b] - m[a][c] * e[b][c]
                own[a] = own[a] - m[a][c] * own[c]
        back = [own[c] * inverse[c] for c in range(8)]
        for b in range(7, 0, -1):
            for c in range(b):
                back[c] = back[c] - m[b][c] * back[b]
        for i in range(g + 1, count):
            terms = [spread(rows[i][:, 8 * g + c:8 * g + c + 1]) * back[c] for c in range(8)]
            while len(terms) > 1:
                terms = [terms[k] + terms[k + 1] for k in range(0, len(terms), 2)]
            rows[i] = jnp.where(inside, 0.0, rows[i]) - terms[0]
        pivots, done = e[0][0], own[0]
        for c in range(1, 8):
            pivots = jnp.where(sub == c, e[c][c], pivots)
            done = jnp.where(sub == c, own[c], done)
        out.append(jnp.where(lane <= sub + 8 * g, done * lax.rsqrt(pivots), 0.0))
        if g == count // 2 - 1:
            halfway()
    return out


def dot_t(a, b):
    return lax.dot_general(a, b, (((1,), (1,)), ((), ())), precision=HIGH, preferred_element_type=F32)


def dot(a, b):
    return jnp.dot(a, b, precision=HIGH, preferred_element_type=F32)


def factor_inverse(a_ref, x_ref, between):
    n = a_ref.shape[0]
    x_ref[...] = jnp.zeros_like(x_ref)
    for k in range(n // NB):
        lo, hi = k * NB, (k + 1) * NB
        part = tile_inverse(
            [a_ref[lo + 8 * i:lo + 8 * i + 8, lo:hi] for i in range(NB // 8)], lambda: between(2 * k)
        )
        for i, rows in enumerate(part):
            x_ref[lo + 8 * i:lo + 8 * i + 8, lo:hi] = rows
        x = x_ref[lo:hi, lo:hi]
        if hi < n:
            low = dot_t(a_ref[hi:, lo:hi], x)
            a_ref[hi:, lo:hi] = low
            a_ref[hi:, hi:] = a_ref[hi:, hi:] - dot_t(low, low)
        between(2 * k + 1)
        if k:
            x_ref[lo:hi, :lo] = -dot(x, dot(a_ref[lo:hi, :lo], x_ref[:lo, :lo]))


def cross(a, b):
    return lax.dot_general(a, b, (((0,), (0,)), ((), ())), preferred_element_type=F32)


def turned(row):
    return jnp.broadcast_to(row, (128, 128)).astype(F32).T


def main_kernel(
    total_rows, full, tok_ref, gate_ref, up_ref, route_in, live_in,
    hp_ref, hcol_ref, hl_ref, x_ref, ridge_ref,
    tk, gw, uw, route_ref, live_ref, spots, tg, tu, rgx, rg1, rg2, ru1, ru2, rux, uout, hid, corner, tr, tz, ty, own_sem,
    a_send, a_recv, r_send, r_recv, p1s, p1r, p2s, p2r, p3s, p3r, ts, tq, hs, hr_sem, qs, qr, ls, lr,
):
    xh, z, core = (lax.axis_index(a) for a in ROW)
    xl, y = (lax.axis_index(a) for a in COL)
    oh, oc, ol = 1 - xh, 1 - core, 1 - xl
    zn, zp, zf = (z + 1) % 4, (z + 3) % 4, (z + 2) % 4
    yn, yp, yf = (y + 1) % 4, (y + 3) % 4, (y + 2) % 4
    ci, ki = xl * 4 + y, xh * 4 + z
    ri = ki * 2 + core
    to_x, to_core = {"row_0": oh}, {"row_2": oc}
    to_zn, to_zp, to_zf = {"row_1": zn}, {"row_1": zp}, {"row_1": zf}
    to_l, to_yn, to_yp = {"col_0": ol}, {"col_1": yn}, {"col_1": yp}
    mirror = {"row_0": xl, "row_1": y, "col_0": xh, "col_1": z}
    away = jnp.logical_or(xh != xl, z != y)
    m = tok_ref.shape[0]
    cut = m * 5 // 8
    to_yf = {"col_1": yf}
    peers = [to_x, to_core, to_zn, to_zp, to_zf, to_l, to_yn, to_yp, to_yf]
    col_from = {(a, b): (xl + a) % 2 * 4 + (y + 4 - b) % 4 for a in range(2) for b in range(4)}

    own = pltpu.make_async_copy(tok_ref, tk.at[xh, z, core], own_sem.at[0])
    own.start()
    lists = [
        pltpu.make_async_copy(src, dst, own_sem.at[3 + i])
        for i, (src, dst) in enumerate(((route_in, route_ref), (live_in, live_ref)))
    ]
    for copy in lists:
        copy.start()
    gcopy = pltpu.make_async_copy(gate_ref, gw, own_sem.at[1])
    gcopy.start()
    ucopy = pltpu.make_async_copy(up_ref, uw, own_sem.at[2])
    ucopy.start()
    barrier = pltpu.get_barrier_semaphore()
    for peer in peers:
        pl.semaphore_signal(barrier, inc=1, device_id=peer, device_id_type=MESH)

    @pl.when(away)
    def _():
        pl.semaphore_signal(barrier, inc=1, device_id=mirror, device_id_type=MESH)

    rows = total_rows // 8
    for copy in lists:
        copy.wait()
    for t in range(8):
        spots[pl.ds(t * rows, rows), :] = turned(route_ref[t:t + 1, :]).astype(jnp.int32)
    own.wait()

    @pl.when(away)
    def _():
        pl.semaphore_wait(barrier, len(peers) + 1)

    @pl.when(jnp.logical_not(away))
    def _():
        pl.semaphore_wait(barrier, len(peers))

    started = []

    def send(sems, slot, src, dst, where):
        copy = remote(src, dst, sems, slot, where)
        copy.start()
        started.append(copy)

    def arrive(sems, slot, ref):
        remote(ref, ref, sems, slot, to_core).wait_recv()

    def pass_on(sems, slot, ref, where):
        send(sems, slot, ref, ref, where)

    A = (a_send, a_recv)

    def block(h, zz, k, lo=0, n=m):
        return tk.at[h, zz, k, pl.ds(lo, n)]

    pass_on(A, 0, block(xh, z, core), to_x)
    pass_on(A, 1, block(xh, z, core), to_zn)
    pass_on(A, 2, block(xh, z, core), to_zp)
    pass_on(A, 3, block(xh, z, core), to_zf)
    pass_on(A, 10, block(xh, z, core), to_core)
    arrive(A, 1, block(xh, zp, core))
    pass_on(A, 7, block(xh, zp, core, cut, m - cut), to_x)
    pass_on(A, 11, block(xh, zp, core), to_core)
    arrive(A, 2, block(xh, zn, core))
    pass_on(A, 8, block(xh, zn, core, cut, m - cut), to_x)
    pass_on(A, 12, block(xh, zn, core), to_core)
    arrive(A, 0, block(oh, z, core))
    pass_on(A, 4, block(oh, z, core, 0, cut), to_zn)
    pass_on(A, 5, block(oh, z, core, 0, cut), to_zp)
    pass_on(A, 6, block(oh, z, core, 0, cut), to_zf)
    pass_on(A, 14, block(oh, z, core), to_core)
    arrive(A, 3, block(xh, zf, core))
    pass_on(A, 9, block(xh, zf, core, cut, m - cut), to_x)
    pass_on(A, 13, block(xh, zf, core), to_core)
    for slot, zz in ((0, zp), (1, zn), (2, zf)):
        arrive(A, 4 + slot, block(oh, zz, core, 0, cut))
        pass_on(A, 15 + slot, block(oh, zz, core, 0, cut), to_core)
        arrive(A, 7 + slot, block(oh, zz, core, cut, m - cut))
        pass_on(A, 18 + slot, block(oh, zz, core, cut, m - cut), to_core)
    for slot, (h, zz) in enumerate(((xh, z), (xh, zp), (xh, zn), (xh, zf), (oh, z))):
        arrive(A, 10 + slot, block(h, zz, oc))
    for slot, zz in ((0, zp), (1, zn), (2, zf)):
        arrive(A, 15 + slot, block(oh, zz, oc, 0, cut))
        arrive(A, 18 + slot, block(oh, zz, oc, cut, m - cut))
    gcopy.wait()
    ucopy.wait()

    R = (r_send, r_recv)
    hr = rows // 2
    pool = 16 * m
    width = tk.shape[-1]

    def tile(b, slot):
        spot = jnp.concatenate(
            [spots[pl.ds(pl.multiple_of((e * 4 + b) * rows, rows), rows), :] for e in range(2)], axis=0
        )
        spot = jnp.concatenate([spot] * (pool // 128), axis=1)
        hot = (spot == lax.broadcasted_iota(jnp.int32, (2 * rows, pool), 1)).astype(F32).astype(BF16)
        chosen = jnp.dot(hot, tk[...].reshape(pool, width), preferred_element_type=F32).astype(BF16)
        g = jnp.dot(chosen, gw[...], preferred_element_type=F32)
        for e in range(2):
            tg[e, b] = g[e * rows:(e + 1) * rows]
        send(R, slot, tg.at[ol, b], rgx.at[slot], to_l)
        u = jnp.dot(chosen, uw[...], preferred_element_type=F32)
        for e in range(2):
            tu[e, b] = u[e * rows:(e + 1) * rows]

    top, bottom = pl.ds(0, hr), pl.ds(hr, hr)
    tile(yf, 0)
    send(R, 4, tu.at[0, yf], ru1.at[0], to_yn)
    send(R, 5, tu.at[1, yf], ru1.at[1], to_yp)
    tile(yn, 1)
    send(R, 6, tu.at[1, yn], ru2.at[0, 1], to_yn)
    tile(yp, 2)
    send(R, 7, tu.at[0, yp], ru2.at[1, 0], to_yp)
    tile(y, 3)
    arrive(R, 4, ru1.at[0])
    tu[0, yn] = tu[0, yn] + ru1[0]
    send(R, 8, tu.at[0, yn], ru2.at[0, 0], to_yn)
    arrive(R, 5, ru1.at[1])
    tu[1, yp] = tu[1, yp] + ru1[1]
    send(R, 9, tu.at[1, yp], ru2.at[1, 1], to_yp)
    arrive(R, 0, rgx.at[0])
    tg[xl, yf] = tg[xl, yf] + rgx[0]
    send(R, 10, tg.at[xl, yf, top], rg1.at[0], to_yn)
    send(R, 11, tg.at[xl, yf, bottom], rg1.at[1], to_yp)
    arrive(R, 1, rgx.at[1])
    tg[xl, yn] = tg[xl, yn] + rgx[1]
    send(R, 12, tg.at[xl, yn, bottom], rg2.at[0, bottom], to_yn)
    arrive(R, 2, rgx.at[2])
    tg[xl, yp] = tg[xl, yp] + rgx[2]
    send(R, 13, tg.at[xl, yp, top], rg2.at[1, top], to_yp)
    arrive(R, 6, ru2.at[0, 1])
    arrive(R, 8, ru2.at[0, 0])
    arrive(R, 7, ru2.at[1, 0])
    arrive(R, 9, ru2.at[1, 1])
    uout[...] = tu[ol, y] + ru2[0, ol] + ru2[1, ol]
    send(R, 14, uout, rux, to_l)
    arrive(R, 10, rg1.at[0])
    tg[xl, yn, top] = tg[xl, yn, top] + rg1[0]
    send(R, 15, tg.at[xl, yn, top], rg2.at[0, top], to_yn)
    arrive(R, 11, rg1.at[1])
    tg[xl, yp, bottom] = tg[xl, yp, bottom] + rg1[1]
    send(R, 16, tg.at[xl, yp, bottom], rg2.at[1, bottom], to_yp)
    mask = jnp.concatenate([turned(live_ref[pl.ds(ci, 1), :])] * (hid.shape[1] // 128), axis=1)
    arrive(R, 3, rgx.at[3])
    arrive(R, 12, rg2.at[0, bottom])
    arrive(R, 13, rg2.at[1, top])
    arrive(R, 15, rg2.at[0, top])
    arrive(R, 16, rg2.at[1, bottom])
    gate = tg[xl, y] + rgx[3] + rg2[0] + rg2[1]
    part = tu[xl, y] + ru2[0, xl] + ru2[1, xl]
    act = gate / (1.0 + jnp.exp(-gate)) * mask
    arrive(R, 14, rux)
    made = (act * (part + rux[...])).astype(BF16)
    hid[...] = made
    hcol_ref[ci] = made

    half = rows // 2
    at_root = jnp.logical_and(xh == 0, z == 0)
    holder = jnp.logical_and(at_root, core == 0)

    def by_half(c, k):
        return hp_ref.at[c, pl.ds(pl.multiple_of(k * half, half), half)]

    mine = by_half(ci, core)
    give = remote(hid.at[pl.ds(half, half)], hp_ref.at[ci, pl.ds(half, half)], (p1s, p1r), 0, to_core)
    hops = [
        pltpu.make_async_remote_copy(mine, mine, p1s.at[1 + i], p1r.at[0], device_id=where, device_id_type=MESH)
        for i, where in enumerate((to_x, to_zn, to_zp, to_zf))
    ]

    @pl.when(holder)
    def _():
        hp_ref[ci, pl.ds(0, half)] = made[:half]
        give.start()
        for hop in hops:
            hop.start()

    along = ((1, to_yn), (3, to_yp), (2, to_yf))
    across = remote(hid, hl_ref.at[core, ci], (qs, qr), 0, mirror)
    stay = pltpu.make_async_copy(hid, hl_ref.at[core, ci], own_sem.at[0])
    four, five, six = (hs, hr_sem), (qs, qr), (ls, lr)
    cp = ol * 4 + y

    @pl.when(away)
    def _():
        across.start()

    @pl.when(jnp.logical_not(away))
    def _():
        stay.start()

    wide = made.astype(F32)
    squares = jnp.zeros((8, 128), F32)
    for i in range(0, rows, 8):
        for j in range(0, hid.shape[1], 128):
            piece = wide[i:i + 8, j:j + 128]
            squares = squares + piece * piece
    seven = (ts, tq)
    tr[0] = squares
    send(seven, 0, tr.at[0], tr.at[1], to_core)
    arrive(seven, 0, tr.at[1])
    tr[2] = tr[0] + tr[1]
    send(seven, 1, tr.at[2], tr.at[3], to_x)

    @pl.when(jnp.logical_not(holder))
    def _():
        arrive((p1s, p1r), 0, mine)

    @pl.when(jnp.logical_and(at_root, core == 1))
    def _():
        hops[0].start()

    @pl.when(jnp.logical_and(z == 0, jnp.logical_not(holder)))
    def _():
        for hop in hops[1:]:
            hop.start()

    two, three = (p2s, p2r), (p3s, p3r)
    pass_on(two, 4, mine, to_l)
    for d, where in along:
        pass_on(two, d, mine, where)
    pass_on(three, 0, mine, to_core)

    def spread_block(h, zz, k):
        return hl_ref.at[k, h * 4 + zz]

    arrive(seven, 1, tr.at[3])
    tz[z] = tr[2] + tr[3]
    for d, where in ((1, to_zn), (3, to_zp), (2, to_zf)):
        pass_on(seven, 1 + d, tz.at[z], where)
    here = spread_block(xh, z, core)

    @pl.when(away)
    def _():
        across.wait_recv()

    @pl.when(jnp.logical_not(away))
    def _():
        stay.wait()

    for slot, where in ((1, to_x), (2, to_zn), (3, to_zp), (4, to_zf)):
        pass_on(five, slot, here, where)
    arrive(two, 4, by_half(cp, core))
    for d, where in along:
        pass_on(two, 4 + d, by_half(cp, core), where)
    pass_on(three, 4, by_half(cp, core), to_core)
    for d, zz in ((1, zp), (3, zn), (2, zf)):
        arrive(seven, 1 + d, tz.at[zz])
    tr[4] = jnp.sum(tz[...], axis=0)
    send(seven, 5, tr.at[4], tr.at[5], to_l)
    send(four, 4, hid, hcol_ref.at[ci], to_l)
    order = [(0, 1), (0, 3), (0, 2), (1, 1), (1, 3), (1, 2)]
    for s in order:
        slot = s[0] * 4 + s[1]
        arrive(two, slot, by_half(col_from[s], core))
        pass_on(three, slot, by_half(col_from[s], core), to_core)
        if s == (0, 2):
            arrive(seven, 5, tr.at[5])
            ty[y] = tr[4] + tr[5]
            for d, where in along:
                pass_on(seven, 5 + d, ty.at[y], where)
            for d, where in along:
                send(four, d, hid, hcol_ref.at[ci], where)
    arrive(five, 1, spread_block(oh, z, core))
    for slot, where in ((5, to_zn), (6, to_zp), (7, to_zf)):
        pass_on(five, slot, spread_block(oh, z, core), where)
    pass_on(six, 0, here, to_core)
    pass_on(six, 1, spread_block(oh, z, core), to_core)
    arrive(three, 0, by_half(ci, oc))
    arrive(three, 4, by_half(cp, oc))
    for s in order:
        arrive(three, s[0] * 4 + s[1], by_half(col_from[s], oc))
    panel = corner.shape[0]
    hp = hp_ref[...].reshape(total_rows, panel)
    on_line = lax.broadcasted_iota(jnp.int32, (panel, panel), 0) == lax.broadcasted_iota(jnp.int32, (panel, panel), 1)
    gram = cross(hp, hp) / total_rows
    for d, yy in ((1, yp), (3, yn), (2, yf)):
        arrive(seven, 5 + d, ty.at[yy])
    total = jnp.sum(jnp.sum(ty[...], axis=0), axis=(0, 1), keepdims=True)
    ridge = damping * total / (total_rows * full)
    ridge_ref[...] = jnp.broadcast_to(ridge, (8, 128))
    scale = 1.0 / ridge
    corner[...] = (gram + jnp.where(on_line, ridge, 0.0)) * scale

    def between(k):
        if k == 0:
            arrive(four, 4, hcol_ref.at[cp])
            for d, where in along:
                pass_on(four, 4 + d, hcol_ref.at[cp], where)

        elif k == 2:
            for slot, zz in ((2, zp), (3, zn), (4, zf)):
                arrive(five, slot, spread_block(xh, zz, core))
                pass_on(six, slot, spread_block(xh, zz, core), to_core)
        elif k == 5:
            for slot, zz in ((5, zp), (6, zn), (7, zf)):
                arrive(five, slot, spread_block(oh, zz, core))
                pass_on(six, slot, spread_block(oh, zz, core), to_core)

    factor_inverse(corner, x_ref, between)
    x_ref[...] = x_ref[...] * jnp.sqrt(scale)
    for slot, (h, zz) in enumerate(((xh, z), (oh, z), (xh, zp), (xh, zn), (xh, zf), (oh, zp), (oh, zn), (oh, zf))):
        arrive(six, slot, spread_block(h, zz, oc))
    for s in order:
        arrive(four, s[0] * 4 + s[1], hcol_ref.at[col_from[s]])
    for copy in started:
        copy.wait_send()

    @pl.when(away)
    def _():
        across.wait_send()

    @pl.when(holder)
    def _():
        give.wait_send()

    @pl.when(at_root)
    def _():
        hops[0].wait_send()

    @pl.when(z == 0)
    def _():
        for hop in hops[1:]:
            hop.wait_send()


def main_of(tokens, gate_weight, up_weight, route, live, full):
    m, width = tokens.shape
    own = gate_weight.shape[1]
    rows_all = route.shape[0]
    rows = rows_all // 8
    hr = rows // 2
    vm = pltpu.VMEM
    dma = pltpu.SemaphoreType.DMA
    hbm = pl.BlockSpec(memory_space=pltpu.HBM)
    whole = pl.BlockSpec(memory_space=pltpu.VMEM)
    operands = (tokens, gate_weight, up_weight, route.reshape(8, rows), live.reshape(8, rows))
    return pl.pallas_call(
        functools.partial(main_kernel, rows_all, full),
        name="hidden_factor",
        out_shape=(
            jax.ShapeDtypeStruct((8, rows, own), BF16),
            jax.ShapeDtypeStruct((8, rows, own), BF16),
            jax.ShapeDtypeStruct((2, 8, rows, own), BF16),
            jax.ShapeDtypeStruct((PANEL, PANEL), F32),
            jax.ShapeDtypeStruct((8, 128), F32),
        ),
        in_specs=[hbm] * 5,
        out_specs=(whole,) * 5,
        scratch_shapes=[
            vm((2, 4, 2, m, width), BF16),
            vm(gate_weight.shape, BF16),
            vm(up_weight.shape, BF16),
            vm((8, rows), jnp.int32),
            vm((8, rows), jnp.int32),
            vm((rows_all, 128), jnp.int32),
            vm((2, 4, rows, own), F32),
            vm((2, 4, rows, own), F32),
            vm((4, rows, own), F32),
            vm((2, hr, own), F32),
            vm((2, rows, own), F32),
            vm((2, rows, own), F32),
            vm((2, 2, rows, own), F32),
            vm((rows, own), F32),
            vm((rows, own), F32),
            vm((rows, own), BF16),
            vm((PANEL, PANEL), F32),
            vm((6, 8, 128), F32),
            vm((4, 8, 128), F32),
            vm((4, 8, 128), F32),
            dma((5,)),
            dma((21,)), dma((21,)),
            dma((17,)), dma((17,)),
            dma((5,)), dma((1,)),
            dma((8,)), dma((8,)),
            dma((8,)), dma((8,)),
            dma((9,)), dma((9,)),
            dma((8,)), dma((8,)),
            dma((8,)), dma((8,)),
            dma((8,)), dma((8,)),
        ],
        compiler_params=pltpu.CompilerParams(collective_id=0, has_side_effects=True, vmem_limit_bytes=46000 * 2**10),
    )(*(pltpu.with_memory_space_constraint(a, pltpu.HBM) for a in operands))


def pair(a):
    high = a.astype(BF16)
    return high, (a - high.astype(F32)).astype(BF16)


def dot3_t(a, b):
    def one(u, v):
        return lax.dot_general(u, v, (((1,), (1,)), ((), ())), preferred_element_type=F32)

    return one(a[0], b[0]) + (one(a[0], b[1]) + one(a[1], b[0]))


def outputs_kernel(hp_ref, hcol_ref, hl_ref, x_ref, ridge_ref, panel_ref, trailing_ref, panel, trailing, sems):
    xh, z, core = (lax.axis_index(a) for a in ROW)
    xl, y = (lax.axis_index(a) for a in COL)
    ci, ri = xl * 4 + y, (xh * 4 + z) * 2 + core
    rows_all = hp_ref.shape[0] * hp_ref.shape[1]
    n = x_ref.shape[0]
    ridge = ridge_ref[0:1, 0:1]
    on_line = lax.broadcasted_iota(jnp.int32, (n, n), 0) == lax.broadcasted_iota(jnp.int32, (n, n), 1)
    hp = hp_ref[...].reshape(rows_all, n)
    hcol = hcol_ref[...].reshape(rows_all, n)
    x = pair(x_ref[...])

    def with_ridge(gram, here):
        return gram / rows_all + jnp.where(jnp.logical_and(on_line, here), ridge, 0.0)

    right = pair(dot3_t(pair(with_ridge(cross(hcol, hp), ri == 0)), x))
    copies = []
    for j in range(2):
        here = pl.ds(j * n, n)
        left = hl_ref[j].reshape(rows_all, n)
        down = dot3_t(pair(with_ridge(cross(left, hp), ci * 2 + j == 0)), x)
        panel[here, :] = down
        copies.append(pltpu.make_async_copy(panel.at[here], panel_ref.at[here], sems.at[j]))
        copies[-1].start()
        trailing[here, :] = with_ridge(cross(left, hcol), ci * 2 + j == ri) - dot3_t(pair(down), right)
        copies.append(pltpu.make_async_copy(trailing.at[here], trailing_ref.at[here], sems.at[2 + j]))
        copies[-1].start()
    for copy in copies:
        copy.wait()


def outputs_of(hp, hcol, hl, x, ridge):
    n = x.shape[0]
    hbm = pl.BlockSpec(memory_space=pl.ANY)
    whole = pl.BlockSpec(memory_space=pltpu.VMEM)
    return pl.pallas_call(
        outputs_kernel,
        name="outputs",
        out_shape=(jax.ShapeDtypeStruct((2 * n, n), F32), jax.ShapeDtypeStruct((2 * n, n), F32)),
        in_specs=[whole] * 5,
        out_specs=(hbm, hbm),
        scratch_shapes=[pltpu.VMEM((2 * n, n), F32), pltpu.VMEM((2 * n, n), F32), pltpu.SemaphoreType.DMA((4,))],
        compiler_params=pltpu.CompilerParams(vmem_limit_bytes=28 * 2**20),
    )(hp, hcol, hl, x, ridge)


def per_device(tokens, gate_weight, up_weight, route, live):
    full = gate_weight.shape[1] * lax.axis_size(ROW)
    return outputs_of(*main_of(tokens, gate_weight, up_weight, route, live, full))


def solution(mesh):
    finer = Mesh(mesh.devices.reshape(2, 4, 2, 2, 4), ("row_0", "row_1", "row_2", "col_0", "col_1"))
    placed = (P(ROW, COL), P(COL, ROW), P(COL, ROW), P(), P())
    return jax.shard_map(
        per_device,
        mesh=finer,
        in_specs=placed,
        out_specs=(P(COL, None), P(COL, ROW)),
        check_vma=False,
    )
```
